128 devices in a mesh: row: 8 (over y, z_lo), col: 16 (over z_hi, x, core).
Axes of the slice: x: 4, y: 4, z: 4 (z_hi: 2, z_lo: 2; z = z_hi * 2 + z_lo), core: 2. Of those that a mesh axis runs over, the one named last changes fastest.
Arguments:
- hidden: bfloat16 [5120, 5120], P('col'), may hold values from -26 to 26
- lengths: int32 [4], replicated, may hold values from 512 to 2048, as said below
- owner: int32 [4], replicated, may hold values from 0 to 15, as said below
- page_table: int32 [4, 16], replicated, may hold values from 0 to 15, as said below
- qkv_train: float32 [3, 5120, 3072], P(None, 'row', 'col'), may hold values from -1 to 1
- qk_gain: float32 [2, 3072], P(None, 'row'), may hold values from 0.1 to 1.9
- o_weight: bfloat16 [3072, 5120], P('row'), may hold values from -1.5 to 1.5
- post_gain: float32 [5120], P('row'), may hold values from 0.1 to 1.9
- gate_up_train: float32 [2, 5120, 13824], P(None, 'row', 'col'), may hold values from -0.078125 to 0.078125
Outputs:
- layer_out: bfloat16 [5120, 5120], P('col', 'row')
- kv_cache: bfloat16 [16, 16, 2, 128, 3072], P('col', None, None, None, 'row')
- qkv_server: bfloat16 [3, 8, 640, 3072], P(None, None, 'col', 'row')
- gate_up_server: bfloat16 [2, 8, 640, 13824], P(None, None, 'col', 'row')
The draws below stay inside these ranges and needn't reach their ends.
Inputs may be any that keep to these rules, and one draw needn't show every extreme that they name: The lengths add up to 5120; one prompt has 2048 tokens and one 512. `owner`: the owners are distinct. `page_table`: each row is a permutation of the 16 slots.
All inputs are finite; a program needn't handle non-finite values.
Results may differ from the reference program's by a relative error of at most 0.025.
Values may be sent and summed in bfloat16 or wider, within the bound.
A program may use at most 128 MiB of HBM per device.

```python
import math
import jax
import jax.numpy as jnp
from jax import lax

D = 5120
HD = 128
FF = 13824
HEADS = 24
PROMPTS = 4
LMAX = 2048
LMIN = 512
PAGE = 128
PAGES = 16
TOKENS = 5120
N_ROW = 8
N_COL = 16


def draw_hidden(key, part):
    noise_key = jax.random.fold_in(key, 11)
    values = jnp.clip(jax.random.normal(noise_key, (TOKENS, D), jnp.float32), -6.0, 6.0)
    return values.astype(jnp.bfloat16)


def draw_qkv_train(key, part):
    heads_width = HEADS * HD
    columns = jnp.arange(heads_width, dtype=jnp.float32)
    column_scale = jnp.sqrt(3.0 ** (columns / heads_width))[None, None, :]
    base_draw = jnp.clip(jax.random.normal(jax.random.fold_in(key, 22), (3, D, heads_width), jnp.float32), -6.0, 6.0)
    values = base_draw * column_scale / math.sqrt(D)
    return values


def draw_o_weight(key, part):
    columns = jnp.arange(D, dtype=jnp.float32)
    column_scale = jnp.sqrt(3.0 ** (columns / D))[None, :] / math.sqrt(HEADS * HD)
    base_draw = jnp.clip(jax.random.normal(jax.random.fold_in(key, 32), (HEADS * HD, D), jnp.float32), -6.0, 6.0)
    return (base_draw * column_scale).astype(jnp.bfloat16)


def draw_lengths(key, part):
    middle = jax.random.randint(jax.random.fold_in(key, 41), (), LMIN, LMAX + 1).astype(jnp.int32)
    values = jnp.stack([jnp.int32(LMAX), jnp.int32(LMIN), middle, jnp.int32(LMAX + LMIN) - middle]).astype(jnp.int32)
    return values[jax.random.permutation(jax.random.fold_in(key, 42), PROMPTS)]


def draw_owner(key, part):
    middle = jax.random.permutation(jax.random.fold_in(key, 51), N_COL - 2)[:PROMPTS - 2] + 1
    values = jnp.concatenate([jnp.array([0, N_COL - 1], jnp.int32), middle.astype(jnp.int32)])
    return values[jax.random.permutation(jax.random.fold_in(key, 52), PROMPTS)]


def draw_page_table(key, part):
    row_keys = jax.random.split(jax.random.fold_in(key, 61), PROMPTS)
    return jax.vmap(lambda row_key: jax.random.permutation(row_key, PAGES))(row_keys).astype(jnp.int32)


def block_levels(key, extent, pieces, smallest, largest):
    gain = 1.0
    for axis_at, shards_of in pieces:
        steps = jax.random.uniform(jax.random.fold_in(jax.random.fold_in(key, 6), axis_at), (shards_of,), jnp.float32, smallest / len(pieces), largest / len(pieces))
        gain = gain * jnp.repeat(jnp.exp(steps), extent[axis_at] // shards_of).reshape((-1,) + (1,) * (len(extent) - 1 - axis_at))
    return gain


def normal_values(key, extent, scale, most, cuts=(), kind=jnp.bfloat16):
    result = jax.random.normal(key, extent, jnp.float32) * scale
    if len(cuts) > 0:
        result = block_levels(key, extent, cuts, -0.22, 0.18) * result
    return jnp.clip(result, min=-most, max=most).astype(kind)


def setup_inputs(seed: int = 0) -> dict:
    key_list = jax.random.split(jax.random.key(seed), 10)
    hidden = draw_hidden(jax.random.fold_in(key_list[9], 71), 0)
    lengths = draw_lengths(jax.random.fold_in(key_list[9], 71), 0)
    owner = draw_owner(jax.random.fold_in(key_list[9], 71), 0)
    page_table = draw_page_table(jax.random.fold_in(key_list[9], 71), 0)
    qkv_train = draw_qkv_train(jax.random.fold_in(key_list[9], 71), 0)
    qk_gain = jnp.clip(1.0 + 0.18 * jax.random.normal(key_list[5], (2, HEADS * HD), jnp.float32), 0.1, 1.9)
    o_weight = draw_o_weight(jax.random.fold_in(key_list[9], 71), 0)
    post_gain = jnp.clip(1.0 + 0.18 * jax.random.normal(key_list[7], (D,), jnp.float32), 0.1, 1.9)
    gate_up_train = normal_values(key_list[8], (2, D, FF), D ** -0.5, 0.078125, ((1, 8), (2, 16)), jnp.float32)
    return dict(hidden=hidden, lengths=lengths, owner=owner, page_table=page_table, qkv_train=qkv_train, qk_gain=qk_gain, o_weight=o_weight, post_gain=post_gain, gate_up_train=gate_up_train)


norm_epsilon = 1e-06
rope_theta = 500000.0
big_negative = -1e+30

def inverse_rms(squares, features):
    return lax.rsqrt(squares / features + norm_epsilon)

def rotate_heads(inputs, positions):
    half_dim = inputs.shape[-1] // 2
    frequency = rope_theta ** (-2.0 * jnp.arange(half_dim, dtype=jnp.float32) / inputs.shape[-1])
    angles = positions.astype(jnp.float32)[:, None] * frequency[None, :]
    cosine = jnp.cos(angles)[:, None, :]
    sine_part = jnp.sin(angles)[:, None, :]
    lower_half = inputs[..., :half_dim]
    upper_half = inputs[..., half_dim:]
    return jnp.concatenate([lower_half * cosine - upper_half * sine_part, upper_half * cosine + lower_half * sine_part], axis=-1)

def locate_tokens(token_index, lengths):
    prompt_ends = jnp.cumsum(lengths).astype(jnp.int32)
    prompt_starts = prompt_ends - lengths
    segment = lax.optimization_barrier(jnp.sum((token_index[:, None] >= prompt_ends[None, :]).astype(jnp.int32), axis=1))
    onehot = segment[:, None] == jnp.arange(lengths.shape[0], dtype=jnp.int32)[None, :]
    position = token_index - lax.optimization_barrier(jnp.sum(jnp.where(onehot, prompt_starts[None, :], 0), axis=1))
    return (segment, position)

def reference(hidden, lengths, owner, page_table, qkv_train, qk_gain, o_weight, post_gain, gate_up_train):
    heads_width = HEADS * HD
    row_width = D // N_ROW
    col_block = D // (N_ROW * N_COL)
    qkv_server = qkv_train.astype(jnp.bfloat16).reshape(3, N_ROW, row_width, heads_width)
    gate_up_server = gate_up_train.astype(jnp.bfloat16).reshape(2, N_ROW, row_width, FF)
    token_index = jnp.arange(TOKENS, dtype=jnp.int32)
    segment, position = locate_tokens(token_index, lengths)
    hidden_blocks = hidden.astype(jnp.float32).reshape(TOKENS, N_ROW, N_COL, col_block)
    weight_blocks = qkv_server.astype(jnp.float32).reshape(3, N_ROW, N_COL, col_block, heads_width)
    projected = jnp.zeros((3, TOKENS, heads_width), jnp.float32)
    for column in range(N_COL):
        block_product = jnp.einsum('trb,jrbh->jth', hidden_blocks[:, :, column], weight_blocks[:, :, column])
        projected = projected + lax.optimization_barrier(block_product.astype(jnp.bfloat16)).astype(jnp.float32)
    query_rows = projected[0]
    key_rows = projected[1]
    value_rows = projected[2]
    query_norm = query_rows * inverse_rms(lax.optimization_barrier(jnp.sum(query_rows * query_rows, axis=1)), heads_width)[:, None] * qk_gain[0]
    key_norm = key_rows * inverse_rms(lax.optimization_barrier(jnp.sum(key_rows * key_rows, axis=1)), heads_width)[:, None] * qk_gain[1]
    query_rot = rotate_heads(query_norm.reshape(TOKENS, HEADS, HD), position).astype(jnp.bfloat16)
    key_rot = rotate_heads(key_norm.reshape(TOKENS, HEADS, HD), position).astype(jnp.bfloat16)
    value_heads = value_rows.reshape(TOKENS, HEADS, HD).astype(jnp.bfloat16)
    allowed = (segment[:, None] == segment[None, :]) & (token_index[None, :] <= token_index[:, None])

    def one_head(operands):
        query_head, key_head, value_head = operands
        scores = jnp.dot(query_head, key_head.T, preferred_element_type=jnp.float32) / math.sqrt(HD)
        masked = jnp.where(allowed, scores, big_negative)
        row_max = lax.optimization_barrier(jnp.max(masked, axis=1, keepdims=True))
        exponent = jnp.where(allowed, jnp.exp(masked - row_max), 0.0)
        numerator = jnp.dot(exponent.astype(jnp.bfloat16), value_head, preferred_element_type=jnp.float32)
        return numerator / lax.optimization_barrier(jnp.sum(exponent, axis=1, keepdims=True))
    attention = lax.map(one_head, (query_rot.transpose(1, 0, 2), key_rot.transpose(1, 0, 2), value_heads.transpose(1, 0, 2)))
    attention = attention.transpose(1, 0, 2).reshape(TOKENS, heads_width).astype(jnp.bfloat16)
    heads_per_row = heads_width // N_ROW
    attention_out = jnp.zeros((TOKENS, D), jnp.float32)
    for group in range(N_ROW):
        lower = group * heads_per_row
        group_product = jnp.dot(attention[:, lower:lower + heads_per_row], o_weight[lower:lower + heads_per_row], preferred_element_type=jnp.float32)
        attention_out = attention_out + lax.optimization_barrier(group_product.astype(jnp.bfloat16)).astype(jnp.float32)
    normalized = attention_out * inverse_rms(lax.optimization_barrier(jnp.sum(attention_out * attention_out, axis=1)), D)[:, None] * post_gain
    layer_out = (hidden.astype(jnp.float32) + normalized).astype(jnp.bfloat16)
    stacked = jnp.stack([key_rot.reshape(TOKENS, heads_width), value_heads.reshape(TOKENS, heads_width)], axis=1)
    padded = jnp.concatenate([stacked, jnp.zeros((LMAX, 2, heads_width), jnp.bfloat16)], axis=0)
    prompt_ends = jnp.cumsum(lengths).astype(jnp.int32)
    prompt_starts = prompt_ends - lengths
    kv_cache = jnp.zeros((N_COL, PAGES, 2, PAGE, heads_width), jnp.bfloat16)
    for prompt in range(PROMPTS):
        window = lax.dynamic_slice_in_dim(padded, prompt_starts[prompt].astype(jnp.int32), LMAX, 0)
        inside = jnp.arange(LMAX, dtype=jnp.int32) < lengths[prompt]
        window = jnp.where(inside[:, None, None], window, jnp.zeros((), jnp.bfloat16))
        pages_data = window.reshape(PAGES, PAGE, 2, heads_width).transpose(0, 2, 1, 3)
        kv_cache = kv_cache.at[owner[prompt], page_table[prompt]].set(pages_data)
    return (layer_out, kv_cache, qkv_server, gate_up_server)
```

```python
import functools
import math

import jax
import jax.numpy as jnp
from jax import lax
from jax.experimental import pallas as pl
from jax.experimental.pallas import tpu as pltpu
from jax.sharding import PartitionSpec as P

HD = 128
HEADS = 24
PAGE = 128
PAGES = 16
LMAX = 2048

norm_epsilon = 1e-06
rope_theta = 500000.0
big_negative = -1e30


def inverse_rms(squares, features):
    return lax.rsqrt(squares / features + norm_epsilon)


def rotate_heads(inputs, positions):
    half_dim = inputs.shape[-1] // 2
    frequency = rope_theta ** (-2.0 * jnp.arange(half_dim, dtype=jnp.float32) / inputs.shape[-1])
    angles = positions.astype(jnp.float32)[:, None] * frequency[None, :]
    cosine = jnp.cos(angles)[:, None, :]
    sine_part = jnp.sin(angles)[:, None, :]
    lower_half = inputs[..., :half_dim]
    upper_half = inputs[..., half_dim:]
    return jnp.concatenate(
        [
            lower_half * cosine - upper_half * sine_part,
            upper_half * cosine + lower_half * sine_part,
        ],
        axis=-1,
    )


def locate_tokens(token_index, lengths):
    prompt_ends = jnp.cumsum(lengths)
    prompt_starts = prompt_ends - lengths
    segment = jnp.sum((token_index[:, None] >= prompt_ends[None, :]).astype(jnp.int32), axis=1)
    onehot = segment[:, None] == jnp.arange(lengths.shape[0], dtype=jnp.int32)[None, :]
    start = jnp.sum(jnp.where(onehot, prompt_starts[None, :], 0), axis=1)
    return start


ALIGN = 16
WINDOW = PAGE + ALIGN


def cache_body(meta_ref, kv_ref, out_ref):
    tokens = kv_ref.shape[1]
    start, length = meta_ref[0], meta_ref[1]

    @pl.loop(0, PAGES)
    def _(page):
        first = jnp.minimum(start + page * PAGE, tokens - 1)
        base = jnp.minimum((first // ALIGN) * ALIGN, tokens - WINDOW)
        base = pl.multiple_of(base, ALIGN)
        shift = first - base
        slot = meta_ref[2 + page]
        rows = lax.broadcasted_iota(jnp.int32, (PAGE, 1), 0) + page * PAGE
        inside = rows < length
        for part in range(2):
            piece = kv_ref[part, pl.ds(base, WINDOW), :].astype(jnp.float32)
            piece = pltpu.roll(piece, lax.rem(WINDOW - shift, WINDOW), 0)[:PAGE]
            out_ref[slot, part] = jnp.where(inside, piece, 0.0).astype(jnp.bfloat16)


def build_cache(meta, kv):
    width = kv.shape[2]
    return pl.pallas_call(
        cache_body,
        out_shape=jax.ShapeDtypeStruct((PAGES, 2, PAGE, width), jnp.bfloat16),
        in_specs=[
            pl.BlockSpec(memory_space=pltpu.SMEM),
            pl.BlockSpec(memory_space=pltpu.VMEM),
        ],
        out_specs=pl.BlockSpec(memory_space=pltpu.VMEM),
        compiler_params=pltpu.CompilerParams(vmem_limit_bytes=40 << 20),
        cost_estimate=pl.CostEstimate(flops=10_000_000, bytes_accessed=11_000_000, transcendentals=0),
        name="cache_pages",
    )(meta, kv)


def attend_body(first_ref, start_ref, query_ref, kv_ref, out_ref, *, span):
    rows = query_ref.shape[0]
    heads = query_ref.shape[1] // HD
    first_query, first_key = first_ref[0], first_ref[1]
    first_key = pl.multiple_of(first_key, 64)
    query_index = first_query + lax.broadcasted_iota(jnp.int32, (rows, 1), 0)
    key_index = first_key + lax.broadcasted_iota(jnp.int32, (1, span), 1)
    allowed = (key_index <= query_index) & (key_index >= start_ref[...])
    for head in range(heads):
        lanes = slice(head * HD, (head + 1) * HD)
        keys = kv_ref[0, pl.ds(first_key, span), lanes]
        values = kv_ref[1, pl.ds(first_key, span), lanes]
        scores = lax.dot_general(
            query_ref[:, lanes], keys, (((1,), (1,)), ((), ())), preferred_element_type=jnp.float32
        ) * (1.0 / math.sqrt(HD))
        scores = jnp.where(allowed, scores, big_negative)
        exponent = jnp.exp(scores - jnp.max(scores, axis=1, keepdims=True))
        total = jnp.sum(exponent, axis=1, keepdims=True)
        mixed = jnp.dot(exponent.astype(jnp.bfloat16), values, preferred_element_type=jnp.float32)
        out_ref[:, lanes] = (mixed / total).astype(jnp.bfloat16)


def attend(first, start, query, kv, span):
    return pl.pallas_call(
        functools.partial(attend_body, span=span),
        out_shape=jax.ShapeDtypeStruct(query.shape, jnp.bfloat16),
        in_specs=[pl.BlockSpec(memory_space=pltpu.SMEM)]
        + [pl.BlockSpec(memory_space=pltpu.VMEM)] * 3,
        out_specs=pl.BlockSpec(memory_space=pltpu.VMEM),
        compiler_params=pltpu.CompilerParams(vmem_limit_bytes=48 << 20),
        cost_estimate=pl.CostEstimate(
            flops=4 * query.shape[0] * span * query.shape[1],
            bytes_accessed=8_000_000,
            transcendentals=3 * query.shape[0] * span,
        ),
        name="attend",
    )(first, start, query, kv)


def local(
    hidden, lengths, owner, page_table, qkv_train, qk_gain, o_weight, post_gain, gate_up_train
):
    n_row = lax.axis_size("row")
    n_col = lax.axis_size("col")
    col_index = lax.axis_index("col")
    row_index = lax.axis_index("row")
    tok_rows = hidden.shape[0]
    model_width = hidden.shape[1]
    row_width = model_width // n_row
    col_block = row_width // n_col
    trainer_qkv = qkv_train.astype(jnp.bfloat16)
    trainer_gate_up = gate_up_train.astype(jnp.bfloat16)
    server_qkv, server_gate_up = (
        lax.all_to_all(
            lax.all_to_all(trainer_qkv, "col", split_axis=1, concat_axis=2, tiled=True),
            "row",
            split_axis=2,
            concat_axis=1,
            tiled=True,
        ),
        lax.all_to_all(
            lax.all_to_all(trainer_gate_up, "col", split_axis=1, concat_axis=2, tiled=True),
            "row",
            split_axis=2,
            concat_axis=1,
            tiled=True,
        ),
    )
    heads_width = server_qkv.shape[2]
    local_heads = heads_width // HD
    weight_blocks = server_qkv.reshape(3, n_row, col_block, heads_width)
    gate_up_blocks = server_gate_up.reshape(2, n_row, col_block, server_gate_up.shape[2])
    hidden_three = hidden.reshape(tok_rows, n_row, row_width)
    shard_piece = lax.all_gather(weight_blocks, "col", axis=2, tiled=True)
    shards = shard_piece.shape[2] // col_block
    projected = jnp.einsum(
        "trb,jrbh->tjh", hidden_three, shard_piece, preferred_element_type=jnp.float32
    )
    query_rows = projected[:, 0]
    key_rows = projected[:, 1]
    value_rows = projected[:, 2]
    query_squares, key_squares = lax.psum(
        (jnp.sum(query_rows * query_rows, axis=1), jnp.sum(key_rows * key_rows, axis=1)), "row"
    )
    full_heads = HEADS * HD
    query_norm = query_rows * inverse_rms(query_squares, full_heads)[:, None] * qk_gain[0]
    key_norm = key_rows * inverse_rms(key_squares, full_heads)[:, None] * qk_gain[1]
    token_index = col_index * tok_rows + jnp.arange(tok_rows, dtype=jnp.int32)
    token_start = locate_tokens(token_index, lengths)
    position = token_index - token_start
    query_rot = rotate_heads(query_norm.reshape(tok_rows, local_heads, HD), position).astype(
        jnp.bfloat16
    ).reshape(tok_rows, heads_width)
    key_rot = (
        rotate_heads(key_norm.reshape(tok_rows, local_heads, HD), position)
        .astype(jnp.bfloat16)
        .reshape(tok_rows, heads_width)
    )
    value_flat = value_rows.astype(jnp.bfloat16)
    kv = lax.all_gather(jnp.stack([key_rot, value_flat]), "col", axis=1, tiled=True)

    prompt_starts = jnp.cumsum(lengths) - lengths
    owned = owner == col_index
    my_start = jnp.sum(jnp.where(owned, prompt_starts, 0))
    my_length = jnp.sum(jnp.where(owned, lengths, 0))
    my_pages = jnp.where(
        jnp.any(owned),
        jnp.sum(jnp.where(owned[:, None], page_table, 0), axis=0),
        jnp.arange(PAGES, dtype=jnp.int32),
    )
    meta = jnp.concatenate([jnp.stack([my_start, my_length]), my_pages]).astype(jnp.int32)
    cache_pages = build_cache(meta, kv)

    reach = -(-(LMAX - 1) // tok_rows)
    span = min(reach + 1, n_col) * tok_rows
    first_key = jnp.maximum(col_index - reach, 0) * tok_rows
    first = jnp.stack([col_index * tok_rows, first_key]).astype(jnp.int32)
    attention = attend(first, token_start[:, None], query_rot, kv, span)

    o_columns = lax.all_to_all(o_weight, "row", split_axis=1, concat_axis=0, tiled=True)
    attention_all = lax.all_gather(attention, "row", axis=1, tiled=True)
    own_out = jnp.dot(attention_all, o_columns, preferred_element_type=jnp.float32)
    out_squares = lax.psum(jnp.sum(own_out * own_out, axis=1), "row")
    normalized = own_out * inverse_rms(out_squares, model_width)[:, None] * post_gain
    residual = lax.dynamic_slice_in_dim(hidden, row_index * row_width, row_width, 1).astype(
        jnp.float32
    )
    layer_out = (residual + normalized).astype(jnp.bfloat16)
    return (layer_out, cache_pages[None], weight_blocks, gate_up_blocks)


def solution(mesh):
    in_specs = (
        P("col", None),
        P(),
        P(),
        P(),
        P(None, "row", "col"),
        P(None, "row"),
        P("row", None),
        P("row"),
        P(None, "row", "col"),
    )
    out_specs = (
        P("col", "row"),
        P("col", None, None, None, "row"),
        P(None, None, "col", "row"),
        P(None, None, "col", "row"),
    )
    return jax.shard_map(local, mesh=mesh, in_specs=in_specs, out_specs=out_specs, check_vma=False)
```

```python
import functools
import math

import jax
import jax.numpy as jnp
from jax import lax
from jax.experimental import pallas as pl
from jax.experimental.pallas import tpu as pltpu
from jax.sharding import PartitionSpec as P

HD = 128
HEADS = 24
PAGE = 128
PAGES = 16
LMAX = 2048

norm_epsilon = 1e-06
rope_theta = 500000.0
big_negative = -1e30


def inverse_rms(squares, features):
    return lax.rsqrt(squares / features + norm_epsilon)


def rotate_heads(inputs, positions):
    half_dim = inputs.shape[-1] // 2
    frequency = rope_theta ** (-2.0 * jnp.arange(half_dim, dtype=jnp.float32) / inputs.shape[-1])
    angles = positions.astype(jnp.float32)[:, None] * frequency[None, :]
    cosine = jnp.cos(angles)[:, None, :]
    sine_part = jnp.sin(angles)[:, None, :]
    lower_half = inputs[..., :half_dim]
    upper_half = inputs[..., half_dim:]
    return jnp.concatenate(
        [
            lower_half * cosine - upper_half * sine_part,
            upper_half * cosine + lower_half * sine_part,
        ],
        axis=-1,
    )


def locate_tokens(token_index, lengths):
    prompt_ends = jnp.cumsum(lengths)
    prompt_starts = prompt_ends - lengths
    segment = jnp.sum((token_index[:, None] >= prompt_ends[None, :]).astype(jnp.int32), axis=1)
    onehot = segment[:, None] == jnp.arange(lengths.shape[0], dtype=jnp.int32)[None, :]
    start = jnp.sum(jnp.where(onehot, prompt_starts[None, :], 0), axis=1)
    return start


ALIGN = 16
WINDOW = PAGE + ALIGN


def cache_body(meta_ref, kv_ref, out_ref):
    tokens = kv_ref.shape[1]
    start, length = meta_ref[0], meta_ref[1]

    @pl.loop(0, PAGES)
    def _(page):
        first = jnp.minimum(start + page * PAGE, tokens - 1)
        base = jnp.minimum((first // ALIGN) * ALIGN, tokens - WINDOW)
        base = pl.multiple_of(base, ALIGN)
        shift = first - base
        slot = meta_ref[2 + page]
        rows = lax.broadcasted_iota(jnp.int32, (PAGE, 1), 0) + page * PAGE
        inside = rows < length
        for part in range(2):
            piece = kv_ref[part, pl.ds(base, WINDOW), :].astype(jnp.float32)
            piece = pltpu.roll(piece, lax.rem(WINDOW - shift, WINDOW), 0)[:PAGE]
            out_ref[slot, part] = jnp.where(inside, piece, 0.0).astype(jnp.bfloat16)


def build_cache(meta, kv):
    width = kv.shape[2]
    return pl.pallas_call(
        cache_body,
        out_shape=jax.ShapeDtypeStruct((PAGES, 2, PAGE, width), jnp.bfloat16),
        in_specs=[
            pl.BlockSpec(memory_space=pltpu.SMEM),
            pl.BlockSpec(memory_space=pltpu.VMEM),
        ],
        out_specs=pl.BlockSpec(memory_space=pltpu.VMEM),
        compiler_params=pltpu.CompilerParams(vmem_limit_bytes=40 << 20),
        cost_estimate=pl.CostEstimate(flops=10_000_000, bytes_accessed=11_000_000, transcendentals=0),
        name="cache_pages",
    )(meta, kv)


def attend_body(first_ref, start_ref, query_ref, kv_ref, out_ref, *, span):
    rows = query_ref.shape[0]
    heads = query_ref.shape[1] // HD
    first_query, first_key = first_ref[0], first_ref[1]
    first_key = pl.multiple_of(first_key, 64)
    query_index = first_query + lax.broadcasted_iota(jnp.int32, (rows, 1), 0)
    key_index = first_key + lax.broadcasted_iota(jnp.int32, (1, span), 1)
    allowed = (key_index <= query_index) & (key_index >= start_ref[...])
    for head in range(heads):
        lanes = slice(head * HD, (head + 1) * HD)
        keys = kv_ref[0, pl.ds(first_key, span), lanes]
        values = kv_ref[1, pl.ds(first_key, span), lanes]
        scores = lax.dot_general(
            query_ref[:, lanes], keys, (((1,), (1,)), ((), ())), preferred_element_type=jnp.float32
        ) * (1.0 / math.sqrt(HD))
        scores = jnp.where(allowed, scores, big_negative)
        exponent = jnp.exp(scores - jnp.max(scores, axis=1, keepdims=True))
        total = jnp.sum(exponent, axis=1, keepdims=True)
        mixed = jnp.dot(exponent.astype(jnp.bfloat16), values, preferred_element_type=jnp.float32)
        out_ref[:, lanes] = (mixed / total).astype(jnp.bfloat16)


def attend(first, start, query, kv, span):
    return pl.pallas_call(
        functools.partial(attend_body, span=span),
        out_shape=jax.ShapeDtypeStruct(query.shape, jnp.bfloat16),
        in_specs=[pl.BlockSpec(memory_space=pltpu.SMEM)]
        + [pl.BlockSpec(memory_space=pltpu.VMEM)] * 3,
        out_specs=pl.BlockSpec(memory_space=pltpu.VMEM),
        compiler_params=pltpu.CompilerParams(vmem_limit_bytes=48 << 20),
        cost_estimate=pl.CostEstimate(
            flops=4 * query.shape[0] * span * query.shape[1],
            bytes_accessed=8_000_000,
            transcendentals=3 * query.shape[0] * span,
        ),
        name="attend",
    )(first, start, query, kv)


def rdma(src, dst, send_sem, recv_sem, row, col):
    return pltpu.make_async_remote_copy(
        src_ref=src,
        dst_ref=dst,
        send_sem=send_sem,
        recv_sem=recv_sem,
        device_id=(row, col),
        device_id_type=pl.DeviceIdType.MESH,
    )


def each(count, body):
    lax.fori_loop(0, count, lambda i, carry: (body(i), carry)[1], 0)


def signal(sem, row, col):
    pl.semaphore_signal(sem, inc=1, device_id=(row, col), device_id_type=pl.DeviceIdType.MESH)


def sync_body(
    qkv_ref, gate_hbm, hid_ref, ow_hbm,
    proj_ref, qblk_ref, gblk_ref, ocol_ref,
    qsrc, qstage, w_all, gf32, gsrc, gstage,
    q_send, q_recv, w_send, w_fwd, w_recv, g_send, g_recv, o_send, o_fwd, o_recv, local_sem,
    *, n_row, n_col,
):
    row, col = lax.axis_index("row"), lax.axis_index("col")
    chip, core = col // 2, lax.rem(col, 2)
    chips = n_col // 2
    half_rows = n_row // 2
    step = qkv_ref.shape[1] // chips
    fine = step // 2
    sib = col + 1 - 2 * core
    target_core = row // half_rows
    self_row = chip == row

    gate_copy = pltpu.make_async_copy(gate_hbm, gf32, local_sem.at[0])
    gate_copy.start()

    barrier = pltpu.get_barrier_semaphore()

    def greet(i):
        peer_row, peer_col = i // 2, 2 * row + lax.rem(i, 2)

        @pl.when(jnp.logical_or(peer_row != row, peer_col != col))
        def _():
            signal(barrier, peer_row, peer_col)

    each(2 * n_row, greet)
    each(chips - 1, lambda i: signal(barrier, row, 2 * lax.rem(chip + 1 + i, chips) + core))
    signal(barrier, row, sib)
    each(n_row - 1, lambda i: signal(barrier, lax.rem(row + 1 + i, n_row), col))

    for j in range(3):
        qsrc[j] = qkv_ref[j].astype(jnp.bfloat16)
    pl.semaphore_wait(barrier, n_col + (chips - 1) + 1 + (n_row - 1) - self_row.astype(jnp.int32))

    def piece(to_chip):
        return qsrc.at[:, pl.ds(pl.multiple_of(to_chip * step, 16), step), :]

    def q_copy(i):
        to_chip = lax.rem(chip + i, chips)
        return rdma(
            piece(to_chip), qstage.at[core, lax.rem(row, half_rows)],
            q_send.at[i], q_recv.at[core, lax.rem(row, half_rows)],
            chip, 2 * to_chip + target_core,
        )

    q_self = jnp.logical_and(self_row, target_core == core)
    own_q = pltpu.make_async_copy(
        piece(chip), qstage.at[core, lax.rem(row, half_rows)],
        q_recv.at[core, lax.rem(row, half_rows)],
    )

    def q_start(i):
        away = jnp.logical_or(i > 0, jnp.logical_not(q_self))

        @pl.when(away)
        def _():
            q_copy(i).start()

    each(chips, q_start)

    @pl.when(q_self)
    def _():
        own_q.start()

    gate_copy.wait()
    for c in range(n_col):
        for j in range(2):
            gsrc[c, j] = gf32[j, c * fine:(c + 1) * fine, :].astype(jnp.bfloat16)

    def q_wait(i):
        half, src = lax.rem(i, 2), i // 2
        rdma(
            piece(0), qstage.at[half, src], q_send.at[0], q_recv.at[half, src], row, col
        ).wait_recv()

    each(2 * half_rows, q_wait)
    width = w_all.shape[3]
    place = pl.multiple_of(chip * step, 16)
    for s in range(half_rows):
        for j in range(3):
            both = jnp.concatenate(
                [qstage[0, s, j].astype(jnp.float32), qstage[1, s, j].astype(jnp.float32)], axis=1
            )
            w_all[j, core * half_rows + s, pl.ds(place, step), :] = both.astype(jnp.bfloat16)

    def block(of_chip, of_core):
        return w_all.at[
            :, pl.ds(of_core * half_rows, half_rows),
            pl.ds(pl.multiple_of(of_chip * step, 16), step), :
        ]

    def w_copy(i):
        to_chip = lax.rem(chip + 1 + i, chips)
        return rdma(
            block(chip, core), block(chip, core),
            w_send.at[i], w_recv.at[chip, core], row, 2 * to_chip + core,
        )

    def w_forward(of_chip):
        return rdma(
            block(of_chip, core), block(of_chip, core),
            w_fwd.at[of_chip], w_recv.at[of_chip, core], row, sib,
        )

    def w_arrived(of_chip, of_core):
        rdma(
            block(of_chip, of_core), block(of_chip, of_core),
            w_send.at[0], w_recv.at[of_chip, of_core], row, col,
        ).wait_recv()

    each(chips - 1, lambda i: w_copy(i).start())
    w_forward(chip).start()

    def g_copy(i):
        to_col = lax.rem(col + i, n_col)
        return rdma(
            gsrc.at[to_col], gstage.at[core, row], g_send.at[i], g_recv.at[core, row], chip, to_col
        )

    own_g = pltpu.make_async_copy(gsrc.at[col], gstage.at[core, row], g_recv.at[core, row])

    def g_start(i):
        @pl.when(jnp.logical_or(i > 0, jnp.logical_not(self_row)))
        def _():
            g_copy(i).start()

    each(n_col, g_start)

    @pl.when(self_row)
    def _():
        own_g.start()

    own_rows = ow_hbm.shape[0]
    half_o = own_rows // 2
    out_width = ocol_ref.shape[1]

    def o_src(of_core, to_row):
        return ow_hbm.at[
            pl.ds(pl.multiple_of(of_core * half_o, 16), half_o),
            pl.ds(pl.multiple_of(to_row * out_width, 128), out_width),
        ]

    def o_dst(of_row, of_core):
        return ocol_ref.at[
            pl.ds(pl.multiple_of(of_row * own_rows + of_core * half_o, 16), half_o), :
        ]

    def o_copy(i):
        to_row = lax.rem(row + 1 + i, n_row)
        return rdma(
            o_src(core, to_row), o_dst(row, core), o_send.at[i], o_recv.at[row, core], to_row, col
        )

    def o_forward(of_row):
        return rdma(
            o_dst(of_row, core), o_dst(of_row, core),
            o_fwd.at[of_row], o_recv.at[of_row, core], row, sib,
        )

    def o_arrived(of_row, of_core):
        rdma(
            o_dst(of_row, of_core), o_dst(of_row, of_core),
            o_send.at[0], o_recv.at[of_row, of_core], row, col,
        ).wait_recv()

    own_o = pltpu.make_async_copy(
        ow_hbm.at[:, pl.ds(pl.multiple_of(row * out_width, 128), out_width)],
        ocol_ref.at[pl.ds(pl.multiple_of(row * own_rows, 16), own_rows), :],
        local_sem.at[1],
    )
    each(n_row - 1, lambda i: o_copy(i).start())
    own_o.start()

    def w_relay(i):
        of_chip = lax.rem(chip + chips - 1 - i, chips)
        w_arrived(of_chip, core)
        w_forward(of_chip).start()

    each(chips - 1, w_relay)

    def o_relay(i):
        of_row = lax.rem(row + n_row - 1 - i, n_row)
        o_arrived(of_row, core)
        o_forward(of_row).start()

    each(n_row - 1, o_relay)
    each(chips, lambda i: w_arrived(lax.rem(chip + chips - i, chips), 1 - core))

    row_width = w_all.shape[2]
    for j in range(3):
        proj_ref[j] = jnp.zeros_like(proj_ref[j])

    def project(r):
        lanes = pl.ds(pl.multiple_of(r * row_width, 128), row_width)
        for j in range(3):
            proj_ref[j] += jnp.dot(
                hid_ref[:, lanes], w_all[j, r], preferred_element_type=jnp.float32
            )

    each(n_row, project)

    def own_rows_of(r):
        for j in range(3):
            rows = w_all[j, r, pl.ds(place, step), :].astype(jnp.float32)
            rows = jnp.where(core == 0, rows[:fine], rows[fine:])
            qblk_ref[j, r] = rows.astype(jnp.bfloat16)

    each(n_row, own_rows_of)

    def g_wait(i):
        half, src = lax.rem(i, 2), i // 2
        rdma(
            gsrc.at[0], gstage.at[half, src], g_send.at[0], g_recv.at[half, src], row, col
        ).wait_recv()

    each(2 * n_row, g_wait)

    def g_join(r):
        for j in range(2):
            both = jnp.concatenate(
                [gstage[0, r, j].astype(jnp.float32), gstage[1, r, j].astype(jnp.float32)], axis=1
            )
            gblk_ref[j, r] = both.astype(jnp.bfloat16)

    each(n_row, g_join)

    each(n_row - 1, lambda i: o_arrived(lax.rem(row + 1 + i, n_row), 1 - core))
    own_o.wait()

    def q_done(i):
        @pl.when(jnp.logical_or(i > 0, jnp.logical_not(q_self)))
        def _():
            q_copy(i).wait_send()

    def g_done(i):
        @pl.when(jnp.logical_or(i > 0, jnp.logical_not(self_row)))
        def _():
            g_copy(i).wait_send()

    each(chips, q_done)
    each(n_col, g_done)
    each(chips - 1, lambda i: w_copy(i).wait_send())
    each(chips, lambda i: w_forward(i).wait_send())
    each(n_row - 1, lambda i: o_copy(i).wait_send())
    each(n_row - 1, lambda i: o_forward(lax.rem(row + 1 + i, n_row)).wait_send())


def sync_weights(qkv_train, gate_up_train, hidden, o_weight, n_row, n_col):
    tok, width_model = hidden.shape
    row_width, part = qkv_train.shape[1:]
    gate_part = gate_up_train.shape[2]
    width = 2 * part
    chips = n_col // 2
    half_rows = n_row // 2
    step = row_width // chips
    fine = step // 2
    bf16, f32 = jnp.bfloat16, jnp.float32
    dma = pltpu.SemaphoreType.DMA
    vmem, anywhere = pl.BlockSpec(memory_space=pltpu.VMEM), pl.BlockSpec(memory_space=pl.ANY)
    return pl.pallas_call(
        functools.partial(sync_body, n_row=n_row, n_col=n_col),
        out_shape=(
            jax.ShapeDtypeStruct((3, tok, width), f32),
            jax.ShapeDtypeStruct((3, n_row, fine, width), bf16),
            jax.ShapeDtypeStruct((2, n_row, fine, 2 * gate_part), bf16),
            jax.ShapeDtypeStruct((n_row * o_weight.shape[0], width_model // n_row), bf16),
        ),
        in_specs=[vmem, anywhere, vmem, anywhere],
        out_specs=(vmem, vmem, vmem, anywhere),
        scratch_shapes=[
            pltpu.VMEM((3, row_width, part), bf16),
            pltpu.VMEM((2, half_rows, 3, step, part), bf16),
            pltpu.VMEM((3, n_row, row_width, width), bf16),
            pltpu.VMEM((2, row_width, gate_part), f32),
            pltpu.VMEM((n_col, 2, fine, gate_part), bf16),
            pltpu.VMEM((2, n_row, 2, fine, gate_part), bf16),
            dma((chips,)),
            dma((2, half_rows)),
            dma((chips,)),
            dma((chips,)),
            dma((chips, 2)),
            dma((n_col,)),
            dma((2, n_row)),
            dma((n_row,)),
            dma((n_row,)),
            dma((n_row, 2)),
            dma((2,)),
        ],
        compiler_params=pltpu.CompilerParams(
            collective_id=1, has_side_effects=True, vmem_limit_bytes=60 << 20
        ),
        cost_estimate=pl.CostEstimate(
            flops=2 * 3 * tok * width_model * width, bytes_accessed=30_000_000, transcendentals=0
        ),
        name="sync_weights",
    )(qkv_train, gate_up_train, hidden, o_weight)


def local(
    hidden, lengths, owner, page_table, qkv_train, qk_gain, o_weight, post_gain, gate_up_train
):
    n_row = lax.axis_size("row")
    n_col = lax.axis_size("col")
    col_index = lax.axis_index("col")
    row_index = lax.axis_index("row")
    tok_rows = hidden.shape[0]
    model_width = hidden.shape[1]
    row_width = model_width // n_row
    col_block = row_width // n_col
    projected, weight_blocks, gate_up_blocks, o_columns = sync_weights(
        qkv_train, gate_up_train, hidden, o_weight, n_row, n_col
    )
    heads_width = projected.shape[2]
    local_heads = heads_width // HD
    query_rows = projected[0]
    key_rows = projected[1]
    value_rows = projected[2]
    query_squares, key_squares = lax.psum(
        (jnp.sum(query_rows * query_rows, axis=1), jnp.sum(key_rows * key_rows, axis=1)), "row"
    )
    full_heads = HEADS * HD
    query_norm = query_rows * inverse_rms(query_squares, full_heads)[:, None] * qk_gain[0]
    key_norm = key_rows * inverse_rms(key_squares, full_heads)[:, None] * qk_gain[1]
    token_index = col_index * tok_rows + jnp.arange(tok_rows, dtype=jnp.int32)
    token_start = locate_tokens(token_index, lengths)
    position = token_index - token_start
    query_rot = rotate_heads(query_norm.reshape(tok_rows, local_heads, HD), position).astype(
        jnp.bfloat16
    ).reshape(tok_rows, heads_width)
    key_rot = (
        rotate_heads(key_norm.reshape(tok_rows, local_heads, HD), position)
        .astype(jnp.bfloat16)
        .reshape(tok_rows, heads_width)
    )
    value_flat = value_rows.astype(jnp.bfloat16)
    kv = lax.all_gather(jnp.stack([key_rot, value_flat]), "col", axis=1, tiled=True)

    prompt_starts = jnp.cumsum(lengths) - lengths
    owned = owner == col_index
    my_start = jnp.sum(jnp.where(owned, prompt_starts, 0))
    my_length = jnp.sum(jnp.where(owned, lengths, 0))
    my_pages = jnp.where(
        jnp.any(owned),
        jnp.sum(jnp.where(owned[:, None], page_table, 0), axis=0),
        jnp.arange(PAGES, dtype=jnp.int32),
    )
    meta = jnp.concatenate([jnp.stack([my_start, my_length]), my_pages]).astype(jnp.int32)
    cache_pages = build_cache(meta, kv)

    reach = -(-(LMAX - 1) // tok_rows)
    span = min(reach + 1, n_col) * tok_rows
    first_key = jnp.maximum(col_index - reach, 0) * tok_rows
    first = jnp.stack([col_index * tok_rows, first_key]).astype(jnp.int32)
    attention = attend(first, token_start[:, None], query_rot, kv, span)

    attention_all = lax.all_gather(attention, "row", axis=1, tiled=True)
    own_out = jnp.dot(attention_all, o_columns, preferred_element_type=jnp.float32)
    out_squares = lax.psum(jnp.sum(own_out * own_out, axis=1), "row")
    normalized = own_out * inverse_rms(out_squares, model_width)[:, None] * post_gain
    residual = lax.dynamic_slice_in_dim(hidden, row_index * row_width, row_width, 1).astype(
        jnp.float32
    )
    layer_out = (residual + normalized).astype(jnp.bfloat16)
    return (layer_out, cache_pages[None], weight_blocks, gate_up_blocks)


def solution(mesh):
    in_specs = (
        P("col", None),
        P(),
        P(),
        P(),
        P(None, "row", "col"),
        P(None, "row"),
        P("row", None),
        P("row"),
        P(None, "row", "col"),
    )
    out_specs = (
        P("col", "row"),
        P("col", None, None, None, "row"),
        P(None, None, "col", "row"),
        P(None, None, "col", "row"),
    )
    return jax.shard_map(local, mesh=mesh, in_specs=in_specs, out_specs=out_specs, check_vma=False)
```

```python
import functools
import math

import jax
import jax.numpy as jnp
from jax import lax
from jax.experimental import pallas as pl
from jax.experimental.pallas import tpu as pltpu
from jax.sharding import PartitionSpec as P

HD = 128
HEADS = 24
PAGE = 128
PAGES = 16
LMAX = 2048

norm_epsilon = 1e-06
rope_theta = 500000.0
big_negative = -1e30


def inverse_rms(squares, features):
    return lax.rsqrt(squares / features + norm_epsilon)


def rotate_heads(inputs, positions):
    half_dim = inputs.shape[-1] // 2
    frequency = rope_theta ** (-2.0 * jnp.arange(half_dim, dtype=jnp.float32) / inputs.shape[-1])
    angles = positions.astype(jnp.float32)[:, None] * frequency[None, :]
    cosine = jnp.cos(angles)[:, None, :]
    sine_part = jnp.sin(angles)[:, None, :]
    lower_half = inputs[..., :half_dim]
    upper_half = inputs[..., half_dim:]
    return jnp.concatenate(
        [
            lower_half * cosine - upper_half * sine_part,
            upper_half * cosine + lower_half * sine_part,
        ],
        axis=-1,
    )


def locate_tokens(token_index, lengths):
    prompt_ends = jnp.cumsum(lengths)
    prompt_starts = prompt_ends - lengths
    segment = jnp.sum((token_index[:, None] >= prompt_ends[None, :]).astype(jnp.int32), axis=1)
    onehot = segment[:, None] == jnp.arange(lengths.shape[0], dtype=jnp.int32)[None, :]
    start = jnp.sum(jnp.where(onehot, prompt_starts[None, :], 0), axis=1)
    return start


ALIGN = 16
WINDOW = PAGE + ALIGN


def cache_body(meta_ref, kv_ref, out_ref):
    tokens = kv_ref.shape[1]
    start, length = meta_ref[0], meta_ref[1]

    @pl.loop(0, PAGES)
    def _(page):
        first = jnp.minimum(start + page * PAGE, tokens - 1)
        base = jnp.minimum((first // ALIGN) * ALIGN, tokens - WINDOW)
        base = pl.multiple_of(base, ALIGN)
        shift = first - base
        slot = meta_ref[2 + page]
        rows = lax.broadcasted_iota(jnp.int32, (PAGE, 1), 0) + page * PAGE
        inside = rows < length
        for part in range(2):
            piece = kv_ref[part, pl.ds(base, WINDOW), :].astype(jnp.float32)
            piece = pltpu.roll(piece, lax.rem(WINDOW - shift, WINDOW), 0)[:PAGE]
            out_ref[slot, part] = jnp.where(inside, piece, 0.0).astype(jnp.bfloat16)


def build_cache(meta, kv):
    width = kv.shape[2]
    return pl.pallas_call(
        cache_body,
        out_shape=jax.ShapeDtypeStruct((PAGES, 2, PAGE, width), jnp.bfloat16),
        in_specs=[
            pl.BlockSpec(memory_space=pltpu.SMEM),
            pl.BlockSpec(memory_space=pltpu.VMEM),
        ],
        out_specs=pl.BlockSpec(memory_space=pltpu.VMEM),
        compiler_params=pltpu.CompilerParams(vmem_limit_bytes=40 << 20),
        cost_estimate=pl.CostEstimate(flops=10_000_000, bytes_accessed=11_000_000, transcendentals=0),
        name="cache_pages",
    )(meta, kv)


def attend_body(first_ref, start_ref, query_ref, kv_ref, out_ref, *, span):
    rows = query_ref.shape[0]
    heads = query_ref.shape[1] // HD
    first_query, first_key = first_ref[0], first_ref[1]
    first_key = pl.multiple_of(first_key, 64)
    query_index = first_query + lax.broadcasted_iota(jnp.int32, (rows, 1), 0)
    key_index = first_key + lax.broadcasted_iota(jnp.int32, (1, span), 1)
    allowed = (key_index <= query_index) & (key_index >= start_ref[...])
    for head in range(heads):
        lanes = slice(head * HD, (head + 1) * HD)
        keys = kv_ref[0, pl.ds(first_key, span), lanes]
        values = kv_ref[1, pl.ds(first_key, span), lanes]
        scores = lax.dot_general(
            query_ref[:, lanes], keys, (((1,), (1,)), ((), ())), preferred_element_type=jnp.float32
        ) * (1.0 / math.sqrt(HD))
        scores = jnp.where(allowed, scores, big_negative)
        exponent = jnp.exp(scores - jnp.max(scores, axis=1, keepdims=True))
        total = jnp.sum(exponent, axis=1, keepdims=True)
        mixed = jnp.dot(exponent.astype(jnp.bfloat16), values, preferred_element_type=jnp.float32)
        out_ref[:, lanes] = (mixed / total).astype(jnp.bfloat16)


def attend(first, start, query, kv, span):
    return pl.pallas_call(
        functools.partial(attend_body, span=span),
        out_shape=jax.ShapeDtypeStruct(query.shape, jnp.bfloat16),
        in_specs=[pl.BlockSpec(memory_space=pltpu.SMEM)]
        + [pl.BlockSpec(memory_space=pltpu.VMEM)] * 3,
        out_specs=pl.BlockSpec(memory_space=pltpu.VMEM),
        compiler_params=pltpu.CompilerParams(vmem_limit_bytes=48 << 20),
        cost_estimate=pl.CostEstimate(
            flops=4 * query.shape[0] * span * query.shape[1],
            bytes_accessed=8_000_000,
            transcendentals=3 * query.shape[0] * span,
        ),
        name="attend",
    )(first, start, query, kv)


def rdma(src, dst, send_sem, recv_sem, device):
    return pltpu.make_async_remote_copy(
        src_ref=src,
        dst_ref=dst,
        send_sem=send_sem,
        recv_sem=recv_sem,
        device_id=device,
        device_id_type=pl.DeviceIdType.MESH,
    )


def arrived(ref, recv_sem, send_sem, here):
    rdma(ref, ref, send_sem, recv_sem, here).wait_recv()


def each(count, body):
    lax.fori_loop(0, count, lambda i, carry: (body(i), carry)[1], 0)


def wrap(value, size):
    return lax.rem(value + size, size)


class Place:
    def __init__(self):
        self.row, self.col = lax.axis_index("row"), lax.axis_index("col")
        self.y, self.zl = self.row // 2, lax.rem(self.row, 2)
        self.zh, self.x, self.core = self.col // 8, lax.rem(self.col // 2, 4), lax.rem(self.col, 2)
        self.chip = self.col // 2
        self.here = (self.row, self.col)

    def at(self, y=None, zl=None, zh=None, x=None, core=None):
        y, zl = (self.y if y is None else y), (self.zl if zl is None else zl)
        zh, x = (self.zh if zh is None else zh), (self.x if x is None else x)
        core = self.core if core is None else core
        return (2 * y + zl, 8 * zh + 2 * x + core)


def signal(sem, device):
    pl.semaphore_signal(sem, inc=1, device_id=device, device_id_type=pl.DeviceIdType.MESH)


class Relay:
    def __init__(self, me, src, stages, send, recv):
        self.me, self.src, self.stages, self.send, self.recv = me, src, stages, send, recv

    def go(self, away, stage, number, slot, src, device):
        dst, recv = self.stages[stage].at[slot], self.recv.at[stage, slot]

        @pl.when(away)
        def _():
            rdma(src, dst, self.send.at[stage, number], recv, device).start()

        @pl.when(jnp.logical_not(away))
        def _():
            pltpu.make_async_copy(src, dst, recv).start()

    def got(self, stage, slot):
        arrived(
            self.stages[stage].at[slot], self.recv.at[stage, slot], self.send.at[stage, 0],
            self.me.here,
        )

    def first(self):
        me = self.me

        def send(i):
            dx, dk, zh = i // 4, lax.rem(i // 2, 2), lax.rem(i, 2)
            x, core = lax.rem(me.x + dx, 4), lax.rem(me.core + dk, 2)
            device = me.at(x=x, core=core)
            slot = (me.x * 2 + me.core) * 2 + zh
            self.go(i >= 2, 0, i, slot, self.src.at[zh * 8 + 2 * x + core], device)

        each(16, send)

    def second(self):
        me = self.me

        def send(i):
            dx, ks, zh = i // 4, lax.rem(i // 2, 2), lax.rem(i, 2)
            xs = wrap(me.x - dx, 4)
            came = (xs * 2 + ks) * 2 + zh
            self.got(0, came)
            zl = lax.rem(xs, 2)
            away = jnp.logical_or(zl != me.zl, zh != me.zh)
            slot = ((me.zh * 2 + me.zl) * 2 + xs // 2) * 2 + ks
            self.go(away, 1, came, slot, self.stages[0].at[came], me.at(zl=zl, zh=zh))

        each(16, send)

    def third(self):
        me = self.me

        def send(i):
            zs = lax.rem(me.zh * 2 + me.zl + i // 4, 4)
            xh, ks = lax.rem(i // 2, 2), lax.rem(i, 2)
            came = (zs * 2 + xh) * 2 + ks
            self.got(1, came)
            y = (zs // 2) * 2 + xh
            slot = ks * 8 + me.y * 2 + lax.rem(zs, 2)
            self.go(y != me.y, 2, came, slot, self.stages[1].at[came], me.at(y=y))

        each(16, send)

    def last(self):
        each(16, lambda i: self.got(2, i))

    def drain(self):
        me = self.me

        def sent(away, stage, number):
            @pl.when(away)
            def _():
                rdma(
                    self.src.at[0], self.src.at[0], self.send.at[stage, number],
                    self.recv.at[stage, 0], me.here,
                ).wait_send()

        def each_piece(i):
            sent(i >= 2, 0, i)
            xs, zh = i // 4, lax.rem(i, 2)
            sent(jnp.logical_or(lax.rem(xs, 2) != me.zl, zh != me.zh), 1, i)
            zs, xh = i // 4, lax.rem(i // 2, 2)
            sent((zs // 2) * 2 + xh != me.y, 2, i)

        each(16, each_piece)


class ColGather:
    def __init__(self, me, view, send, recv):
        self.me, self.view, self.send, self.recv = me, view, send, recv
        self.sent = []

    def chip(self, dz, dx):
        return wrap(self.me.zh + dz, 2) * 4 + wrap(self.me.x + dx, 4)

    def copy(self, chip, half, kind):
        me = self.me
        device = [
            me.at(x=wrap(me.x + 1, 4)), me.at(x=wrap(me.x - 1, 4)), me.at(zh=1 - me.zh),
            me.at(core=1 - me.core),
        ][kind]
        ref = self.view(chip, me.core, half)
        return rdma(
            ref, ref, self.send.at[chip, half, kind], self.recv.at[chip, me.core, half], device
        )

    def go(self, chip, half, *kinds):
        for kind in kinds:
            self.copy(chip, half, kind).start()
            self.sent.append((chip, half, kind))

    def got(self, chip, core, half):
        arrived(
            self.view(chip, core, half), self.recv.at[chip, core, half], self.send.at[0, 0, 0],
            self.me.here,
        )

    def start(self):
        for half in range(2):
            self.go(self.chip(0, 0), half, 2, 0, 1, 3)

    def z_turn(self):
        for half in range(2):
            self.got(self.chip(1, 0), self.me.core, half)
            self.go(self.chip(1, 0), half, 0, 1, 3)

    def x_turn(self, dz, *more):
        left, right = self.chip(dz, -1), self.chip(dz, 1)
        core = self.me.core
        self.got(left, core, 0)
        self.go(left, 0, 0, *more, 3)
        self.got(right, core, 1)
        self.go(right, 1, 1, *more, 3)
        self.got(left, core, 1)
        self.go(left, 1, *more, 3)
        self.got(right, core, 0)
        self.go(right, 0, *more, 3)

    def x_end(self, dz, *more):
        for half in range(2):
            self.got(self.chip(dz, 2), self.me.core, half)
            self.go(self.chip(dz, 2), half, *more, 3)

    def z_end(self):
        for dx in (0, -1, 1, 2):
            for half in range(2):
                self.got(self.chip(1, dx), self.me.core, half)
                self.go(self.chip(1, dx), half, 3)

    def sibling(self, dz, dx):
        for half in range(2):
            self.got(self.chip(dz, dx), 1 - self.me.core, half)

    def drain(self):
        for which in self.sent:
            self.copy(*which).wait_send()
        self.sent = []


def sync_body(
    qkv_ref, gate_hbm, hid_ref, ow_hbm,
    proj_ref, qblk_ref, gblk_ref, ocol_ref,
    hid_parts, qsrc, q1, q2, q3, w_all, gf32, gsrc, g1, g2, g3,
    q_send, q_recv, g_send, g_recv, w_send, w_recv, o_send, o_fwd, o_recv, local_sem,
    *, n_row, n_col,
):
    me = Place()
    row, col, core = me.row, me.col, me.core
    width_row = qkv_ref.shape[2]
    fine = width_row // n_col
    bf16, f32 = jnp.bfloat16, jnp.float32

    def fetch(j):
        return pltpu.make_async_copy(gate_hbm.at[j], gf32.at[j], local_sem.at[j])

    for j in range(2):
        fetch(j).start()

    barrier = pltpu.get_barrier_semaphore()
    for i in range(1, 8):
        signal(barrier, me.at(x=lax.rem(me.x + i // 2, 4), core=lax.rem(me.core + i, 2)))
    for i in range(1, 4):
        signal(barrier, me.at(zh=lax.rem(me.zh + i // 2, 2), zl=lax.rem(me.zl + i, 2)))
    for i in range(1, n_row):
        signal(barrier, (lax.rem(row + i, n_row), col))

    for j in range(3):
        turned = qkv_ref[j].T
        for c in range(n_col):
            qsrc[c, j] = turned[c * fine:(c + 1) * fine, :].astype(bf16)
    pl.semaphore_wait(barrier, 7 + 3 + n_row - 1)

    qkv = Relay(me, qsrc, (q1, q2, q3), q_send, q_recv)
    gate = Relay(me, gsrc, (g1, g2, g3), g_send, g_recv)
    qkv.first()
    for j in range(2):
        fetch(j).wait()
        turned = gf32[j].T
        for c in range(n_col):
            gsrc[c, j] = turned[c * fine:(c + 1) * fine, :].astype(bf16)
    qkv.second()
    gate.first()
    qkv.third()
    qkv.last()

    def join(stage, r, j):
        return jnp.concatenate(
            [stage[r, j].astype(f32), stage[n_row + r, j].astype(f32)], axis=1
        )

    for j in range(3):
        for pair in range(n_row // 2):
            first, second = join(q3, 2 * pair, j), join(q3, 2 * pair + 1, j)
            qblk_ref[j, 2 * pair] = first.astype(bf16)
            qblk_ref[j, 2 * pair + 1] = second.astype(bf16)
            both = jnp.concatenate([first, second], axis=0).astype(bf16)
            w_all[me.chip, core, j, pair * 2 * fine:(pair + 1) * 2 * fine, :] = both

    depth = w_all.shape[3] // 2
    weights = ColGather(me, lambda p, k, h: w_all.at[p, k, :, h * depth:(h + 1) * depth, :], w_send, w_recv)
    weights.start()

    own_rows = ow_hbm.shape[0]
    half_o = own_rows // 2
    out_width = ocol_ref.shape[1]

    def o_src(to_row):
        return ow_hbm.at[
            pl.ds(pl.multiple_of(core * half_o, 16), half_o),
            pl.ds(pl.multiple_of(to_row * out_width, 128), out_width),
        ]

    def o_dst(of_row, of_core):
        return ocol_ref.at[
            pl.ds(pl.multiple_of(of_row * own_rows + of_core * half_o, 16), half_o), :
        ]

    def o_copy(i):
        to_row = lax.rem(row + 1 + i, n_row)
        return rdma(
            o_src(to_row), o_dst(row, core), o_send.at[i], o_recv.at[row, core], (to_row, col)
        )

    def o_forward(of_row):
        return rdma(
            o_dst(of_row, core), o_dst(of_row, core), o_fwd.at[of_row], o_recv.at[of_row, core],
            me.at(core=1 - core),
        )

    def o_arrived(of_row, of_core):
        arrived(o_dst(of_row, of_core), o_recv.at[of_row, of_core], o_send.at[0], me.here)

    own_o = pltpu.make_async_copy(
        ow_hbm.at[:, pl.ds(pl.multiple_of(row * out_width, 128), out_width)],
        ocol_ref.at[pl.ds(pl.multiple_of(row * own_rows, 16), own_rows), :],
        local_sem.at[2],
    )
    own_o.start()

    def part(c):
        return jnp.concatenate(
            [
                hid_ref[:, r * width_row + c * fine:r * width_row + (c + 1) * fine].astype(f32)
                for r in range(n_row)
            ],
            axis=1,
        ).astype(bf16)

    for c in range(n_col):
        hid_parts[c] = part(c)

    gate.second()
    weights.z_turn()
    each(n_row - 1, lambda i: o_copy(i).start())
    weights.x_turn(0)
    weights.x_turn(1)
    gate.third()
    weights.x_end(0)
    weights.x_end(1)

    for j in range(3):
        proj_ref[j] = jnp.zeros_like(proj_ref[j])

    def project(chip, of_core):
        lhs = hid_parts[2 * chip + of_core]
        for j in range(3):
            proj_ref[j] += jnp.dot(lhs, w_all[chip, of_core, j], preferred_element_type=f32)

    each(n_col // 2, lambda chip: project(chip, core))
    for dz in range(2):
        for dx in (0, -1, 1, 2):
            weights.sibling(dz, dx)
    each(n_col // 2, lambda chip: project(chip, 1 - core))

    def o_relay(i):
        of_row = lax.rem(row + n_row - 1 - i, n_row)
        o_arrived(of_row, core)
        o_forward(of_row).start()

    each(n_row - 1, o_relay)
    gate.last()

    def g_join(r):
        for j in range(2):
            gblk_ref[j, r] = join(g3, r, j).astype(bf16)

    each(n_row, g_join)
    each(n_row - 1, lambda i: o_arrived(lax.rem(row + 1 + i, n_row), 1 - core))
    own_o.wait()
    qkv.drain()
    gate.drain()
    weights.drain()
    each(n_row - 1, lambda i: o_copy(i).wait_send())
    each(n_row - 1, lambda i: o_forward(lax.rem(row + 1 + i, n_row)).wait_send())


def sync_weights(qkv_train, gate_up_train, hidden, o_weight, n_row, n_col):
    tok, width_model = hidden.shape
    row_width, part = qkv_train.shape[1:]
    gate_part = gate_up_train.shape[2]
    width = 2 * part
    fine = row_width // n_col
    bf16, f32 = jnp.bfloat16, jnp.float32
    dma = pltpu.SemaphoreType.DMA
    vmem, anywhere = pl.BlockSpec(memory_space=pltpu.VMEM), pl.BlockSpec(memory_space=pl.ANY)
    q_piece = pltpu.VMEM((n_col, 3, fine, part), bf16)
    g_piece = pltpu.VMEM((n_col, 2, fine, gate_part), bf16)
    return pl.pallas_call(
        functools.partial(sync_body, n_row=n_row, n_col=n_col),
        out_shape=(
            jax.ShapeDtypeStruct((3, tok, width), f32),
            jax.ShapeDtypeStruct((3, n_row, fine, width), bf16),
            jax.ShapeDtypeStruct((2, n_row, fine, 2 * gate_part), bf16),
            jax.ShapeDtypeStruct((n_row * o_weight.shape[0], width_model // n_row), bf16),
        ),
        in_specs=[vmem, anywhere, vmem, anywhere],
        out_specs=(vmem, vmem, vmem, anywhere),
        scratch_shapes=[
            pltpu.VMEM((n_col, tok, n_row * fine), bf16),
            q_piece, q_piece, q_piece, q_piece,
            pltpu.VMEM((n_col // 2, 2, 3, n_row * fine, width), bf16),
            pltpu.VMEM((2, gate_part, row_width), f32),
            g_piece, g_piece, g_piece, g_piece,
            dma((3, n_col)),
            dma((3, n_col)),
            dma((3, n_col)),
            dma((3, n_col)),
            dma((n_col // 2, 2, 4)),
            dma((n_col // 2, 2, 2)),
            dma((n_row,)),
            dma((n_row,)),
            dma((n_row, 2)),
            dma((3,)),
        ],
        compiler_params=pltpu.CompilerParams(
            collective_id=1, has_side_effects=True, vmem_limit_bytes=60 << 20
        ),
        cost_estimate=pl.CostEstimate(
            flops=2 * 3 * tok * width_model * width, bytes_accessed=30_000_000, transcendentals=0
        ),
        name="sync_weights",
    )(qkv_train.swapaxes(1, 2), gate_up_train.swapaxes(1, 2), hidden, o_weight)


def local(
    hidden, lengths, owner, page_table, qkv_train, qk_gain, o_weight, post_gain, gate_up_train
):
    n_row = lax.axis_size("row")
    n_col = lax.axis_size("col")
    col_index = lax.axis_index("col")
    row_index = lax.axis_index("row")
    tok_rows = hidden.shape[0]
    model_width = hidden.shape[1]
    row_width = model_width // n_row
    col_block = row_width // n_col
    projected, weight_blocks, gate_up_blocks, o_columns = sync_weights(
        qkv_train, gate_up_train, hidden, o_weight, n_row, n_col
    )
    heads_width = projected.shape[2]
    local_heads = heads_width // HD
    query_rows = projected[0]
    key_rows = projected[1]
    value_rows = projected[2]
    query_squares, key_squares = lax.psum(
        (jnp.sum(query_rows * query_rows, axis=1), jnp.sum(key_rows * key_rows, axis=1)), "row"
    )
    full_heads = HEADS * HD
    query_norm = query_rows * inverse_rms(query_squares, full_heads)[:, None] * qk_gain[0]
    key_norm = key_rows * inverse_rms(key_squares, full_heads)[:, None] * qk_gain[1]
    token_index = col_index * tok_rows + jnp.arange(tok_rows, dtype=jnp.int32)
    token_start = locate_tokens(token_index, lengths)
    position = token_index - token_start
    query_rot = rotate_heads(query_norm.reshape(tok_rows, local_heads, HD), position).astype(
        jnp.bfloat16
    ).reshape(tok_rows, heads_width)
    key_rot = (
        rotate_heads(key_norm.reshape(tok_rows, local_heads, HD), position)
        .astype(jnp.bfloat16)
        .reshape(tok_rows, heads_width)
    )
    value_flat = value_rows.astype(jnp.bfloat16)
    kv = lax.all_gather(jnp.stack([key_rot, value_flat]), "col", axis=1, tiled=True)

    prompt_starts = jnp.cumsum(lengths) - lengths
    owned = owner == col_index
    my_start = jnp.sum(jnp.where(owned, prompt_starts, 0))
    my_length = jnp.sum(jnp.where(owned, lengths, 0))
    my_pages = jnp.where(
        jnp.any(owned),
        jnp.sum(jnp.where(owned[:, None], page_table, 0), axis=0),
        jnp.arange(PAGES, dtype=jnp.int32),
    )
    meta = jnp.concatenate([jnp.stack([my_start, my_length]), my_pages]).astype(jnp.int32)
    cache_pages = build_cache(meta, kv)

    reach = -(-(LMAX - 1) // tok_rows)
    span = min(reach + 1, n_col) * tok_rows
    first_key = jnp.maximum(col_index - reach, 0) * tok_rows
    first = jnp.stack([col_index * tok_rows, first_key]).astype(jnp.int32)
    attention = attend(first, token_start[:, None], query_rot, kv, span)

    attention_all = lax.all_gather(attention, "row", axis=1, tiled=True)
    own_out = jnp.dot(attention_all, o_columns, preferred_element_type=jnp.float32)
    out_squares = lax.psum(jnp.sum(own_out * own_out, axis=1), "row")
    normalized = own_out * inverse_rms(out_squares, model_width)[:, None] * post_gain
    residual = lax.dynamic_slice_in_dim(hidden, row_index * row_width, row_width, 1).astype(
        jnp.float32
    )
    layer_out = (residual + normalized).astype(jnp.bfloat16)
    return (layer_out, cache_pages[None], weight_blocks, gate_up_blocks)


def solution(mesh):
    in_specs = (
        P("col", None),
        P(),
        P(),
        P(),
        P(None, "row", "col"),
        P(None, "row"),
        P("row", None),
        P("row"),
        P(None, "row", "col"),
    )
    out_specs = (
        P("col", "row"),
        P("col", None, None, None, "row"),
        P(None, None, "col", "row"),
        P(None, None, "col", "row"),
    )
    return jax.shard_map(local, mesh=mesh, in_specs=in_specs, out_specs=out_specs, check_vma=False)
```

```python
import functools
import math

import jax
import jax.numpy as jnp
from jax import lax
from jax.experimental import pallas as pl
from jax.experimental.pallas import tpu as pltpu
from jax.sharding import PartitionSpec as P

HD = 128
HEADS = 24
PAGE = 128
PAGES = 16
LMAX = 2048

norm_epsilon = 1e-06
rope_theta = 500000.0
big_negative = -1e30


def locate_tokens(token_index, lengths):
    prompt_ends = jnp.cumsum(lengths)
    prompt_starts = prompt_ends - lengths
    segment = jnp.sum((token_index[:, None] >= prompt_ends[None, :]).astype(jnp.int32), axis=1)
    onehot = segment[:, None] == jnp.arange(lengths.shape[0], dtype=jnp.int32)[None, :]
    start = jnp.sum(jnp.where(onehot, prompt_starts[None, :], 0), axis=1)
    return start


ALIGN = 16
WINDOW = PAGE + ALIGN


def rdma(src, dst, send_sem, recv_sem, device):
    return pltpu.make_async_remote_copy(
        src_ref=src,
        dst_ref=dst,
        send_sem=send_sem,
        recv_sem=recv_sem,
        device_id=device,
        device_id_type=pl.DeviceIdType.MESH,
    )


def arrived(ref, recv_sem, send_sem, here):
    rdma(ref, ref, send_sem, recv_sem, here).wait_recv()


def each(count, body):
    lax.fori_loop(0, count, lambda i, carry: (body(i), carry)[1], 0)


def wrap(value, size):
    return lax.rem(value + size, size)


class Place:
    def __init__(self):
        self.row, self.col = lax.axis_index("row"), lax.axis_index("col")
        self.y, self.zl = self.row // 2, lax.rem(self.row, 2)
        self.zh, self.x, self.core = self.col // 8, lax.rem(self.col // 2, 4), lax.rem(self.col, 2)
        self.chip = self.col // 2
        self.here = (self.row, self.col)

    def at(self, y=None, zl=None, zh=None, x=None, core=None):
        y, zl = (self.y if y is None else y), (self.zl if zl is None else zl)
        zh, x = (self.zh if zh is None else zh), (self.x if x is None else x)
        core = self.core if core is None else core
        return (2 * y + zl, 8 * zh + 2 * x + core)


def signal(sem, device):
    pl.semaphore_signal(sem, inc=1, device_id=device, device_id_type=pl.DeviceIdType.MESH)


class Relay:
    def __init__(self, me, src, stages, send, recv):
        self.me, self.src, self.stages, self.send, self.recv = me, src, stages, send, recv

    def go(self, away, stage, number, slot, src, device):
        dst, recv = self.stages[stage].at[slot], self.recv.at[stage, slot]

        @pl.when(away)
        def _():
            rdma(src, dst, self.send.at[stage, number], recv, device).start()

        @pl.when(jnp.logical_not(away))
        def _():
            pltpu.make_async_copy(src, dst, recv).start()

    def got(self, stage, slot):
        arrived(
            self.stages[stage].at[slot], self.recv.at[stage, slot], self.send.at[stage, 0],
            self.me.here,
        )

    def first(self):
        me = self.me

        def send(i):
            dx, dk, zh = i // 4, lax.rem(i // 2, 2), lax.rem(i, 2)
            x, core = lax.rem(me.x + dx, 4), lax.rem(me.core + dk, 2)
            device = me.at(x=x, core=core)
            slot = (me.x * 2 + me.core) * 2 + zh
            self.go(i >= 2, 0, i, slot, self.src.at[zh * 8 + 2 * x + core], device)

        each(16, send)

    def second(self):
        me = self.me

        def send(i):
            dx, ks, zh = i // 4, lax.rem(i // 2, 2), lax.rem(i, 2)
            xs = wrap(me.x - dx, 4)
            came = (xs * 2 + ks) * 2 + zh
            self.got(0, came)
            zl = lax.rem(xs, 2)
            away = jnp.logical_or(zl != me.zl, zh != me.zh)
            slot = ((me.zh * 2 + me.zl) * 2 + xs // 2) * 2 + ks
            self.go(away, 1, came, slot, self.stages[0].at[came], me.at(zl=zl, zh=zh))

        each(16, send)

    def third(self):
        me = self.me

        def send(i):
            zs = lax.rem(me.zh * 2 + me.zl + i // 4, 4)
            xh, ks = lax.rem(i // 2, 2), lax.rem(i, 2)
            came = (zs * 2 + xh) * 2 + ks
            self.got(1, came)
            y = (zs // 2) * 2 + xh
            slot = ks * 8 + me.y * 2 + lax.rem(zs, 2)
            self.go(y != me.y, 2, came, slot, self.stages[1].at[came], me.at(y=y))

        each(16, send)

    def last(self):
        each(16, lambda i: self.got(2, i))

    def drain(self):
        me = self.me

        def sent(away, stage, number):
            @pl.when(away)
            def _():
                rdma(
                    self.src.at[0], self.src.at[0], self.send.at[stage, number],
                    self.recv.at[stage, 0], me.here,
                ).wait_send()

        def each_piece(i):
            sent(i >= 2, 0, i)
            xs, zh = i // 4, lax.rem(i, 2)
            sent(jnp.logical_or(lax.rem(xs, 2) != me.zl, zh != me.zh), 1, i)
            zs, xh = i // 4, lax.rem(i // 2, 2)
            sent((zs // 2) * 2 + xh != me.y, 2, i)

        each(16, each_piece)


class Gather:
    def __init__(self, me, over_col, view, send, recv):
        self.me, self.over_col, self.view, self.send, self.recv = me, over_col, view, send, recv
        self.hand = (3,) if over_col else ()
        self.sent = []

    def block(self, dz, dr):
        me = self.me
        if self.over_col:
            return wrap(me.zh + dz, 2) * 4 + wrap(me.x + dr, 4)
        return wrap(me.y + dr, 4) * 2 + wrap(me.zl + dz, 2)

    def copy(self, dz, dr, half, kind):
        me = self.me
        if kind == 3:
            device = me.at(core=1 - me.core)
        elif kind == 2:
            device = me.at(zh=1 - me.zh) if self.over_col else me.at(zl=1 - me.zl)
        else:
            turn = 1 - 2 * kind
            device = (
                me.at(x=wrap(me.x + turn, 4)) if self.over_col else me.at(y=wrap(me.y + turn, 4))
            )
        block = self.block(dz, dr)
        ref = self.view(block, me.core, half)
        return rdma(
            ref, ref, self.send.at[block, half, kind], self.recv.at[block, me.core, half], device
        )

    def go(self, dz, dr, half, *kinds):
        for kind in kinds + self.hand:
            self.copy(dz, dr, half, kind).start()
            self.sent.append((dz, dr, half, kind))

    def got(self, dz, dr, half, sibling=False):
        block = self.block(dz, dr)
        core = 1 - self.me.core if sibling else self.me.core
        arrived(
            self.view(block, core, half), self.recv.at[block, core, half], self.send.at[0, 0, 0],
            self.me.here,
        )

    def start(self, half):
        self.go(0, 0, half, 2, 0, 1)

    def z_turn(self):
        for half in range(2):
            self.got(1, 0, half)
            self.go(1, 0, half, 0, 1)

    def x_turn(self, dz, *more):
        self.got(dz, -1, 0)
        self.go(dz, -1, 0, 0, *more)
        self.got(dz, 1, 0)
        self.go(dz, 1, 0, *more)
        self.got(dz, 1, 1)
        self.go(dz, 1, 1, 1, *more)
        self.got(dz, -1, 1)
        self.go(dz, -1, 1, *more)

    def x_end(self, dz, *more):
        for half in range(2):
            self.got(dz, 2, half)
            self.go(dz, 2, half, *more)

    def z_end(self):
        for half in range(2):
            for dr in (0, -1, 1, 2):
                self.got(1, dr, half)
                self.go(1, dr, half)

    def sibling(self, dz, dr):
        for half in range(2):
            self.got(dz, dr, half, sibling=True)

    def drain(self):
        for which in self.sent:
            self.copy(*which).wait_send()
        self.sent = []


def by_core(me, run):
    @pl.when(me.core == 0)
    def _():
        run(True)

    @pl.when(me.core == 1)
    def _():
        run(False)


def sync_body(
    qkv_ref, gate_hbm, hid_ref, ow_hbm,
    proj_ref, qblk_ref, gblk_ref, ocol_ref,
    hid_parts, qsrc, q1, q2, q3, w_all, gf32, gsrc, g1, g2, g3,
    q_send, q_recv, g_send, g_recv, w_send, w_recv, o_send, o_fwd, o_recv, local_sem,
    *, n_row, n_col,
):
    me = Place()
    row, col, core = me.row, me.col, me.core
    width_row = qkv_ref.shape[2]
    fine = width_row // n_col
    bf16, f32 = jnp.bfloat16, jnp.float32

    def fetch(j):
        return pltpu.make_async_copy(gate_hbm.at[j], gf32.at[j], local_sem.at[j])

    for j in range(2):
        fetch(j).start()

    barrier = pltpu.get_barrier_semaphore()
    for i in range(1, 8):
        signal(barrier, me.at(x=lax.rem(me.x + i // 2, 4), core=lax.rem(me.core + i, 2)))
    for i in range(1, 4):
        signal(barrier, me.at(zh=lax.rem(me.zh + i // 2, 2), zl=lax.rem(me.zl + i, 2)))
    for i in range(1, n_row):
        signal(barrier, (lax.rem(row + i, n_row), col))

    for j in range(3):
        turned = qkv_ref[j].T
        for c in range(n_col):
            qsrc[c, j] = turned[c * fine:(c + 1) * fine, :].astype(bf16)
    pl.semaphore_wait(barrier, 7 + 3 + n_row - 1)

    qkv = Relay(me, qsrc, (q1, q2, q3), q_send, q_recv)
    gate = Relay(me, gsrc, (g1, g2, g3), g_send, g_recv)
    qkv.first()
    for j in range(2):
        fetch(j).wait()
        turned = gf32[j].T
        for c in range(n_col):
            gsrc[c, j] = turned[c * fine:(c + 1) * fine, :].astype(bf16)
    qkv.second()
    gate.first()
    qkv.third()
    qkv.last()

    def join(stage, r, j):
        return jnp.concatenate(
            [stage[r, j].astype(f32), stage[n_row + r, j].astype(f32)], axis=1
        )

    for j in range(3):
        for pair in range(n_row // 2):
            first, second = join(q3, 2 * pair, j), join(q3, 2 * pair + 1, j)
            qblk_ref[j, 2 * pair] = first.astype(bf16)
            qblk_ref[j, 2 * pair + 1] = second.astype(bf16)
            both = jnp.concatenate([first, second], axis=0).astype(bf16)
            w_all[me.chip, core, j, pair * 2 * fine:(pair + 1) * 2 * fine, :] = both

    depth = w_all.shape[3] // 2
    weights = Gather(me, True, lambda p, k, h: w_all.at[p, k, :, h * depth:(h + 1) * depth, :], w_send, w_recv)
    weights.start(0)
    weights.start(1)

    own_rows = ow_hbm.shape[0]
    half_o = own_rows // 2
    out_width = ocol_ref.shape[1]

    def o_src(to_row):
        return ow_hbm.at[
            pl.ds(pl.multiple_of(core * half_o, 16), half_o),
            pl.ds(pl.multiple_of(to_row * out_width, 128), out_width),
        ]

    def o_dst(of_row, of_core):
        return ocol_ref.at[
            pl.ds(pl.multiple_of(of_row * own_rows + of_core * half_o, 16), half_o), :
        ]

    def o_copy(i):
        to_row = lax.rem(row + 1 + i, n_row)
        return rdma(
            o_src(to_row), o_dst(row, core), o_send.at[i], o_recv.at[row, core], (to_row, col)
        )

    def o_forward(of_row):
        return rdma(
            o_dst(of_row, core), o_dst(of_row, core), o_fwd.at[of_row], o_recv.at[of_row, core],
            me.at(core=1 - core),
        )

    def o_arrived(of_row, of_core):
        arrived(o_dst(of_row, of_core), o_recv.at[of_row, of_core], o_send.at[0], me.here)

    own_o = pltpu.make_async_copy(
        ow_hbm.at[:, pl.ds(pl.multiple_of(row * out_width, 128), out_width)],
        ocol_ref.at[pl.ds(pl.multiple_of(row * own_rows, 16), own_rows), :],
        local_sem.at[2],
    )
    own_o.start()

    def part(c):
        return jnp.concatenate(
            [
                hid_ref[:, r * width_row + c * fine:r * width_row + (c + 1) * fine].astype(f32)
                for r in range(n_row)
            ],
            axis=1,
        ).astype(bf16)

    for c in range(n_col):
        hid_parts[c] = part(c)

    gate.second()
    weights.z_turn()
    each(n_row - 1, lambda i: o_copy(i).start())
    weights.x_turn(0)
    weights.x_turn(1)
    gate.third()
    weights.x_end(0)
    weights.x_end(1)

    for j in range(3):
        proj_ref[j] = jnp.zeros_like(proj_ref[j])

    def project(chip, of_core):
        lhs = hid_parts[2 * chip + of_core]
        for j in range(3):
            proj_ref[j] += jnp.dot(lhs, w_all[chip, of_core, j], preferred_element_type=f32)

    each(n_col // 2, lambda chip: project(chip, core))
    for dz in range(2):
        for dx in (0, -1, 1, 2):
            weights.sibling(dz, dx)
    each(n_col // 2, lambda chip: project(chip, 1 - core))

    def o_relay(i):
        of_row = lax.rem(row + n_row - 1 - i, n_row)
        o_arrived(of_row, core)
        o_forward(of_row).start()

    each(n_row - 1, o_relay)
    gate.last()

    def g_join(r):
        for j in range(2):
            gblk_ref[j, r] = join(g3, r, j).astype(bf16)

    each(n_row, g_join)
    each(n_row - 1, lambda i: o_arrived(lax.rem(row + 1 + i, n_row), 1 - core))
    own_o.wait()
    qkv.drain()
    gate.drain()
    weights.drain()
    each(n_row - 1, lambda i: o_copy(i).wait_send())
    each(n_row - 1, lambda i: o_forward(lax.rem(row + 1 + i, n_row)).wait_send())


def sync_weights(qkv_train, gate_up_train, hidden, o_weight, n_row, n_col):
    tok, width_model = hidden.shape
    row_width, part = qkv_train.shape[1:]
    gate_part = gate_up_train.shape[2]
    width = 2 * part
    fine = row_width // n_col
    bf16, f32 = jnp.bfloat16, jnp.float32
    dma = pltpu.SemaphoreType.DMA
    vmem, anywhere = pl.BlockSpec(memory_space=pltpu.VMEM), pl.BlockSpec(memory_space=pl.ANY)
    q_piece = pltpu.VMEM((n_col, 3, fine, part), bf16)
    g_piece = pltpu.VMEM((n_col, 2, fine, gate_part), bf16)
    return pl.pallas_call(
        functools.partial(sync_body, n_row=n_row, n_col=n_col),
        out_shape=(
            jax.ShapeDtypeStruct((3, tok, width), f32),
            jax.ShapeDtypeStruct((3, n_row, fine, width), bf16),
            jax.ShapeDtypeStruct((2, n_row, fine, 2 * gate_part), bf16),
            jax.ShapeDtypeStruct((n_row * o_weight.shape[0], width_model // n_row), bf16),
        ),
        in_specs=[vmem, anywhere, vmem, anywhere],
        out_specs=(vmem, vmem, vmem, anywhere),
        scratch_shapes=[
            pltpu.VMEM((n_col, tok, n_row * fine), bf16),
            q_piece, q_piece, q_piece, q_piece,
            pltpu.VMEM((n_col // 2, 2, 3, n_row * fine, width), bf16),
            pltpu.VMEM((2, gate_part, row_width), f32),
            g_piece, g_piece, g_piece, g_piece,
            dma((3, n_col)),
            dma((3, n_col)),
            dma((3, n_col)),
            dma((3, n_col)),
            dma((n_col // 2, 2, 4)),
            dma((n_col // 2, 2, 2)),
            dma((n_row,)),
            dma((n_row,)),
            dma((n_row, 2)),
            dma((3,)),
        ],
        compiler_params=pltpu.CompilerParams(
            collective_id=1, has_side_effects=True, vmem_limit_bytes=60 << 20
        ),
        cost_estimate=pl.CostEstimate(
            flops=2 * 3 * tok * width_model * width, bytes_accessed=30_000_000, transcendentals=0
        ),
        name="sync_weights",
    )(qkv_train.swapaxes(1, 2), gate_up_train.swapaxes(1, 2), hidden, o_weight)


def column_of(sums, at_row):
    pick = (lax.broadcasted_iota(jnp.int32, (8, 128), 0) == at_row).astype(jnp.float32)
    return lax.dot_general(
        sums, pick, (((0,), (0,)), ((), ())),
        precision=lax.Precision.HIGHEST, preferred_element_type=jnp.float32,
    )


def lane_sums(values):
    return lax.dot_general(
        jnp.ones((8, values.shape[1]), jnp.float32), values * values, (((1,), (1,)), ((), ())),
        precision=lax.Precision.HIGHEST, preferred_element_type=jnp.float32,
    )


def layer_body(
    proj_ref, cos_ref, sin_ref, gain_ref, start_ref, ocol_ref, post_ref, hid_hbm,
    out_ref, kv_out,
    query, kv, mixed_all, residual, sq_in, sq_out,
    kv_send, kv_recv, a_send, a_recv, s_send, s_recv, t_send, t_recv, local_sem,
    *, n_row, n_col,
):
    me = Place()
    row, col = me.row, me.col
    bf16, f32 = jnp.bfloat16, jnp.float32
    tok, width = query.shape
    heads = width // HD
    out_width = out_ref.shape[1]
    keep = pltpu.make_async_copy(
        hid_hbm.at[:, pl.ds(pl.multiple_of(row * out_width, 128), out_width)], residual, local_sem.at[0]
    )
    keep.start()

    barrier = pltpu.get_barrier_semaphore()
    signal(barrier, me.at(x=wrap(me.x + 1, 4)))
    signal(barrier, me.at(x=wrap(me.x - 1, 4)))
    signal(barrier, me.at(zh=1 - me.zh))
    signal(barrier, me.at(core=1 - me.core))
    for i in range(1, n_row):
        signal(barrier, (lax.rem(row + i, n_row), col))

    own = pl.ds(pl.multiple_of(col * tok, 64), tok)
    kv[1, own, :] = proj_ref[2].astype(bf16)
    top = lax.broadcasted_iota(jnp.int32, (8, tok), 0) < 4
    sq_in[row] = jnp.where(top, lane_sums(proj_ref[0]), lane_sums(proj_ref[1]))
    pl.semaphore_wait(barrier, 4 + n_row - 1)

    def share(buffer, send, recv, i):
        return rdma(
            buffer.at[row], buffer.at[row], send.at[i], recv.at[row],
            (lax.rem(row + 1 + i, n_row), col),
        )

    def shared(buffer, send, recv):
        def wait(i):
            src = lax.rem(row + 1 + i, n_row)
            arrived(buffer.at[src], recv.at[src], send.at[0], me.here)

        each(n_row - 1, wait)
        total = buffer[0]
        for src in range(1, n_row):
            total = total + buffer[src]
        return total

    each(n_row - 1, lambda i: share(sq_in, s_send, s_recv, i).start())

    def tokens_of(block, core, half):
        rows = pl.ds(pl.multiple_of((2 * block + core) * tok, 64), tok)
        return kv.at[1 - half, rows, :]

    gathers = [Gather(me, True, tokens_of, kv_send, kv_recv) for _ in range(2)]
    first_sends = Gather(me, True, tokens_of, kv_send, kv_recv)
    first_sends.start(0)

    squares = shared(sq_in, s_send, s_recv)
    cosine, sine = cos_ref[...], sin_ref[...]
    for which in (1, 0):
        scale = lax.rsqrt(column_of(squares, 4 * which) / (n_row * width) + norm_epsilon)
        for head in range(heads):
            lanes = slice(head * HD, (head + 1) * HD)
            x = proj_ref[which, :, lanes] * scale * gain_ref[which:which + 1, lanes]
            turned = (x * cosine + pltpu.roll(x, HD // 2, 1) * sine).astype(bf16)
            if which == 1:
                kv[0, own, lanes] = turned
            else:
                query[:, lanes] = turned
        if which == 1:
            first_sends.start(1)

    def kv_gather(z_first):
        g = gathers[0 if z_first else 1]
        if z_first:
            g.z_turn()
            g.x_turn(0)
            g.x_turn(1)
            g.x_end(0)
            g.x_end(1)
        else:
            g.x_turn(0, 2)
            g.x_end(0, 2)
            g.z_end()

    by_core(me, kv_gather)
    for dz in range(2):
        for dx in range(4):
            if (dz, dx) != (0, 0):
                gathers[0].sibling(dz, dx)
    gathers[0].sibling(0, 0)

    give = pltpu.make_async_copy(kv, kv_out, local_sem.at[1])
    give.start()

    reach = -(-(LMAX - 1) // tok)
    span = min(reach + 1, n_col) * tok
    first_key = pl.multiple_of(jnp.maximum(col - reach, 0) * tok, 64)
    query_index = col * tok + lax.broadcasted_iota(jnp.int32, (tok, 1), 0)
    key_index = first_key + lax.broadcasted_iota(jnp.int32, (1, span), 1)
    allowed = (key_index <= query_index) & (key_index >= start_ref[...])
    for head in range(heads):
        lanes = slice(head * HD, (head + 1) * HD)
        keys = kv[0, pl.ds(first_key, span), lanes]
        values = kv[1, pl.ds(first_key, span), lanes]
        scores = lax.dot_general(
            query[:, lanes], keys, (((1,), (1,)), ((), ())), preferred_element_type=f32
        ) * (1.0 / math.sqrt(HD))
        scores = jnp.where(allowed, scores, big_negative)
        exponent = jnp.exp(scores - jnp.max(scores, axis=1, keepdims=True))
        total = jnp.sum(exponent, axis=1, keepdims=True)
        mixed = jnp.dot(exponent.astype(bf16), values, preferred_element_type=f32)
        mixed_all[row, :, lanes] = (mixed / total).astype(bf16)

    half_tok = tok // 2
    row_gathers = [
        Gather(
            me, False,
            lambda block, core, half: mixed_all.at[block, pl.ds(half * half_tok, half_tok), :],
            a_send, a_recv,
        )
        for _ in range(2)
    ]

    def row_gather(z_first):
        g = row_gathers[0 if z_first else 1]
        g.start(0)
        g.start(1)
        if z_first:
            g.z_turn()
            g.x_turn(0)
            g.x_turn(1)
            g.x_end(0)
            g.x_end(1)
        else:
            g.x_turn(0, 2)
            g.x_end(0, 2)
            g.z_end()

    by_core(me, row_gather)

    product = jnp.zeros((tok, out_width), f32)
    for src in range(n_row):
        product += jnp.dot(
            mixed_all[src], ocol_ref[src * width:(src + 1) * width, :], preferred_element_type=f32
        )
    sq_out[row] = lane_sums(product)
    each(n_row - 1, lambda i: share(sq_out, t_send, t_recv, i).start())
    keep.wait()

    each(n_row - 1, lambda i: share(sq_in, s_send, s_recv, i).wait_send())
    first_sends.drain()

    def drain(z_first):
        which = 0 if z_first else 1
        gathers[which].drain()
        row_gathers[which].drain()

    by_core(me, drain)

    scale = lax.rsqrt(column_of(shared(sq_out, t_send, t_recv), 0) / (n_row * out_width) + norm_epsilon)
    for at in range(0, out_width, 128):
        lanes = slice(at, at + 128)
        out_ref[:, lanes] = (
            residual[:, lanes].astype(f32) + product[:, lanes] * scale * post_ref[:, lanes]
        ).astype(bf16)
    each(n_row - 1, lambda i: share(sq_out, t_send, t_recv, i).wait_send())
    give.wait()


def attention_layer(projected, cosine, sine, gain, start, o_columns, post, hidden, n_row, n_col):
    _, tok, width = projected.shape
    out_width = o_columns.shape[1]
    bf16, f32 = jnp.bfloat16, jnp.float32
    dma = pltpu.SemaphoreType.DMA
    vmem, anywhere = pl.BlockSpec(memory_space=pltpu.VMEM), pl.BlockSpec(memory_space=pl.ANY)
    return pl.pallas_call(
        functools.partial(layer_body, n_row=n_row, n_col=n_col),
        out_shape=(
            jax.ShapeDtypeStruct((tok, out_width), bf16),
            jax.ShapeDtypeStruct((2, n_col * tok, width), bf16),
        ),
        in_specs=[vmem] * 7 + [anywhere],
        out_specs=(vmem, anywhere),
        scratch_shapes=[
            pltpu.VMEM((tok, width), bf16),
            pltpu.VMEM((2, n_col * tok, width), bf16),
            pltpu.VMEM((n_row, tok, width), bf16),
            pltpu.VMEM((tok, out_width), bf16),
            pltpu.VMEM((n_row, 8, tok), f32),
            pltpu.VMEM((n_row, 8, tok), f32),
            dma((n_col // 2, 2, 4)),
            dma((n_col // 2, 2, 2)),
            dma((n_row, 2, 4)),
            dma((n_row, 2, 2)),
            dma((n_row,)),
            dma((n_row,)),
            dma((n_row,)),
            dma((n_row,)),
            dma((2,)),
        ],
        compiler_params=pltpu.CompilerParams(
            collective_id=2, has_side_effects=True, vmem_limit_bytes=60 << 20
        ),
        cost_estimate=pl.CostEstimate(
            flops=8_000_000_000, bytes_accessed=20_000_000, transcendentals=3_000_000
        ),
        name="attention_layer",
    )(projected, cosine, sine, gain, start, o_columns, post, hidden)


def cache_body(meta_ref, kv_hbm, out_ref, windows, sems):
    tokens = kv_hbm.shape[1]
    begin, length = meta_ref[0], meta_ref[1]

    def locate(slot):
        first = jnp.minimum(begin + meta_ref[2 + slot] * PAGE, tokens - 1)
        base = pl.multiple_of(jnp.minimum((first // ALIGN) * ALIGN, tokens - WINDOW), ALIGN)
        return first, base

    def fetch(slot):
        _, base = locate(slot)
        return pltpu.make_async_copy(
            kv_hbm.at[:, pl.ds(base, WINDOW), :], windows.at[slot], sems.at[slot]
        )

    each(PAGES, lambda slot: fetch(slot).start())

    def place(slot):
        fetch(slot).wait()
        first, base = locate(slot)
        turn = lax.rem(WINDOW - (first - base), WINDOW)
        rows = lax.broadcasted_iota(jnp.int32, (PAGE, 1), 0) + meta_ref[2 + slot] * PAGE
        for part in range(2):
            piece = pltpu.roll(windows[slot, part].astype(jnp.float32), turn, 0)[:PAGE]
            out_ref[slot, part] = jnp.where(rows < length, piece, 0.0).astype(jnp.bfloat16)

    each(PAGES, place)


def build_cache(meta, kv):
    width = kv.shape[2]
    return pl.pallas_call(
        cache_body,
        out_shape=jax.ShapeDtypeStruct((PAGES, 2, PAGE, width), jnp.bfloat16),
        in_specs=[pl.BlockSpec(memory_space=pltpu.SMEM), pl.BlockSpec(memory_space=pl.ANY)],
        out_specs=pl.BlockSpec(memory_space=pltpu.VMEM),
        scratch_shapes=[
            pltpu.VMEM((PAGES, 2, WINDOW, width), jnp.bfloat16),
            pltpu.SemaphoreType.DMA((PAGES,)),
        ],
        compiler_params=pltpu.CompilerParams(vmem_limit_bytes=16 << 20),
        cost_estimate=pl.CostEstimate(flops=10_000_000, bytes_accessed=7_000_000, transcendentals=0),
        name="cache_pages",
    )(meta, kv)


def local(
    hidden, lengths, owner, page_table, qkv_train, qk_gain, o_weight, post_gain, gate_up_train
):
    n_row = lax.axis_size("row")
    n_col = lax.axis_size("col")
    col_index = lax.axis_index("col")
    tok_rows = hidden.shape[0]
    projected, weight_blocks, gate_up_blocks, o_columns = sync_weights(
        qkv_train, gate_up_train, hidden, o_weight, n_row, n_col
    )
    token_index = col_index * tok_rows + jnp.arange(tok_rows, dtype=jnp.int32)
    token_start = locate_tokens(token_index, lengths)
    half_dim = HD // 2
    frequency = rope_theta ** (-2.0 * jnp.arange(half_dim, dtype=jnp.float32) / HD)
    angles = (token_index - token_start).astype(jnp.float32)[:, None] * frequency[None, :]
    cosine, sine = jnp.cos(angles), jnp.sin(angles)
    cosine = jnp.concatenate([cosine, cosine], axis=1)
    sine = jnp.concatenate([-sine, sine], axis=1)

    prompt_starts = jnp.cumsum(lengths) - lengths
    owned = owner == col_index
    my_start = jnp.sum(jnp.where(owned, prompt_starts, 0))
    my_length = jnp.sum(jnp.where(owned, lengths, 0))
    my_pages = jnp.sum(jnp.where(owned[:, None], page_table, 0), axis=0)
    slots = jnp.arange(PAGES, dtype=jnp.int32)
    page_of = jnp.sum(jnp.where(my_pages[None, :] == slots[:, None], slots[None, :], 0), axis=1)
    page_of = jnp.where(my_length > 0, page_of, slots)
    meta = jnp.concatenate([jnp.stack([my_start, my_length]), page_of]).astype(jnp.int32)

    layer_out, kv = attention_layer(
        projected, cosine, sine, qk_gain, token_start[:, None], o_columns,
        post_gain[None, :], hidden, n_row, n_col,
    )
    cache_pages = build_cache(meta, kv)
    return (layer_out, cache_pages[None], weight_blocks, gate_up_blocks)


def solution(mesh):
    in_specs = (
        P("col", None),
        P(),
        P(),
        P(),
        P(None, "row", "col"),
        P(None, "row"),
        P("row", None),
        P("row"),
        P(None, "row", "col"),
    )
    out_specs = (
        P("col", "row"),
        P("col", None, None, None, "row"),
        P(None, None, "col", "row"),
        P(None, None, "col", "row"),
    )
    return jax.shard_map(local, mesh=mesh, in_specs=in_specs, out_specs=out_specs, check_vma=False)
```

```python
import functools
import math

import jax
import jax.numpy as jnp
from jax import lax
from jax.experimental import pallas as pl
from jax.experimental.pallas import tpu as pltpu
from jax.sharding import PartitionSpec as P

HD = 128
HEADS = 24
PAGE = 128
PAGES = 16
LMAX = 2048

norm_epsilon = 1e-06
rope_theta = 500000.0
big_negative = -1e30


ALIGN = 16
WINDOW = PAGE + ALIGN


def rdma(src, dst, send_sem, recv_sem, device):
    return pltpu.make_async_remote_copy(
        src_ref=src,
        dst_ref=dst,
        send_sem=send_sem,
        recv_sem=recv_sem,
        device_id=device,
        device_id_type=pl.DeviceIdType.MESH,
    )


def arrived(ref, recv_sem, send_sem, here):
    rdma(ref, ref, send_sem, recv_sem, here).wait_recv()


def each(count, body):
    lax.fori_loop(0, count, lambda i, carry: (body(i), carry)[1], 0)


def wrap(value, size):
    return lax.rem(value + size, size)


class Place:
    def __init__(self):
        self.row, self.col = lax.axis_index("row"), lax.axis_index("col")
        self.y, self.zl = self.row // 2, lax.rem(self.row, 2)
        self.zh, self.x, self.core = self.col // 8, lax.rem(self.col // 2, 4), lax.rem(self.col, 2)
        self.chip = self.col // 2
        self.here = (self.row, self.col)

    def at(self, y=None, zl=None, zh=None, x=None, core=None):
        y, zl = (self.y if y is None else y), (self.zl if zl is None else zl)
        zh, x = (self.zh if zh is None else zh), (self.x if x is None else x)
        core = self.core if core is None else core
        return (2 * y + zl, 8 * zh + 2 * x + core)


def signal(sem, device):
    pl.semaphore_signal(sem, inc=1, device_id=device, device_id_type=pl.DeviceIdType.MESH)


class Relay:
    def __init__(self, me, src, stages, send, recv):
        self.me, self.src, self.stages, self.send, self.recv = me, src, stages, send, recv

    def go(self, i, stage, slot, src, dst, device):
        recv = self.recv.at[stage, slot]
        if i == 0:
            pltpu.make_async_copy(src, dst, recv).start()
        else:
            rdma(src, dst, self.send.at[stage, i], recv, device).start()

    def to(self, stage, slot):
        if stage == 0:
            return self.stages[0].at[slot // 4, lax.rem(slot // 2, 2), lax.rem(slot, 2)]
        if stage == 1:
            return self.stages[1].at[slot // 2, lax.rem(slot, 2)]
        return self.stages[2].at[slot]

    def got(self, stage, count):
        for slot in range(count):
            arrived(
                self.to(stage, slot), self.recv.at[stage, slot], self.send.at[stage, 0],
                self.me.here,
            )

    def first(self):
        me = self.me
        slot = me.x * 2 + me.core
        for i in (3, 5, 2, 7, 4, 6, 1, 0):
            x, core = lax.rem(me.x + i // 2, 4), lax.rem(me.core + i, 2)
            self.go(
                i, 0, slot, self.src.at[:, x * 2 + core], self.to(0, slot), me.at(x=x, core=core)
            )

    def second(self):
        me = self.me
        self.got(0, 8)
        slot = me.zh * 2 + me.zl
        for i in (2, 1, 3, 0):
            z = lax.rem(slot + i, 4)
            zh, zl = z // 2, lax.rem(z, 2)
            self.go(
                i, 1, slot, self.stages[0].at[:, zl, :, zh], self.to(1, slot), me.at(zh=zh, zl=zl)
            )

    def third(self):
        me = self.me
        self.got(1, 4)
        for i in (2, 1, 3, 0):
            y = lax.rem(me.y + i, 4)
            self.go(
                i, 2, me.y, self.stages[1].at[y // 2, :, lax.rem(y, 2)], self.to(2, me.y),
                me.at(y=y),
            )

    def last(self):
        self.got(2, 4)

    def drain(self):
        for stage, count in ((0, 8), (1, 4), (2, 4)):
            for i in range(1, count):
                ref = self.to(stage, 0)
                rdma(
                    ref, ref, self.send.at[stage, i], self.recv.at[stage, 0], self.me.here
                ).wait_send()


class Gather:
    def __init__(self, me, over_col, view, send, recv):
        self.me, self.over_col, self.view, self.send, self.recv = me, over_col, view, send, recv
        self.hand = (3,) if over_col else ()
        self.sent = []

    def block(self, dz, dr):
        me = self.me
        if self.over_col:
            return wrap(me.zh + dz, 2) * 4 + wrap(me.x + dr, 4)
        return wrap(me.y + dr, 4) * 2 + wrap(me.zl + dz, 2)

    def copy(self, dz, dr, half, kind):
        me = self.me
        if kind == 3:
            device = me.at(core=1 - me.core)
        elif kind == 2:
            device = me.at(zh=1 - me.zh) if self.over_col else me.at(zl=1 - me.zl)
        else:
            turn = 1 - 2 * kind
            device = (
                me.at(x=wrap(me.x + turn, 4)) if self.over_col else me.at(y=wrap(me.y + turn, 4))
            )
        block = self.block(dz, dr)
        ref = self.view(block, me.core, half)
        return rdma(
            ref, ref, self.send.at[block, half, kind], self.recv.at[block, me.core, half], device
        )

    def go(self, dz, dr, half, *kinds):
        for kind in kinds + self.hand:
            self.copy(dz, dr, half, kind).start()
            self.sent.append((dz, dr, half, kind))

    def got(self, dz, dr, half, sibling=False):
        block = self.block(dz, dr)
        core = 1 - self.me.core if sibling else self.me.core
        arrived(
            self.view(block, core, half), self.recv.at[block, core, half], self.send.at[0, 0, 0],
            self.me.here,
        )

    def start(self, half):
        self.go(0, 0, half, 2, 0, 1)

    def z_turn(self):
        for half in range(2):
            self.got(1, 0, half)
            self.go(1, 0, half, 0, 1)

    def x_turn(self, dz, *more):
        self.got(dz, -1, 0)
        self.go(dz, -1, 0, 0, *more)
        self.got(dz, 1, 0)
        self.go(dz, 1, 0, *more)
        self.got(dz, 1, 1)
        self.go(dz, 1, 1, 1, *more)
        self.got(dz, -1, 1)
        self.go(dz, -1, 1, *more)

    def x_end(self, dz, *more):
        for half in range(2):
            self.got(dz, 2, half)
            self.go(dz, 2, half, *more)

    def z_end(self):
        for half in range(2):
            for dr in (0, -1, 1, 2):
                self.got(1, dr, half)
                self.go(1, dr, half)

    def sibling(self, dz, dr):
        for half in range(2):
            self.got(dz, dr, half, sibling=True)

    def drain(self):
        for which in self.sent:
            self.copy(*which).wait_send()
        self.sent = []


def by_core(me, run):
    @pl.when(me.core == 0)
    def _():
        run(True)

    @pl.when(me.core == 1)
    def _():
        run(False)


def sync_body(
    qkv_ref, gate_hbm, hid_ref, ow_hbm,
    proj_ref, qblk_ref, gblk_ref, ocol_ref,
    hid_parts, qsrc, q1, q2, q3, w_all, gf32, gsrc, g1, g2, g3,
    q_send, q_recv, g_send, g_recv, w_send, w_recv, o_send, o_fwd, o_recv, local_sem,
    *, n_row, n_col,
):
    me = Place()
    row, col, core = me.row, me.col, me.core
    width_row = qkv_ref.shape[2]
    fine = width_row // n_col
    bf16, f32 = jnp.bfloat16, jnp.float32

    def fetch(j):
        return pltpu.make_async_copy(gate_hbm.at[j], gf32.at[j], local_sem.at[j])

    for j in range(2):
        fetch(j).start()

    barrier = pltpu.get_barrier_semaphore()
    for i in range(1, 8):
        signal(barrier, me.at(x=lax.rem(me.x + i // 2, 4), core=lax.rem(me.core + i, 2)))
    for i in range(1, 4):
        signal(barrier, me.at(zh=lax.rem(me.zh + i // 2, 2), zl=lax.rem(me.zl + i, 2)))
    for i in range(1, n_row):
        signal(barrier, (lax.rem(row + i, n_row), col))

    for j in range(3):
        turned = qkv_ref[j].T
        for c in range(n_col):
            qsrc[c // 8, c % 8, j] = turned[c * fine:(c + 1) * fine, :].astype(bf16)
    pl.semaphore_wait(barrier, 7 + 3 + n_row - 1)

    qkv = Relay(me, qsrc, (q1, q2, q3), q_send, q_recv)
    gate = Relay(me, gsrc, (g1, g2, g3), g_send, g_recv)
    qkv.first()
    for j in range(2):
        fetch(j).wait()
        turned = gf32[j].T
        for c in range(n_col):
            gsrc[c // 8, c % 8, j] = turned[c * fine:(c + 1) * fine, :].astype(bf16)
    gate.first()
    qkv.second()
    qkv.third()
    qkv.last()

    depth = w_all.shape[2] // 4

    def join(stage, r, j):
        return jnp.concatenate(
            [stage[r // 2, r % 2, 0, j].astype(f32), stage[r // 2, r % 2, 1, j].astype(f32)], axis=1
        )

    for j in range(3):
        for pair in range(n_row // 2):
            first, second = join(q3, 2 * pair, j), join(q3, 2 * pair + 1, j)
            qblk_ref[j, 2 * pair] = first.astype(bf16)
            qblk_ref[j, 2 * pair + 1] = second.astype(bf16)
            both = jnp.concatenate([first, second], axis=0).astype(bf16)
            at = pl.multiple_of(core * depth * 2 + pair * 2 * fine, 16)
            w_all[me.chip, j, pl.ds(at, 2 * fine), :] = both


    def weight_rows(chip, of_core, half):
        at = pl.multiple_of((of_core * 2 + half) * depth, 16)
        return w_all.at[chip, :, pl.ds(at, depth), :]

    weights = Gather(me, True, weight_rows, w_send, w_recv)
    weights.start(0)
    weights.start(1)

    own_rows = ow_hbm.shape[0]
    half_o = own_rows // 2
    out_width = ocol_ref.shape[1]

    def o_src(to_row):
        return ow_hbm.at[
            pl.ds(pl.multiple_of(core * half_o, 16), half_o),
            pl.ds(pl.multiple_of(to_row * out_width, 128), out_width),
        ]

    def o_dst(of_row, of_core):
        return ocol_ref.at[
            pl.ds(pl.multiple_of(of_row * own_rows + of_core * half_o, 16), half_o), :
        ]

    def o_copy(i):
        to_row = lax.rem(row + 1 + i, n_row)
        return rdma(
            o_src(to_row), o_dst(row, core), o_send.at[i], o_recv.at[row, core], (to_row, col)
        )

    def o_forward(of_row):
        return rdma(
            o_dst(of_row, core), o_dst(of_row, core), o_fwd.at[of_row], o_recv.at[of_row, core],
            me.at(core=1 - core),
        )

    def o_arrived(of_row, of_core):
        arrived(o_dst(of_row, of_core), o_recv.at[of_row, of_core], o_send.at[0], me.here)

    own_o = pltpu.make_async_copy(
        ow_hbm.at[:, pl.ds(pl.multiple_of(row * out_width, 128), out_width)],
        ocol_ref.at[pl.ds(pl.multiple_of(row * own_rows, 16), own_rows), :],
        local_sem.at[2],
    )
    own_o.start()

    def part(chip):
        return jnp.concatenate(
            [
                hid_ref[:, r * width_row + c * fine:r * width_row + (c + 1) * fine]
                for c in (2 * chip, 2 * chip + 1)
                for r in range(n_row)
            ],
            axis=1,
        )

    for chip in range(n_col // 2):
        hid_parts[chip] = part(chip)

    for j in range(3):
        proj_ref[j] = jnp.zeros_like(proj_ref[j])

    def project(dz, dx):
        weights.sibling(dz, dx)
        chip = weights.block(dz, dx)
        for j in range(3):
            proj_ref[j] += jnp.dot(hid_parts[chip], w_all[chip, j], preferred_element_type=f32)

    weights.z_turn()
    each(n_row - 1, lambda i: o_copy(i).start())
    weights.x_turn(0)
    gate.second()
    weights.x_turn(1)
    project(0, 0)
    project(1, 0)
    project(0, -1)
    project(0, 1)
    weights.x_end(0)
    gate.third()
    project(1, -1)
    project(1, 1)
    weights.x_end(1)
    project(0, 2)
    project(1, 2)

    def o_relay(i):
        of_row = lax.rem(row + n_row - 1 - i, n_row)
        o_arrived(of_row, core)
        o_forward(of_row).start()

    each(n_row - 1, o_relay)
    gate.last()

    def g_join(r):
        for j in range(2):
            gblk_ref[j, r] = join(g3, r, j).astype(bf16)

    for r in range(n_row):
        g_join(r)
    each(n_row - 1, lambda i: o_arrived(lax.rem(row + 1 + i, n_row), 1 - core))
    own_o.wait()
    qkv.drain()
    gate.drain()
    weights.drain()
    each(n_row - 1, lambda i: o_copy(i).wait_send())
    each(n_row - 1, lambda i: o_forward(lax.rem(row + 1 + i, n_row)).wait_send())


def sync_weights(qkv_train, gate_up_train, hidden, o_weight, n_row, n_col):
    tok, width_model = hidden.shape
    row_width, part = qkv_train.shape[1:]
    gate_part = gate_up_train.shape[2]
    width = 2 * part
    fine = row_width // n_col
    bf16, f32 = jnp.bfloat16, jnp.float32
    dma = pltpu.SemaphoreType.DMA
    vmem, anywhere = pl.BlockSpec(memory_space=pltpu.VMEM), pl.BlockSpec(memory_space=pl.ANY)
    def pieces(*shape):
        return [
            pltpu.VMEM((2, n_col // 2) + shape, bf16),
            pltpu.VMEM((2, 2, 2, 2) + shape, bf16),
            pltpu.VMEM((2, 2, 2, 2) + shape, bf16),
            pltpu.VMEM((4, 2, 2) + shape, bf16),
        ]

    return pl.pallas_call(
        functools.partial(sync_body, n_row=n_row, n_col=n_col),
        out_shape=(
            jax.ShapeDtypeStruct((3, tok, width), f32),
            jax.ShapeDtypeStruct((3, n_row, fine, width), bf16),
            jax.ShapeDtypeStruct((2, n_row, fine, 2 * gate_part), bf16),
            jax.ShapeDtypeStruct((n_row * o_weight.shape[0], width_model // n_row), bf16),
        ),
        in_specs=[vmem, anywhere, vmem, anywhere],
        out_specs=(vmem, vmem, vmem, anywhere),
        scratch_shapes=[
            pltpu.VMEM((n_col // 2, tok, 2 * n_row * fine), bf16),
            *pieces(3, fine, part),
            pltpu.VMEM((n_col // 2, 3, 2 * n_row * fine, width), bf16),
            pltpu.VMEM((2, gate_part, row_width), f32),
            *pieces(2, fine, gate_part),
            dma((3, 8)),
            dma((3, 8)),
            dma((3, 8)),
            dma((3, 8)),
            dma((n_col // 2, 2, 4)),
            dma((n_col // 2, 2, 2)),
            dma((n_row,)),
            dma((n_row,)),
            dma((n_row, 2)),
            dma((3,)),
        ],
        compiler_params=pltpu.CompilerParams(
            collective_id=1, has_side_effects=True, vmem_limit_bytes=60 << 20
        ),
        cost_estimate=pl.CostEstimate(
            flops=2 * 3 * tok * width_model * width, bytes_accessed=30_000_000, transcendentals=0
        ),
        name="sync_weights",
    )(qkv_train.swapaxes(1, 2), gate_up_train.swapaxes(1, 2), hidden, o_weight)


def column_of(sums, at_row):
    pick = (lax.broadcasted_iota(jnp.int32, (8, 128), 0) == at_row).astype(jnp.float32)
    return lax.dot_general(
        sums, pick, (((0,), (0,)), ((), ())),
        precision=lax.Precision.HIGHEST, preferred_element_type=jnp.float32,
    )


def lane_sums(values):
    return lax.dot_general(
        jnp.ones((8, values.shape[1]), jnp.float32), values * values, (((1,), (1,)), ((), ())),
        precision=lax.Precision.HIGHEST, preferred_element_type=jnp.float32,
    )


def layer_body(
    lengths_ref, proj_ref, cos_ref, sin_ref, gain_ref, ocol_ref, post_ref, hid_hbm,
    out_ref, kv_out,
    query, kv, mixed_all, residual, sq_in, sq_out,
    kv_send, kv_recv, a_send, a_recv, s_send, s_recv, t_send, t_recv, local_sem,
    *, n_row, n_col,
):
    me = Place()
    row, col = me.row, me.col
    bf16, f32 = jnp.bfloat16, jnp.float32
    tok, width = query.shape
    heads = width // HD
    out_width = out_ref.shape[1]
    keep = pltpu.make_async_copy(
        hid_hbm.at[:, pl.ds(pl.multiple_of(row * out_width, 128), out_width)], residual, local_sem.at[0]
    )
    keep.start()

    barrier = pltpu.get_barrier_semaphore()
    signal(barrier, me.at(x=wrap(me.x + 1, 4)))
    signal(barrier, me.at(x=wrap(me.x - 1, 4)))
    signal(barrier, me.at(zh=1 - me.zh))
    signal(barrier, me.at(core=1 - me.core))
    for i in range(1, n_row):
        signal(barrier, (lax.rem(row + i, n_row), col))

    own = pl.ds(pl.multiple_of(col * tok, 64), tok)
    kv[1, own, :] = proj_ref[2].astype(bf16)
    top = lax.broadcasted_iota(jnp.int32, (8, tok), 0) < 4
    sq_in[row] = jnp.where(top, lane_sums(proj_ref[0]), lane_sums(proj_ref[1]))
    pl.semaphore_wait(barrier, 4 + n_row - 1)

    def share(buffer, send, recv, i):
        return rdma(
            buffer.at[row], buffer.at[row], send.at[i], recv.at[row],
            (lax.rem(row + 1 + i, n_row), col),
        )

    def shared(buffer, send, recv):
        def wait(i):
            src = lax.rem(row + 1 + i, n_row)
            arrived(buffer.at[src], recv.at[src], send.at[0], me.here)

        each(n_row - 1, wait)
        total = buffer[0]
        for src in range(1, n_row):
            total = total + buffer[src]
        return total

    each(n_row - 1, lambda i: share(sq_in, s_send, s_recv, i).start())

    def tokens_of(block, core, half):
        rows = pl.ds(pl.multiple_of((2 * block + core) * tok, 64), tok)
        return kv.at[1 - half, rows, :]

    gathers = [Gather(me, True, tokens_of, kv_send, kv_recv) for _ in range(2)]
    first_sends = Gather(me, True, tokens_of, kv_send, kv_recv)
    first_sends.start(0)

    squares = shared(sq_in, s_send, s_recv)
    cosine, sine = cos_ref[...], sin_ref[...]
    for which in (1, 0):
        scale = lax.rsqrt(column_of(squares, 4 * which) / (n_row * width) + norm_epsilon)
        for head in range(heads):
            lanes = slice(head * HD, (head + 1) * HD)
            x = proj_ref[which, :, lanes] * scale * gain_ref[which:which + 1, lanes]
            turned = (x * cosine + pltpu.roll(x, HD // 2, 1) * sine).astype(bf16)
            if which == 1:
                kv[0, own, lanes] = turned
            else:
                query[:, lanes] = turned
        if which == 1:
            first_sends.start(1)

    def kv_gather(z_first):
        g = gathers[0 if z_first else 1]
        if z_first:
            g.z_turn()
            g.x_turn(0)
            g.x_turn(1)
            g.x_end(0)
            g.x_end(1)
        else:
            g.x_turn(0, 2)
            g.x_end(0, 2)
            g.z_end()

    by_core(me, kv_gather)
    for dz in range(2):
        for dx in range(4):
            if (dz, dx) != (0, 0):
                gathers[0].sibling(dz, dx)
    gathers[0].sibling(0, 0)

    give = pltpu.make_async_copy(kv, kv_out, local_sem.at[1])
    give.start()

    reach = -(-(LMAX - 1) // tok)
    span = min(reach + 1, n_col) * tok
    first_key = pl.multiple_of(jnp.maximum(col - reach, 0) * tok, 64)
    query_index = col * tok + lax.broadcasted_iota(jnp.int32, (tok, 1), 0)
    key_index = first_key + lax.broadcasted_iota(jnp.int32, (1, span), 1)
    prompt_start = jnp.zeros((tok, 1), jnp.int32)
    end = 0
    for p in range(lengths_ref.shape[0]):
        end = end + lengths_ref[p]
        prompt_start = jnp.where(query_index >= end, end, prompt_start)
    allowed = (key_index <= query_index) & (key_index >= prompt_start)
    for head in range(heads):
        lanes = slice(head * HD, (head + 1) * HD)
        keys = kv[0, pl.ds(first_key, span), lanes]
        values = kv[1, pl.ds(first_key, span), lanes]
        scores = lax.dot_general(
            query[:, lanes], keys, (((1,), (1,)), ((), ())), preferred_element_type=f32
        ) * (1.0 / math.sqrt(HD))
        scores = jnp.where(allowed, scores, big_negative)
        exponent = jnp.exp(scores - jnp.max(scores, axis=1, keepdims=True))
        total = jnp.sum(exponent, axis=1, keepdims=True)
        mixed = jnp.dot(exponent.astype(bf16), values, preferred_element_type=f32)
        mixed_all[row, :, lanes] = (mixed / total).astype(bf16)

    half_tok = tok // 2
    row_gathers = [
        Gather(
            me, False,
            lambda block, core, half: mixed_all.at[block, pl.ds(half * half_tok, half_tok), :],
            a_send, a_recv,
        )
        for _ in range(2)
    ]

    def row_gather(z_first):
        g = row_gathers[0 if z_first else 1]
        g.start(0)
        g.start(1)
        if z_first:
            g.z_turn()
            g.x_turn(0)
            g.x_turn(1)
            g.x_end(0)
            g.x_end(1)
        else:
            g.x_turn(0, 2)
            g.x_end(0, 2)
            g.z_end()

    by_core(me, row_gather)

    product = jnp.zeros((tok, out_width), f32)
    for src in range(n_row):
        product += jnp.dot(
            mixed_all[src], ocol_ref[src * width:(src + 1) * width, :], preferred_element_type=f32
        )
    sq_out[row] = lane_sums(product)
    each(n_row - 1, lambda i: share(sq_out, t_send, t_recv, i).start())
    keep.wait()

    each(n_row - 1, lambda i: share(sq_in, s_send, s_recv, i).wait_send())
    first_sends.drain()

    def drain(z_first):
        which = 0 if z_first else 1
        gathers[which].drain()
        row_gathers[which].drain()

    by_core(me, drain)

    scale = lax.rsqrt(column_of(shared(sq_out, t_send, t_recv), 0) / (n_row * out_width) + norm_epsilon)
    for at in range(0, out_width, 128):
        lanes = slice(at, at + 128)
        out_ref[:, lanes] = (
            residual[:, lanes].astype(f32) + product[:, lanes] * scale * post_ref[at // 128:at // 128 + 1, :]
        ).astype(bf16)
    each(n_row - 1, lambda i: share(sq_out, t_send, t_recv, i).wait_send())
    give.wait()


def attention_layer(lengths, projected, cosine, sine, gain, o_columns, post, hidden, n_row, n_col):
    _, tok, width = projected.shape
    out_width = o_columns.shape[1]
    bf16, f32 = jnp.bfloat16, jnp.float32
    dma = pltpu.SemaphoreType.DMA
    vmem, anywhere = pl.BlockSpec(memory_space=pltpu.VMEM), pl.BlockSpec(memory_space=pl.ANY)
    return pl.pallas_call(
        functools.partial(layer_body, n_row=n_row, n_col=n_col),
        out_shape=(
            jax.ShapeDtypeStruct((tok, out_width), bf16),
            jax.ShapeDtypeStruct((2, n_col * tok, width), bf16),
        ),
        in_specs=[pl.BlockSpec(memory_space=pltpu.SMEM)] + [vmem] * 6 + [anywhere],
        out_specs=(vmem, anywhere),
        scratch_shapes=[
            pltpu.VMEM((tok, width), bf16),
            pltpu.VMEM((2, n_col * tok, width), bf16),
            pltpu.VMEM((n_row, tok, width), bf16),
            pltpu.VMEM((tok, out_width), bf16),
            pltpu.VMEM((n_row, 8, tok), f32),
            pltpu.VMEM((n_row, 8, tok), f32),
            dma((n_col // 2, 2, 4)),
            dma((n_col // 2, 2, 2)),
            dma((n_row, 2, 4)),
            dma((n_row, 2, 2)),
            dma((n_row,)),
            dma((n_row,)),
            dma((n_row,)),
            dma((n_row,)),
            dma((2,)),
        ],
        compiler_params=pltpu.CompilerParams(
            collective_id=2, has_side_effects=True, vmem_limit_bytes=60 << 20
        ),
        cost_estimate=pl.CostEstimate(
            flops=8_000_000_000, bytes_accessed=20_000_000, transcendentals=3_000_000
        ),
        name="attention_layer",
    )(lengths, projected, cosine, sine, gain, o_columns, post, hidden)


def cache_body(lengths_ref, owner_ref, table_ref, kv_hbm, out_ref, windows, sems):
    tokens = kv_hbm.shape[1]
    col = lax.axis_index("col")
    begin = length = mine = end = 0
    for p in range(lengths_ref.shape[0]):
        here = owner_ref[p] == col
        begin, length = jnp.where(here, end, begin), jnp.where(here, lengths_ref[p], length)
        mine = jnp.where(here, p, mine)
        end = end + lengths_ref[p]

    def locate(page):
        first = jnp.minimum(begin + page * PAGE, tokens - 1)
        base = pl.multiple_of(jnp.minimum((first // ALIGN) * ALIGN, tokens - WINDOW), ALIGN)
        return first, base

    def fetch(page):
        _, base = locate(page)
        return pltpu.make_async_copy(
            kv_hbm.at[:, pl.ds(base, WINDOW), :], windows.at[page], sems.at[page]
        )

    each(PAGES, lambda page: fetch(page).start())

    def place(page):
        fetch(page).wait()
        first, base = locate(page)
        row = lax.broadcasted_iota(jnp.int32, (PAGE, WINDOW), 0)
        source = lax.broadcasted_iota(jnp.int32, (PAGE, WINDOW), 1)
        pick = (row + (first - base) == source) & (row + page * PAGE < length)
        pick = pick.astype(jnp.float32).astype(jnp.bfloat16)
        slot = table_ref[mine, page]
        for part in range(2):
            moved = jnp.dot(pick, windows[page, part], preferred_element_type=jnp.float32)
            out_ref[slot, part] = moved.astype(jnp.bfloat16)

    each(PAGES, place)


def build_cache(lengths, owner, page_table, kv):
    width = kv.shape[2]
    smem = pl.BlockSpec(memory_space=pltpu.SMEM)
    return pl.pallas_call(
        cache_body,
        out_shape=jax.ShapeDtypeStruct((PAGES, 2, PAGE, width), jnp.bfloat16),
        in_specs=[smem, smem, smem, pl.BlockSpec(memory_space=pl.ANY)],
        out_specs=pl.BlockSpec(memory_space=pltpu.VMEM),
        scratch_shapes=[
            pltpu.VMEM((PAGES, 2, WINDOW, width), jnp.bfloat16),
            pltpu.SemaphoreType.DMA((PAGES,)),
        ],
        compiler_params=pltpu.CompilerParams(vmem_limit_bytes=60 << 20),
        cost_estimate=pl.CostEstimate(flops=10_000_000, bytes_accessed=7_000_000, transcendentals=0),
        name="cache_pages",
    )(lengths, owner, page_table, kv)


def local(
    hidden, lengths, owner, page_table, qkv_train, qk_gain, o_weight, post_gain, gate_up_train
):
    n_row = lax.axis_size("row")
    n_col = lax.axis_size("col")
    col_index = lax.axis_index("col")
    tok_rows = hidden.shape[0]
    projected, weight_blocks, gate_up_blocks, o_columns = sync_weights(
        qkv_train, gate_up_train, hidden, o_weight, n_row, n_col
    )
    token_index = col_index * tok_rows + jnp.arange(tok_rows, dtype=jnp.int32)
    token_start = jnp.zeros_like(token_index)
    end = 0
    for p in range(lengths.shape[0]):
        end = end + lengths[p]
        token_start = jnp.where(token_index >= end, end, token_start)
    half_dim = HD // 2
    frequency = rope_theta ** (-2.0 * jnp.arange(half_dim, dtype=jnp.float32) / HD)
    angles = (token_index - token_start).astype(jnp.float32)[:, None] * frequency[None, :]
    cosine, sine = jnp.cos(angles), jnp.sin(angles)
    cosine = jnp.concatenate([cosine, cosine], axis=1)
    sine = jnp.concatenate([-sine, sine], axis=1)

    layer_out, kv = attention_layer(
        lengths, projected, cosine, sine, qk_gain, o_columns,
        post_gain.reshape(-1, 128), hidden, n_row, n_col,
    )
    cache_pages = build_cache(lengths, owner, page_table, kv)
    return (layer_out, cache_pages[None], weight_blocks, gate_up_blocks)


def solution(mesh):
    in_specs = (
        P("col", None),
        P(),
        P(),
        P(),
        P(None, "row", "col"),
        P(None, "row"),
        P("row", None),
        P("row"),
        P(None, "row", "col"),
    )
    out_specs = (
        P("col", "row"),
        P("col", None, None, None, "row"),
        P(None, None, "col", "row"),
        P(None, None, "col", "row"),
    )
    return jax.shard_map(local, mesh=mesh, in_specs=in_specs, out_specs=out_specs, check_vma=False)
```

```python
import functools
import math

import jax
import jax.numpy as jnp
from jax import lax
from jax.experimental import pallas as pl
from jax.experimental.pallas import tpu as pltpu
from jax.sharding import PartitionSpec as P

HD = 128
HEADS = 24
PAGE = 128
PAGES = 16
LMAX = 2048

norm_epsilon = 1e-06
rope_theta = 500000.0
big_negative = -1e30


ALIGN = 16
WINDOW = PAGE + ALIGN


def rdma(src, dst, send_sem, recv_sem, device):
    return pltpu.make_async_remote_copy(
        src_ref=src,
        dst_ref=dst,
        send_sem=send_sem,
        recv_sem=recv_sem,
        device_id=device,
        device_id_type=pl.DeviceIdType.MESH,
    )


def arrived(ref, recv_sem, send_sem, here):
    rdma(ref, ref, send_sem, recv_sem, here).wait_recv()


def each(count, body):
    lax.fori_loop(0, count, lambda i, carry: (body(i), carry)[1], 0)


def wrap(value, size):
    return lax.rem(value + size, size)


class Place:
    def __init__(self):
        self.row, self.col = lax.axis_index("row"), lax.axis_index("col")
        self.y, self.zl = self.row // 2, lax.rem(self.row, 2)
        self.zh, self.x, self.core = self.col // 8, lax.rem(self.col // 2, 4), lax.rem(self.col, 2)
        self.chip = self.col // 2
        self.here = (self.row, self.col)

    def at(self, y=None, zl=None, zh=None, x=None, core=None):
        y, zl = (self.y if y is None else y), (self.zl if zl is None else zl)
        zh, x = (self.zh if zh is None else zh), (self.x if x is None else x)
        core = self.core if core is None else core
        return (2 * y + zl, 8 * zh + 2 * x + core)


def signal(sem, device):
    pl.semaphore_signal(sem, inc=1, device_id=device, device_id_type=pl.DeviceIdType.MESH)


def near_first(step):
    return step + (step // 2) * (1 - 2 * lax.rem(step, 2))


class Relay:
    def __init__(self, me, src, stages, send, recv):
        self.me, self.src, self.stages, self.send, self.recv = me, src, stages, send, recv

    def go(self, away, stage, number, slot, src, device):
        dst = self.stages[stage].at[slot]

        @pl.when(away)
        def _():
            rdma(src, dst, self.send.at[stage, number], self.recv.at[stage, slot], device).start()

        @pl.when(jnp.logical_not(away))
        def _():
            dst[...] = src[...]

    def got(self, away, stage, slot):
        @pl.when(away)
        def _():
            arrived(
                self.stages[stage].at[slot], self.recv.at[stage, slot], self.send.at[stage, 0],
                self.me.here,
            )

    def first(self):
        me = self.me

        def send(i):
            dx, dk, zh = 3 - i // 4, lax.rem(i // 2, 2), lax.rem(i, 2)
            x, core = lax.rem(me.x + near_first(dx), 4), lax.rem(me.core + dk, 2)
            slot = (me.x * 2 + me.core) * 2 + zh
            away = jnp.logical_or(dx > 0, dk > 0)
            self.go(away, 0, i, slot, self.src.at[zh * 8 + 2 * x + core], me.at(x=x, core=core))

        each(16, send)

    def second(self):
        me = self.me

        def send(i):
            ks, zh = lax.rem(i // 2, 2), lax.rem(i, 2)
            xs = wrap(me.x - near_first(i // 4), 4)
            came = (xs * 2 + ks) * 2 + zh
            self.got(jnp.logical_or(i >= 4, ks != me.core), 0, came)
            zl = lax.rem(xs, 2)
            away = jnp.logical_or(zl != me.zl, zh != me.zh)
            slot = ((me.zh * 2 + me.zl) * 2 + xs // 2) * 2 + ks
            self.go(away, 1, came, slot, self.stages[0].at[came], me.at(zl=zl, zh=zh))

        each(16, send)

    def third(self, wait=True):
        me = self.me

        def send(i):
            zs = lax.rem(me.zh * 2 + me.zl + near_first(i // 4), 4)
            xh, ks = lax.rem(i // 2, 2), lax.rem(i, 2)
            came = (zs * 2 + xh) * 2 + ks
            if wait:
                self.got(i >= 4, 1, came)
            y = (zs // 2) * 2 + xh
            slot = (me.y * 2 + lax.rem(zs, 2)) * 2 + ks
            self.go(y != me.y, 2, came, slot, self.stages[1].at[came], me.at(y=y))

        each(16, send)

    def second_last(self):
        me = self.me
        each(16, lambda i: self.got(i // 4 != me.zh * 2 + me.zl, 1, i))

    def last(self):
        each(16, lambda i: self.got(i // 4 != self.me.y, 2, i))

    def drain(self, stages=(0, 1, 2)):
        me = self.me

        def sent(away, stage, number):
            if stage not in stages:
                return

            @pl.when(away)
            def _():
                rdma(
                    self.src.at[0], self.src.at[0], self.send.at[stage, number],
                    self.recv.at[stage, 0], me.here,
                ).wait_send()

        def each_piece(i):
            sent(jnp.logical_or(i < 12, lax.rem(i // 2, 2) > 0), 0, i)
            xs, zh = i // 4, lax.rem(i, 2)
            sent(jnp.logical_or(lax.rem(xs, 2) != me.zl, zh != me.zh), 1, i)
            zs, xh = i // 4, lax.rem(i // 2, 2)
            sent((zs // 2) * 2 + xh != me.y, 2, i)

        each(16, each_piece)


def join(stage, r, j, rows, columns):
    halves = [
        stage[2 * r + half, j * rows:(j + 1) * rows, :columns].astype(jnp.float32)
        for half in range(2)
    ]
    return jnp.concatenate(halves, axis=1)


class Gather:
    def __init__(self, me, over_col, view, send, recv):
        self.me, self.over_col, self.view, self.send, self.recv = me, over_col, view, send, recv
        self.hand = (3,) if over_col else ()
        self.sent = []

    def block(self, dz, dr):
        me = self.me
        if self.over_col:
            return wrap(me.zh + dz, 2) * 4 + wrap(me.x + dr, 4)
        return wrap(me.y + dr, 4) * 2 + wrap(me.zl + dz, 2)

    def copy(self, dz, dr, half, kind):
        me = self.me
        if kind == 3:
            device = me.at(core=1 - me.core)
        elif kind == 2:
            device = me.at(zh=1 - me.zh) if self.over_col else me.at(zl=1 - me.zl)
        else:
            turn = 1 - 2 * kind
            device = (
                me.at(x=wrap(me.x + turn, 4)) if self.over_col else me.at(y=wrap(me.y + turn, 4))
            )
        block = self.block(dz, dr)
        ref = self.view(block, me.core, half)
        return rdma(
            ref, ref, self.send.at[block, half, kind], self.recv.at[block, me.core, half], device
        )

    def go(self, dz, dr, half, *kinds):
        for kind in kinds + self.hand:
            self.copy(dz, dr, half, kind).start()
            self.sent.append((dz, dr, half, kind))

    def got(self, dz, dr, half, sibling=False):
        block = self.block(dz, dr)
        core = 1 - self.me.core if sibling else self.me.core
        arrived(
            self.view(block, core, half), self.recv.at[block, core, half], self.send.at[0, 0, 0],
            self.me.here,
        )

    def start(self, half):
        self.go(0, 0, half, 2, 0, 1)

    def z_turn(self):
        for half in range(2):
            self.got(1, 0, half)
            self.go(1, 0, half, 0, 1)

    def x_turn(self, dz, *more):
        self.got(dz, -1, 0)
        self.go(dz, -1, 0, 0, *more)
        self.got(dz, 1, 0)
        self.go(dz, 1, 0, *more)
        self.got(dz, 1, 1)
        self.go(dz, 1, 1, 1, *more)
        self.got(dz, -1, 1)
        self.go(dz, -1, 1, *more)

    def x_end(self, dz, *more):
        for half in range(2):
            self.got(dz, 2, half)
            self.go(dz, 2, half, *more)

    def z_end(self):
        for half in range(2):
            for dr in (0, -1, 1, 2):
                self.got(1, dr, half)
                self.go(1, dr, half)

    def sibling(self, dz, dr):
        for half in range(2):
            self.got(dz, dr, half, sibling=True)

    def drain(self):
        for which in self.sent:
            self.copy(*which).wait_send()
        self.sent = []


def by_core(me, run):
    @pl.when(me.core == 0)
    def _():
        run(True)

    @pl.when(me.core == 1)
    def _():
        run(False)


def sync_body(
    qkv_ref, gate_hbm, hid_ref, ow_hbm,
    proj_ref, qblk_ref, g2, ocol_ref,
    hid_parts, qsrc, q1, q2, q3, w_all, gf32, gsrc, g1,
    q_send, q_recv, g_send, g_recv, w_send, w_recv, o_send, o_fwd, o_recv, local_sem,
    *, n_row, n_col,
):
    me = Place()
    row, col, core = me.row, me.col, me.core
    width_row = qkv_ref.shape[2]
    fine = width_row // n_col
    bf16, f32 = jnp.bfloat16, jnp.float32

    def fetch(j):
        return pltpu.make_async_copy(gate_hbm.at[j], gf32.at[j], local_sem.at[j])

    for j in range(2):
        fetch(j).start()

    def cut(part, pieces, j):
        turned = part.T
        if pieces.shape[2] > part.shape[0]:
            fill = jnp.zeros((part.shape[1], pieces.shape[2] - part.shape[0]), f32)
            turned = jnp.concatenate([turned, fill], axis=1)
        for c in range(n_col):
            rows = turned[c * fine:(c + 1) * fine, :].astype(bf16)
            pieces[c, j * fine:(j + 1) * fine, :] = rows

    barrier = pltpu.get_barrier_semaphore()
    for i in range(1, 8):
        signal(barrier, me.at(x=lax.rem(me.x + i // 2, 4), core=lax.rem(me.core + i, 2)))
    for i in range(1, 4):
        signal(barrier, me.at(zh=lax.rem(me.zh + i // 2, 2), zl=lax.rem(me.zl + i, 2)))
    for i in range(1, n_row):
        signal(barrier, (lax.rem(row + i, n_row), col))

    for j in range(3):
        cut(qkv_ref[j], qsrc, j)
    pl.semaphore_wait(barrier, 7 + 3 + n_row - 1)

    qkv = Relay(me, qsrc, (q1, q2, q3), q_send, q_recv)
    gate = Relay(me, gsrc, (g1, g2), g_send, g_recv)
    qkv.first()
    for j in range(2):
        fetch(j).wait()
        cut(gf32[j], gsrc, j)
    qkv.second()
    gate.first()
    qkv.third()
    qkv.last()

    depth = w_all.shape[2] // 4

    for j in range(3):
        for pair in range(n_row // 2):
            first, second = (join(q3, 2 * pair + i, j, fine, qkv_ref.shape[1]) for i in range(2))
            qblk_ref[j, 2 * pair] = first.astype(bf16)
            qblk_ref[j, 2 * pair + 1] = second.astype(bf16)
            both = jnp.concatenate([first, second], axis=0).astype(bf16)
            at = pl.multiple_of(core * depth * 2 + pair * 2 * fine, 16)
            w_all[me.chip, j, pl.ds(at, 2 * fine), :] = both


    def weight_rows(chip, of_core, half):
        at = pl.multiple_of((of_core * 2 + half) * depth, 16)
        return w_all.at[chip, :, pl.ds(at, depth), :]

    weights = Gather(me, True, weight_rows, w_send, w_recv)
    weights.start(0)
    weights.start(1)

    own_rows = ow_hbm.shape[0]
    half_o = own_rows // 2
    out_width = ocol_ref.shape[1]

    def o_src(to_row):
        return ow_hbm.at[
            pl.ds(pl.multiple_of(core * half_o, 16), half_o),
            pl.ds(pl.multiple_of(to_row * out_width, 128), out_width),
        ]

    def o_dst(of_row, of_core):
        return ocol_ref.at[
            pl.ds(pl.multiple_of(of_row * own_rows + of_core * half_o, 16), half_o), :
        ]

    def o_copy(i):
        to_row = lax.rem(row + 1 + i, n_row)
        return rdma(
            o_src(to_row), o_dst(row, core), o_send.at[i], o_recv.at[row, core], (to_row, col)
        )

    def o_forward(of_row):
        return rdma(
            o_dst(of_row, core), o_dst(of_row, core), o_fwd.at[of_row], o_recv.at[of_row, core],
            me.at(core=1 - core),
        )

    def o_arrived(of_row, of_core):
        arrived(o_dst(of_row, of_core), o_recv.at[of_row, of_core], o_send.at[0], me.here)

    own_o = pltpu.make_async_copy(
        ow_hbm.at[:, pl.ds(pl.multiple_of(row * out_width, 128), out_width)],
        ocol_ref.at[pl.ds(pl.multiple_of(row * own_rows, 16), own_rows), :],
        local_sem.at[2],
    )
    own_o.start()

    def part(chip):
        return jnp.concatenate(
            [
                hid_ref[:, r * width_row + c * fine:r * width_row + (c + 1) * fine]
                for c in (2 * chip, 2 * chip + 1)
                for r in range(n_row)
            ],
            axis=1,
        )

    for chip in range(n_col // 2):
        hid_parts[chip] = part(chip)

    for j in range(3):
        proj_ref[j] = jnp.zeros_like(proj_ref[j])

    def project(dz, dx):
        weights.sibling(dz, dx)
        chip = weights.block(dz, dx)
        for j in range(3):
            proj_ref[j] += jnp.dot(hid_parts[chip], w_all[chip, j], preferred_element_type=f32)

    gate.second()
    weights.z_turn()
    each(n_row - 1, lambda i: o_copy(i).start())
    weights.x_turn(0)
    project(0, 0)
    weights.x_turn(1)
    project(1, 0)
    weights.x_end(0)
    project(0, -1)
    project(0, 1)
    weights.x_end(1)
    project(1, -1)
    project(1, 1)
    project(0, 2)
    project(1, 2)

    def o_relay(i):
        of_row = lax.rem(row + n_row - 1 - i, n_row)
        o_arrived(of_row, core)
        o_forward(of_row).start()

    each(n_row - 1, o_relay)
    gate.second_last()
    each(n_row - 1, lambda i: o_arrived(lax.rem(row + 1 + i, n_row), 1 - core))
    own_o.wait()
    qkv.drain()
    gate.drain((0, 1))
    weights.drain()
    each(n_row - 1, lambda i: o_copy(i).wait_send())
    each(n_row - 1, lambda i: o_forward(lax.rem(row + 1 + i, n_row)).wait_send())


def sync_weights(qkv_train, gate_up_train, hidden, o_weight, n_row, n_col):
    tok, width_model = hidden.shape
    row_width, part = qkv_train.shape[1:]
    gate_part = gate_up_train.shape[2]
    width = 2 * part
    fine = row_width // n_col
    bf16, f32 = jnp.bfloat16, jnp.float32
    dma = pltpu.SemaphoreType.DMA
    vmem, anywhere = pl.BlockSpec(memory_space=pltpu.VMEM), pl.BlockSpec(memory_space=pl.ANY)
    gate_tiles = -(-gate_part // 128) * 128
    return pl.pallas_call(
        functools.partial(sync_body, n_row=n_row, n_col=n_col),
        out_shape=(
            jax.ShapeDtypeStruct((3, tok, width), f32),
            jax.ShapeDtypeStruct((3, n_row, fine, width), bf16),
            jax.ShapeDtypeStruct((n_col, 2 * fine, gate_tiles), bf16),
            jax.ShapeDtypeStruct((n_row * o_weight.shape[0], width_model // n_row), bf16),
        ),
        in_specs=[vmem, anywhere, vmem, anywhere],
        out_specs=(vmem, vmem, vmem, anywhere),
        scratch_shapes=[
            pltpu.VMEM((n_col // 2, tok, 2 * n_row * fine), bf16),
            *[pltpu.VMEM((n_col, 3 * fine, part), bf16)] * 4,
            pltpu.VMEM((n_col // 2, 3, 2 * n_row * fine, width), bf16),
            pltpu.VMEM((2, gate_part, row_width), f32),
            *[pltpu.VMEM((n_col, 2 * fine, gate_tiles), bf16)] * 2,
            dma((3, n_col)),
            dma((3, n_col)),
            dma((2, n_col)),
            dma((2, n_col)),
            dma((n_col // 2, 2, 4)),
            dma((n_col // 2, 2, 2)),
            dma((n_row,)),
            dma((n_row,)),
            dma((n_row, 2)),
            dma((3,)),
        ],
        compiler_params=pltpu.CompilerParams(
            collective_id=1, has_side_effects=True, vmem_limit_bytes=60 << 20
        ),
        cost_estimate=pl.CostEstimate(
            flops=2 * 3 * tok * width_model * width, bytes_accessed=30_000_000, transcendentals=0
        ),
        name="sync_weights",
    )(qkv_train.swapaxes(1, 2), gate_up_train.swapaxes(1, 2), hidden, o_weight)


def column_of(sums, at_row):
    pick = (lax.broadcasted_iota(jnp.int32, (8, 128), 0) == at_row).astype(jnp.float32)
    return lax.dot_general(
        sums, pick, (((0,), (0,)), ((), ())),
        precision=lax.Precision.HIGHEST, preferred_element_type=jnp.float32,
    )


def lane_sums(values):
    return lax.dot_general(
        jnp.ones((8, values.shape[1]), jnp.float32), values * values, (((1,), (1,)), ((), ())),
        precision=lax.Precision.HIGHEST, preferred_element_type=jnp.float32,
    )


def layer_body(
    lengths_ref, proj_ref, cos_ref, sin_ref, gain_ref, ocol_ref, post_ref, g2, hid_hbm,
    out_ref, kv_out, gblk_ref,
    query, kv, mixed_all, residual, sq_in, sq_out, g3, g_send, g_recv,
    kv_send, kv_recv, a_send, a_recv, s_send, s_recv, t_send, t_recv, local_sem,
    *, n_row, n_col,
):
    me = Place()
    row, col = me.row, me.col
    bf16, f32 = jnp.bfloat16, jnp.float32
    tok, width = query.shape
    heads = width // HD
    out_width = out_ref.shape[1]
    keep = pltpu.make_async_copy(
        hid_hbm.at[:, pl.ds(pl.multiple_of(row * out_width, 128), out_width)], residual, local_sem.at[0]
    )
    keep.start()

    barrier = pltpu.get_barrier_semaphore()
    signal(barrier, me.at(x=wrap(me.x + 1, 4)))
    signal(barrier, me.at(x=wrap(me.x - 1, 4)))
    signal(barrier, me.at(zh=1 - me.zh))
    signal(barrier, me.at(core=1 - me.core))
    for i in range(1, n_row):
        signal(barrier, (lax.rem(row + i, n_row), col))

    own = pl.ds(pl.multiple_of(col * tok, 64), tok)
    kv[1, own, :] = proj_ref[2].astype(bf16)
    top = lax.broadcasted_iota(jnp.int32, (8, tok), 0) < 4
    sq_in[row] = jnp.where(top, lane_sums(proj_ref[0]), lane_sums(proj_ref[1]))
    pl.semaphore_wait(barrier, 4 + n_row - 1)

    def share(buffer, send, recv, i):
        return rdma(
            buffer.at[row], buffer.at[row], send.at[i], recv.at[row],
            (lax.rem(row + 1 + i, n_row), col),
        )

    def shared(buffer, send, recv):
        def wait(i):
            src = lax.rem(row + 1 + i, n_row)
            arrived(buffer.at[src], recv.at[src], send.at[0], me.here)

        each(n_row - 1, wait)
        total = buffer[0]
        for src in range(1, n_row):
            total = total + buffer[src]
        return total

    each(n_row - 1, lambda i: share(sq_in, s_send, s_recv, i).start())

    def tokens_of(block, core, half):
        rows = pl.ds(pl.multiple_of((2 * block + core) * tok, 64), tok)
        return kv.at[1 - half, rows, :]

    gathers = [Gather(me, True, tokens_of, kv_send, kv_recv) for _ in range(2)]
    first_sends = Gather(me, True, tokens_of, kv_send, kv_recv)
    first_sends.start(0)

    gate = Relay(me, g2, (g2, g2, g3), g_send, g_recv)
    gate.third(wait=False)

    squares = shared(sq_in, s_send, s_recv)
    cosine, sine = cos_ref[...], sin_ref[...]
    for which in (1, 0):
        scale = lax.rsqrt(column_of(squares, 4 * which) / (n_row * width) + norm_epsilon)
        for head in range(heads):
            lanes = slice(head * HD, (head + 1) * HD)
            x = proj_ref[which, :, lanes] * scale * gain_ref[which:which + 1, lanes]
            turned = (x * cosine + pltpu.roll(x, HD // 2, 1) * sine).astype(bf16)
            if which == 1:
                kv[0, own, lanes] = turned
            else:
                query[:, lanes] = turned
        if which == 1:
            first_sends.start(1)

    def kv_gather(z_first):
        g = gathers[0 if z_first else 1]
        if z_first:
            g.z_turn()
            g.x_turn(0)
            g.x_turn(1)
            g.x_end(0)
            g.x_end(1)
        else:
            g.x_turn(0, 2)
            g.x_end(0, 2)
            g.z_end()

    by_core(me, kv_gather)
    for dz in range(2):
        for dx in range(4):
            if (dz, dx) != (0, 0):
                gathers[0].sibling(dz, dx)
    gathers[0].sibling(0, 0)

    give = pltpu.make_async_copy(kv, kv_out, local_sem.at[1])
    give.start()

    reach = -(-(LMAX - 1) // tok)
    span = min(reach + 1, n_col) * tok
    first_key = pl.multiple_of(jnp.maximum(col - reach, 0) * tok, 64)
    query_index = col * tok + lax.broadcasted_iota(jnp.int32, (tok, 1), 0)
    key_index = first_key + lax.broadcasted_iota(jnp.int32, (1, span), 1)
    prompt_start = jnp.zeros((tok, 1), jnp.int32)
    end = 0
    for p in range(lengths_ref.shape[0]):
        end = end + lengths_ref[p]
        prompt_start = jnp.where(query_index >= end, end, prompt_start)
    allowed = (key_index <= query_index) & (key_index >= prompt_start)
    for head in range(heads):
        lanes = slice(head * HD, (head + 1) * HD)
        keys = kv[0, pl.ds(first_key, span), lanes]
        values = kv[1, pl.ds(first_key, span), lanes]
        scores = lax.dot_general(
            query[:, lanes], keys, (((1,), (1,)), ((), ())), preferred_element_type=f32
        ) * (1.0 / math.sqrt(HD))
        scores = jnp.where(allowed, scores, big_negative)
        exponent = jnp.exp(scores - jnp.max(scores, axis=1, keepdims=True))
        total = jnp.sum(exponent, axis=1, keepdims=True)
        mixed = jnp.dot(exponent.astype(bf16), values, preferred_element_type=f32)
        mixed_all[row, :, lanes] = (mixed / total).astype(bf16)

    half_tok = tok // 2
    row_gathers = [
        Gather(
            me, False,
            lambda block, core, half: mixed_all.at[block, pl.ds(half * half_tok, half_tok), :],
            a_send, a_recv,
        )
        for _ in range(2)
    ]

    fine = gblk_ref.shape[2]

    def gate_join(r):
        for j in range(2):
            gblk_ref[j, r] = join(g3, r, j, fine, gblk_ref.shape[3] // 2).astype(bf16)

    def row_gather(z_first):
        g = row_gathers[0 if z_first else 1]
        g.start(0)
        g.start(1)
        gate.last()
        each(n_row, gate_join)
        if z_first:
            g.z_turn()
            g.x_turn(0)
            g.x_turn(1)
            g.x_end(0)
            g.x_end(1)
        else:
            g.x_turn(0, 2)
            g.x_end(0, 2)
            g.z_end()

    by_core(me, row_gather)

    product = jnp.zeros((tok, out_width), f32)
    for src in range(n_row):
        product += jnp.dot(
            mixed_all[src], ocol_ref[src * width:(src + 1) * width, :], preferred_element_type=f32
        )
    sq_out[row] = lane_sums(product)
    each(n_row - 1, lambda i: share(sq_out, t_send, t_recv, i).start())
    keep.wait()

    each(n_row - 1, lambda i: share(sq_in, s_send, s_recv, i).wait_send())
    first_sends.drain()

    def drain(z_first):
        which = 0 if z_first else 1
        gathers[which].drain()
        row_gathers[which].drain()

    by_core(me, drain)
    gate.drain((2,))

    scale = lax.rsqrt(column_of(shared(sq_out, t_send, t_recv), 0) / (n_row * out_width) + norm_epsilon)
    for at in range(0, out_width, 128):
        lanes = slice(at, at + 128)
        out_ref[:, lanes] = (
            residual[:, lanes].astype(f32) + product[:, lanes] * scale * post_ref[at // 128:at // 128 + 1, :]
        ).astype(bf16)
    each(n_row - 1, lambda i: share(sq_out, t_send, t_recv, i).wait_send())
    give.wait()


def attention_layer(lengths, projected, cosine, sine, gain, o_columns, post, gate_pieces, gate_shape, hidden, n_row, n_col):
    _, tok, width = projected.shape
    out_width = o_columns.shape[1]
    bf16, f32 = jnp.bfloat16, jnp.float32
    dma = pltpu.SemaphoreType.DMA
    vmem, anywhere = pl.BlockSpec(memory_space=pltpu.VMEM), pl.BlockSpec(memory_space=pl.ANY)
    return pl.pallas_call(
        functools.partial(layer_body, n_row=n_row, n_col=n_col),
        out_shape=(
            jax.ShapeDtypeStruct((tok, out_width), bf16),
            jax.ShapeDtypeStruct((2, n_col * tok, width), bf16),
            jax.ShapeDtypeStruct(gate_shape, bf16),
        ),
        in_specs=[pl.BlockSpec(memory_space=pltpu.SMEM)] + [vmem] * 7 + [anywhere],
        out_specs=(vmem, anywhere, vmem),
        scratch_shapes=[
            pltpu.VMEM((tok, width), bf16),
            pltpu.VMEM((2, n_col * tok, width), bf16),
            pltpu.VMEM((n_row, tok, width), bf16),
            pltpu.VMEM((tok, out_width), bf16),
            pltpu.VMEM((n_row, 8, tok), f32),
            pltpu.VMEM((n_row, 8, tok), f32),
            pltpu.VMEM(gate_pieces.shape, bf16),
            dma((3, n_col)),
            dma((3, n_col)),
            dma((n_col // 2, 2, 4)),
            dma((n_col // 2, 2, 2)),
            dma((n_row, 2, 4)),
            dma((n_row, 2, 2)),
            dma((n_row,)),
            dma((n_row,)),
            dma((n_row,)),
            dma((n_row,)),
            dma((2,)),
        ],
        compiler_params=pltpu.CompilerParams(
            collective_id=2, has_side_effects=True, vmem_limit_bytes=60 << 20
        ),
        cost_estimate=pl.CostEstimate(
            flops=8_000_000_000, bytes_accessed=20_000_000, transcendentals=3_000_000
        ),
        name="attention_layer",
    )(lengths, projected, cosine, sine, gain, o_columns, post, gate_pieces, hidden)


def cache_body(lengths_ref, owner_ref, table_ref, kv_hbm, out_ref, windows, sems):
    tokens = kv_hbm.shape[1]
    col = lax.axis_index("col")
    begin = length = mine = end = 0
    for p in range(lengths_ref.shape[0]):
        here = owner_ref[p] == col
        begin, length = jnp.where(here, end, begin), jnp.where(here, lengths_ref[p], length)
        mine = jnp.where(here, p, mine)
        end = end + lengths_ref[p]

    def locate(page):
        first = jnp.minimum(begin + page * PAGE, tokens - 1)
        base = pl.multiple_of(jnp.minimum((first // ALIGN) * ALIGN, tokens - WINDOW), ALIGN)
        return first, base

    def fetch(page):
        _, base = locate(page)
        return pltpu.make_async_copy(
            kv_hbm.at[:, pl.ds(base, WINDOW), :], windows.at[page], sems.at[page]
        )

    each(PAGES, lambda page: fetch(page).start())

    def place(page):
        fetch(page).wait()
        first, base = locate(page)
        row = lax.broadcasted_iota(jnp.int32, (PAGE, WINDOW), 0)
        source = lax.broadcasted_iota(jnp.int32, (PAGE, WINDOW), 1)
        pick = (row + (first - base) == source) & (row + page * PAGE < length)
        pick = pick.astype(jnp.float32).astype(jnp.bfloat16)
        slot = table_ref[mine, page]
        for part in range(2):
            moved = jnp.dot(pick, windows[page, part], preferred_element_type=jnp.float32)
            out_ref[slot, part] = moved.astype(jnp.bfloat16)

    each(PAGES, place)


def build_cache(lengths, owner, page_table, kv):
    width = kv.shape[2]
    smem = pl.BlockSpec(memory_space=pltpu.SMEM)
    return pl.pallas_call(
        cache_body,
        out_shape=jax.ShapeDtypeStruct((PAGES, 2, PAGE, width), jnp.bfloat16),
        in_specs=[smem, smem, smem, pl.BlockSpec(memory_space=pl.ANY)],
        out_specs=pl.BlockSpec(memory_space=pltpu.VMEM),
        scratch_shapes=[
            pltpu.VMEM((PAGES, 2, WINDOW, width), jnp.bfloat16),
            pltpu.SemaphoreType.DMA((PAGES,)),
        ],
        compiler_params=pltpu.CompilerParams(vmem_limit_bytes=60 << 20),
        cost_estimate=pl.CostEstimate(flops=10_000_000, bytes_accessed=7_000_000, transcendentals=0),
        name="cache_pages",
    )(lengths, owner, page_table, kv)


def local(
    hidden, lengths, owner, page_table, qkv_train, qk_gain, o_weight, post_gain, gate_up_train
):
    n_row = lax.axis_size("row")
    n_col = lax.axis_size("col")
    col_index = lax.axis_index("col")
    tok_rows = hidden.shape[0]
    projected, weight_blocks, gate_pieces, o_columns = sync_weights(
        qkv_train, gate_up_train, hidden, o_weight, n_row, n_col
    )
    token_index = col_index * tok_rows + jnp.arange(tok_rows, dtype=jnp.int32)
    token_start = jnp.zeros_like(token_index)
    end = 0
    for p in range(lengths.shape[0]):
        end = end + lengths[p]
        token_start = jnp.where(token_index >= end, end, token_start)
    half_dim = HD // 2
    frequency = rope_theta ** (-2.0 * jnp.arange(half_dim, dtype=jnp.float32) / HD)
    angles = (token_index - token_start).astype(jnp.float32)[:, None] * frequency[None, :]
    cosine, sine = jnp.cos(angles), jnp.sin(angles)
    cosine = jnp.concatenate([cosine, cosine], axis=1)
    sine = jnp.concatenate([-sine, sine], axis=1)

    _, row_width, gate_part = gate_up_train.shape
    gate_shape = (2, n_row, row_width // n_col, 2 * gate_part)
    layer_out, kv, gate_up_blocks = attention_layer(
        lengths, projected, cosine, sine, qk_gain, o_columns,
        post_gain.reshape(-1, 128), gate_pieces, gate_shape, hidden, n_row, n_col,
    )
    cache_pages = build_cache(lengths, owner, page_table, kv)
    return (layer_out, cache_pages[None], weight_blocks, gate_up_blocks)


def solution(mesh):
    in_specs = (
        P("col", None),
        P(),
        P(),
        P(),
        P(None, "row", "col"),
        P(None, "row"),
        P("row", None),
        P("row"),
        P(None, "row", "col"),
    )
    out_specs = (
        P("col", "row"),
        P("col", None, None, None, "row"),
        P(None, None, "col", "row"),
        P(None, None, "col", "row"),
    )
    return jax.shard_map(local, mesh=mesh, in_specs=in_specs, out_specs=out_specs, check_vma=False)
```

```python
import functools
import math

import jax
import jax.numpy as jnp
from jax import lax
from jax.experimental import pallas as pl
from jax.experimental.pallas import tpu as pltpu
from jax.sharding import PartitionSpec as P

HD = 128
HEADS = 24
PAGE = 128
PAGES = 16
LMAX = 2048

norm_epsilon = 1e-06
rope_theta = 500000.0
big_negative = -1e30


ALIGN = 16
WINDOW = PAGE + ALIGN


def rdma(src, dst, send_sem, recv_sem, device):
    return pltpu.make_async_remote_copy(
        src_ref=src,
        dst_ref=dst,
        send_sem=send_sem,
        recv_sem=recv_sem,
        device_id=device,
        device_id_type=pl.DeviceIdType.MESH,
    )


def arrived(ref, recv_sem, send_sem, here):
    rdma(ref, ref, send_sem, recv_sem, here).wait_recv()


def each(count, body):
    lax.fori_loop(0, count, lambda i, carry: (body(i), carry)[1], 0)


def wrap(value, size):
    return lax.rem(value + size, size)


class Place:
    def __init__(self):
        self.row, self.col = lax.axis_index("row"), lax.axis_index("col")
        self.y, self.zl = self.row // 2, lax.rem(self.row, 2)
        self.zh, self.x, self.core = self.col // 8, lax.rem(self.col // 2, 4), lax.rem(self.col, 2)
        self.chip = self.col // 2
        self.here = (self.row, self.col)

    def at(self, y=None, zl=None, zh=None, x=None, core=None):
        y, zl = (self.y if y is None else y), (self.zl if zl is None else zl)
        zh, x = (self.zh if zh is None else zh), (self.x if x is None else x)
        core = self.core if core is None else core
        return (2 * y + zl, 8 * zh + 2 * x + core)


def signal(sem, device):
    pl.semaphore_signal(sem, inc=1, device_id=device, device_id_type=pl.DeviceIdType.MESH)


def near_first(step):
    return step + (step // 2) * (1 - 2 * lax.rem(step, 2))


class Relay:
    def __init__(self, me, src, stages, send, recv):
        self.me, self.src, self.stages, self.send, self.recv = me, src, stages, send, recv

    def go(self, away, stage, number, slot, src, device):
        dst = self.stages[stage].at[slot]

        @pl.when(away)
        def _():
            rdma(src, dst, self.send.at[stage, number], self.recv.at[stage, slot], device).start()

        @pl.when(jnp.logical_not(away))
        def _():
            dst[...] = src[...]

    def got(self, away, stage, slot):
        @pl.when(away)
        def _():
            arrived(
                self.stages[stage].at[slot], self.recv.at[stage, slot], self.send.at[stage, 0],
                self.me.here,
            )

    def first(self):
        me = self.me

        def send(i):
            dx, dk, zh = 3 - i // 4, lax.rem(i // 2, 2), lax.rem(i, 2)
            x, core = lax.rem(me.x + near_first(dx), 4), lax.rem(me.core + dk, 2)
            slot = (me.x * 2 + me.core) * 2 + zh
            away = jnp.logical_or(dx > 0, dk > 0)
            self.go(away, 0, i, slot, self.src.at[zh * 8 + 2 * x + core], me.at(x=x, core=core))

        each(16, send)

    def second(self):
        me = self.me

        def send(i):
            ks, zh = lax.rem(i // 2, 2), lax.rem(i, 2)
            xs = wrap(me.x - near_first(i // 4), 4)
            came = (xs * 2 + ks) * 2 + zh
            self.got(jnp.logical_or(i >= 4, ks != me.core), 0, came)
            zl = lax.rem(xs, 2)
            away = jnp.logical_or(zl != me.zl, zh != me.zh)
            slot = ((me.zh * 2 + me.zl) * 2 + xs // 2) * 2 + ks
            self.go(away, 1, came, slot, self.stages[0].at[came], me.at(zl=zl, zh=zh))

        each(16, send)

    def third(self, wait=True):
        me = self.me

        def send(i):
            zs = lax.rem(me.zh * 2 + me.zl + near_first(i // 4), 4)
            xh, ks = lax.rem(i // 2, 2), lax.rem(i, 2)
            came = (zs * 2 + xh) * 2 + ks
            if wait:
                self.got(i >= 4, 1, came)
            y = (zs // 2) * 2 + xh
            slot = (me.y * 2 + lax.rem(zs, 2)) * 2 + ks
            self.go(y != me.y, 2, came, slot, self.stages[1].at[came], me.at(y=y))

        each(16, send)

    def second_last(self):
        me = self.me
        each(16, lambda i: self.got(i // 4 != me.zh * 2 + me.zl, 1, i))

    def last(self):
        each(16, lambda i: self.got(i // 4 != self.me.y, 2, i))

    def drain(self, stages=(0, 1, 2)):
        me = self.me

        def sent(away, stage, number):
            if stage not in stages:
                return

            @pl.when(away)
            def _():
                rdma(
                    self.src.at[0], self.src.at[0], self.send.at[stage, number],
                    self.recv.at[stage, 0], me.here,
                ).wait_send()

        def each_piece(i):
            sent(jnp.logical_or(i < 12, lax.rem(i // 2, 2) > 0), 0, i)
            xs, zh = i // 4, lax.rem(i, 2)
            sent(jnp.logical_or(lax.rem(xs, 2) != me.zl, zh != me.zh), 1, i)
            zs, xh = i // 4, lax.rem(i // 2, 2)
            sent((zs // 2) * 2 + xh != me.y, 2, i)

        each(16, each_piece)


def join(stage, r, j, rows, columns):
    halves = [
        stage[2 * r + half, j * rows:(j + 1) * rows, :columns].astype(jnp.float32)
        for half in range(2)
    ]
    return jnp.concatenate(halves, axis=1)


class Gather:
    def __init__(self, me, over_col, view, send, recv):
        self.me, self.over_col, self.view, self.send, self.recv = me, over_col, view, send, recv
        self.hand = (3,) if over_col else ()
        self.sent = []

    def block(self, dz, dr):
        me = self.me
        if self.over_col:
            return wrap(me.zh + dz, 2) * 4 + wrap(me.x + dr, 4)
        return wrap(me.y + dr, 4) * 2 + wrap(me.zl + dz, 2)

    def copy(self, dz, dr, half, kind):
        me = self.me
        if kind == 3:
            device = me.at(core=1 - me.core)
        elif kind == 2:
            device = me.at(zh=1 - me.zh) if self.over_col else me.at(zl=1 - me.zl)
        else:
            turn = 1 - 2 * kind
            device = (
                me.at(x=wrap(me.x + turn, 4)) if self.over_col else me.at(y=wrap(me.y + turn, 4))
            )
        block = self.block(dz, dr)
        ref = self.view(block, me.core, half)
        return rdma(
            ref, ref, self.send.at[block, half, kind], self.recv.at[block, me.core, half], device
        )

    def go(self, dz, dr, half, *kinds):
        for kind in kinds + self.hand:
            self.copy(dz, dr, half, kind).start()
            self.sent.append((dz, dr, half, kind))

    def got(self, dz, dr, half, sibling=False):
        block = self.block(dz, dr)
        core = 1 - self.me.core if sibling else self.me.core
        arrived(
            self.view(block, core, half), self.recv.at[block, core, half], self.send.at[0, 0, 0],
            self.me.here,
        )

    def start(self, half):
        self.go(0, 0, half, 2, 0, 1)

    def z_turn(self):
        for half in range(2):
            self.got(1, 0, half)
            self.go(1, 0, half, 0, 1)

    def x_turn(self, dz, *more):
        self.got(dz, -1, 0)
        self.go(dz, -1, 0, 0, *more)
        self.got(dz, 1, 0)
        self.go(dz, 1, 0, *more)
        self.got(dz, 1, 1)
        self.go(dz, 1, 1, 1, *more)
        self.got(dz, -1, 1)
        self.go(dz, -1, 1, *more)

    def x_end(self, dz, *more):
        for half in range(2):
            self.got(dz, 2, half)
            self.go(dz, 2, half, *more)

    def z_end(self):
        for half in range(2):
            for dr in (0, -1, 1, 2):
                self.got(1, dr, half)
                self.go(1, dr, half)

    def sibling(self, dz, dr):
        for half in range(2):
            self.got(dz, dr, half, sibling=True)

    def drain(self):
        for which in self.sent:
            self.copy(*which).wait_send()
        self.sent = []


def by_core(me, run):
    @pl.when(me.core == 0)
    def _():
        run(True)

    @pl.when(me.core == 1)
    def _():
        run(False)


def sync_body(
    qkv_ref, gate_hbm, hid_ref, ow_hbm,
    proj_ref, qblk_ref, g2, ocol_ref,
    hid_parts, qsrc, q1, q2, q3, w_all, gf32, gsrc, g1,
    q_send, q_recv, g_send, g_recv, w_send, w_recv, o_send, o_fwd, o_recv, local_sem,
    *, n_row, n_col,
):
    me = Place()
    row, col, core = me.row, me.col, me.core
    width_row = qkv_ref.shape[2]
    fine = width_row // n_col
    bf16, f32 = jnp.bfloat16, jnp.float32

    def fetch(j):
        return pltpu.make_async_copy(gate_hbm.at[j], gf32.at[j], local_sem.at[j])

    for j in range(2):
        fetch(j).start()

    def cut(part, pieces, j):
        turned = part.T
        if pieces.shape[2] > part.shape[0]:
            fill = jnp.zeros((part.shape[1], pieces.shape[2] - part.shape[0]), f32)
            turned = jnp.concatenate([turned, fill], axis=1)
        for c in range(n_col):
            rows = turned[c * fine:(c + 1) * fine, :].astype(bf16)
            pieces[c, j * fine:(j + 1) * fine, :] = rows

    barrier = pltpu.get_barrier_semaphore()
    for i in range(1, 8):
        signal(barrier, me.at(x=lax.rem(me.x + i // 2, 4), core=lax.rem(me.core + i, 2)))
    for i in range(1, 4):
        signal(barrier, me.at(zh=lax.rem(me.zh + i // 2, 2), zl=lax.rem(me.zl + i, 2)))
    for i in range(1, n_row):
        signal(barrier, (lax.rem(row + i, n_row), col))

    for j in range(3):
        cut(qkv_ref[j], qsrc, j)
    pl.semaphore_wait(barrier, 7 + 3 + n_row - 1)

    qkv = Relay(me, qsrc, (q1, q2, q3), q_send, q_recv)
    gate = Relay(me, gsrc, (g1, g2), g_send, g_recv)
    qkv.first()
    for j in range(2):
        fetch(j).wait()
        cut(gf32[j], gsrc, j)
    qkv.second()
    gate.first()
    qkv.third()
    qkv.last()

    depth = w_all.shape[2] // 4

    for j in range(3):
        for pair in range(n_row // 2):
            first, second = (join(q3, 2 * pair + i, j, fine, qkv_ref.shape[1]) for i in range(2))
            qblk_ref[j, 2 * pair] = first.astype(bf16)
            qblk_ref[j, 2 * pair + 1] = second.astype(bf16)
            both = jnp.concatenate([first, second], axis=0).astype(bf16)
            at = pl.multiple_of(core * depth * 2 + pair * 2 * fine, 16)
            w_all[me.chip, j, pl.ds(at, 2 * fine), :] = both


    def weight_rows(chip, of_core, half):
        at = pl.multiple_of((of_core * 2 + half) * depth, 16)
        return w_all.at[chip, :, pl.ds(at, depth), :]

    weights = Gather(me, True, weight_rows, w_send, w_recv)
    weights.start(0)
    weights.start(1)

    own_rows = ow_hbm.shape[0]
    half_o = own_rows // 2
    out_width = ocol_ref.shape[1]

    def o_src(to_row):
        return ow_hbm.at[
            pl.ds(pl.multiple_of(core * half_o, 16), half_o),
            pl.ds(pl.multiple_of(to_row * out_width, 128), out_width),
        ]

    def o_dst(of_row, of_core):
        return ocol_ref.at[
            pl.ds(pl.multiple_of(of_row * own_rows + of_core * half_o, 16), half_o), :
        ]

    def o_copy(i):
        to_row = lax.rem(row + 1 + i, n_row)
        return rdma(
            o_src(to_row), o_dst(row, core), o_send.at[i], o_recv.at[row, core], (to_row, col)
        )

    def o_forward(of_row):
        return rdma(
            o_dst(of_row, core), o_dst(of_row, core), o_fwd.at[of_row], o_recv.at[of_row, core],
            me.at(core=1 - core),
        )

    def o_arrived(of_row, of_core):
        arrived(o_dst(of_row, of_core), o_recv.at[of_row, of_core], o_send.at[0], me.here)

    own_o = pltpu.make_async_copy(
        ow_hbm.at[:, pl.ds(pl.multiple_of(row * out_width, 128), out_width)],
        ocol_ref.at[pl.ds(pl.multiple_of(row * own_rows, 16), own_rows), :],
        local_sem.at[2],
    )
    own_o.start()

    def part(chip):
        return jnp.concatenate(
            [
                hid_ref[:, r * width_row + c * fine:r * width_row + (c + 1) * fine]
                for c in (2 * chip, 2 * chip + 1)
                for r in range(n_row)
            ],
            axis=1,
        )

    for chip in range(n_col // 2):
        hid_parts[chip] = part(chip)

    for j in range(3):
        proj_ref[j] = jnp.zeros_like(proj_ref[j])

    def project(dz, dx):
        weights.sibling(dz, dx)
        chip = weights.block(dz, dx)
        for j in range(3):
            proj_ref[j] += jnp.dot(hid_parts[chip], w_all[chip, j], preferred_element_type=f32)

    gate.second()
    weights.z_turn()
    each(n_row - 1, lambda i: o_copy(i).start())
    weights.x_turn(0)
    project(0, 0)
    weights.x_turn(1)
    project(1, 0)
    weights.x_end(0)
    project(0, -1)
    project(0, 1)
    weights.x_end(1)
    project(1, -1)
    project(1, 1)
    project(0, 2)
    project(1, 2)

    def o_relay(i):
        of_row = lax.rem(row + n_row - 1 - i, n_row)
        o_arrived(of_row, core)
        o_forward(of_row).start()

    each(n_row - 1, o_relay)
    gate.second_last()
    each(n_row - 1, lambda i: o_arrived(lax.rem(row + 1 + i, n_row), 1 - core))
    own_o.wait()
    qkv.drain()
    gate.drain((0, 1))
    weights.drain()
    each(n_row - 1, lambda i: o_copy(i).wait_send())
    each(n_row - 1, lambda i: o_forward(lax.rem(row + 1 + i, n_row)).wait_send())


def sync_weights(qkv_train, gate_up_train, hidden, o_weight, n_row, n_col):
    tok, width_model = hidden.shape
    row_width, part = qkv_train.shape[1:]
    gate_part = gate_up_train.shape[2]
    width = 2 * part
    fine = row_width // n_col
    bf16, f32 = jnp.bfloat16, jnp.float32
    dma = pltpu.SemaphoreType.DMA
    vmem, anywhere = pl.BlockSpec(memory_space=pltpu.VMEM), pl.BlockSpec(memory_space=pl.ANY)
    gate_tiles = -(-gate_part // 128) * 128
    return pl.pallas_call(
        functools.partial(sync_body, n_row=n_row, n_col=n_col),
        out_shape=(
            jax.ShapeDtypeStruct((3, tok, width), f32),
            jax.ShapeDtypeStruct((3, n_row, fine, width), bf16),
            jax.ShapeDtypeStruct((n_col, 2 * fine, gate_tiles), bf16),
            jax.ShapeDtypeStruct((n_row * o_weight.shape[0], width_model // n_row), bf16),
        ),
        in_specs=[vmem, anywhere, vmem, anywhere],
        out_specs=(vmem, vmem, vmem, anywhere),
        scratch_shapes=[
            pltpu.VMEM((n_col // 2, tok, 2 * n_row * fine), bf16),
            *[pltpu.VMEM((n_col, 3 * fine, part), bf16)] * 4,
            pltpu.VMEM((n_col // 2, 3, 2 * n_row * fine, width), bf16),
            pltpu.VMEM((2, gate_part, row_width), f32),
            *[pltpu.VMEM((n_col, 2 * fine, gate_tiles), bf16)] * 2,
            dma((3, n_col)),
            dma((3, n_col)),
            dma((2, n_col)),
            dma((2, n_col)),
            dma((n_col // 2, 2, 4)),
            dma((n_col // 2, 2, 2)),
            dma((n_row,)),
            dma((n_row,)),
            dma((n_row, 2)),
            dma((3,)),
        ],
        compiler_params=pltpu.CompilerParams(
            collective_id=1, has_side_effects=True, vmem_limit_bytes=60 << 20
        ),
        cost_estimate=pl.CostEstimate(
            flops=2 * 3 * tok * width_model * width, bytes_accessed=30_000_000, transcendentals=0
        ),
        name="sync_weights",
    )(qkv_train.swapaxes(1, 2), gate_up_train.swapaxes(1, 2), hidden, o_weight)


def column_of(sums, at_row):
    pick = (lax.broadcasted_iota(jnp.int32, (8, 128), 0) == at_row).astype(jnp.float32)
    return lax.dot_general(
        sums, pick, (((0,), (0,)), ((), ())),
        precision=lax.Precision.HIGHEST, preferred_element_type=jnp.float32,
    )


def lane_sums(values):
    return lax.dot_general(
        jnp.ones((8, values.shape[1]), jnp.float32), values * values, (((1,), (1,)), ((), ())),
        precision=lax.Precision.HIGHEST, preferred_element_type=jnp.float32,
    )


def layer_body(
    lengths_ref, proj_ref, cos_ref, sin_ref, gain_ref, ocol_ref, post_ref, g2, hid_hbm,
    out_ref, kv_out, gblk_ref,
    query, kv, mixed_all, residual, sq_in, sq_out, g3, g_send, g_recv,
    kv_send, kv_recv, a_send, a_recv, s_send, s_recv, t_send, t_recv, local_sem,
    *, n_row, n_col,
):
    me = Place()
    row, col = me.row, me.col
    bf16, f32 = jnp.bfloat16, jnp.float32
    tok, width = query.shape
    heads = width // HD
    out_width = out_ref.shape[1]
    keep = pltpu.make_async_copy(
        hid_hbm.at[:, pl.ds(pl.multiple_of(row * out_width, 128), out_width)], residual, local_sem.at[0]
    )
    keep.start()

    barrier = pltpu.get_barrier_semaphore()
    signal(barrier, me.at(x=wrap(me.x + 1, 4)))
    signal(barrier, me.at(x=wrap(me.x - 1, 4)))
    signal(barrier, me.at(zh=1 - me.zh))
    signal(barrier, me.at(core=1 - me.core))
    for i in range(1, n_row):
        signal(barrier, (lax.rem(row + i, n_row), col))

    own = pl.ds(pl.multiple_of(col * tok, 64), tok)
    kv[1, own, :] = proj_ref[2].astype(bf16)
    top = lax.broadcasted_iota(jnp.int32, (8, tok), 0) < 4
    sq_in[row] = jnp.where(top, lane_sums(proj_ref[0]), lane_sums(proj_ref[1]))
    pl.semaphore_wait(barrier, 4 + n_row - 1)

    def share(buffer, send, recv, i):
        return rdma(
            buffer.at[row], buffer.at[row], send.at[i], recv.at[row],
            (lax.rem(row + 1 + i, n_row), col),
        )

    def shared(buffer, send, recv):
        def wait(i):
            src = lax.rem(row + 1 + i, n_row)
            arrived(buffer.at[src], recv.at[src], send.at[0], me.here)

        each(n_row - 1, wait)
        total = buffer[0]
        for src in range(1, n_row):
            total = total + buffer[src]
        return total

    each(n_row - 1, lambda i: share(sq_in, s_send, s_recv, i).start())

    def tokens_of(block, core, half):
        rows = pl.ds(pl.multiple_of((2 * block + core) * tok, 64), tok)
        return kv.at[1 - half, rows, :]

    gathers = [Gather(me, True, tokens_of, kv_send, kv_recv) for _ in range(2)]
    first_sends = Gather(me, True, tokens_of, kv_send, kv_recv)
    first_sends.start(0)

    squares = shared(sq_in, s_send, s_recv)
    cosine, sine = cos_ref[...], sin_ref[...]
    for which in (1, 0):
        scale = lax.rsqrt(column_of(squares, 4 * which) / (n_row * width) + norm_epsilon)
        for head in range(heads):
            lanes = slice(head * HD, (head + 1) * HD)
            x = proj_ref[which, :, lanes] * scale * gain_ref[which:which + 1, lanes]
            turned = (x * cosine + pltpu.roll(x, HD // 2, 1) * sine).astype(bf16)
            if which == 1:
                kv[0, own, lanes] = turned
            else:
                query[:, lanes] = turned
        if which == 1:
            first_sends.start(1)

    gate = Relay(me, g2, (g2, g2, g3), g_send, g_recv)
    gate.third(wait=False)

    def kv_gather(z_first):
        g = gathers[0 if z_first else 1]
        if z_first:
            g.z_turn()
            g.x_turn(0)
            g.x_turn(1)
            g.x_end(0)
            g.x_end(1)
        else:
            g.x_turn(0, 2)
            g.x_end(0, 2)
            g.z_end()

    by_core(me, kv_gather)
    for dz in range(2):
        for dx in range(4):
            if (dz, dx) != (0, 0):
                gathers[0].sibling(dz, dx)
    gathers[0].sibling(0, 0)

    give = pltpu.make_async_copy(kv, kv_out, local_sem.at[1])
    give.start()

    reach = -(-(LMAX - 1) // tok)
    span = min(reach + 1, n_col) * tok
    first_key = pl.multiple_of(jnp.maximum(col - reach, 0) * tok, 64)
    query_index = col * tok + lax.broadcasted_iota(jnp.int32, (tok, 1), 0)
    key_index = first_key + lax.broadcasted_iota(jnp.int32, (1, span), 1)
    prompt_start = jnp.zeros((tok, 1), jnp.int32)
    end = 0
    for p in range(lengths_ref.shape[0]):
        end = end + lengths_ref[p]
        prompt_start = jnp.where(query_index >= end, end, prompt_start)
    allowed = (key_index <= query_index) & (key_index >= prompt_start)
    for head in range(heads):
        lanes = slice(head * HD, (head + 1) * HD)
        keys = kv[0, pl.ds(first_key, span), lanes]
        values = kv[1, pl.ds(first_key, span), lanes]
        scores = lax.dot_general(
            query[:, lanes], keys, (((1,), (1,)), ((), ())), preferred_element_type=f32
        ) * (1.0 / math.sqrt(HD))
        scores = jnp.where(allowed, scores, big_negative)
        exponent = jnp.exp(scores - jnp.max(scores, axis=1, keepdims=True))
        total = jnp.sum(exponent, axis=1, keepdims=True)
        mixed = jnp.dot(exponent.astype(bf16), values, preferred_element_type=f32)
        mixed_all[row, :, lanes] = (mixed / total).astype(bf16)

    half_tok = tok // 2
    row_gathers = [
        Gather(
            me, False,
            lambda block, core, half: mixed_all.at[block, pl.ds(half * half_tok, half_tok), :],
            a_send, a_recv,
        )
        for _ in range(2)
    ]

    fine = gblk_ref.shape[2]

    def gate_join(r):
        for j in range(2):
            gblk_ref[j, r] = join(g3, r, j, fine, gblk_ref.shape[3] // 2).astype(bf16)

    def row_gather(z_first):
        g = row_gathers[0 if z_first else 1]
        g.start(0)
        g.start(1)
        gate.last()
        each(n_row, gate_join)
        if z_first:
            g.z_turn()
            g.x_turn(0)
            g.x_turn(1)
            g.x_end(0)
            g.x_end(1)
        else:
            g.x_turn(0, 2)
            g.x_end(0, 2)
            g.z_end()

    by_core(me, row_gather)

    product = jnp.zeros((tok, out_width), f32)
    for src in range(n_row):
        product += jnp.dot(
            mixed_all[src], ocol_ref[src * width:(src + 1) * width, :], preferred_element_type=f32
        )
    sq_out[row] = lane_sums(product)
    each(n_row - 1, lambda i: share(sq_out, t_send, t_recv, i).start())
    keep.wait()

    each(n_row - 1, lambda i: share(sq_in, s_send, s_recv, i).wait_send())
    first_sends.drain()

    def drain(z_first):
        which = 0 if z_first else 1
        gathers[which].drain()
        row_gathers[which].drain()

    by_core(me, drain)
    gate.drain((2,))

    scale = lax.rsqrt(column_of(shared(sq_out, t_send, t_recv), 0) / (n_row * out_width) + norm_epsilon)
    for at in range(0, out_width, 128):
        lanes = slice(at, at + 128)
        out_ref[:, lanes] = (
            residual[:, lanes].astype(f32) + product[:, lanes] * scale * post_ref[at // 128:at // 128 + 1, :]
        ).astype(bf16)
    each(n_row - 1, lambda i: share(sq_out, t_send, t_recv, i).wait_send())
    give.wait()


def attention_layer(lengths, projected, cosine, sine, gain, o_columns, post, gate_pieces, gate_shape, hidden, n_row, n_col):
    _, tok, width = projected.shape
    out_width = o_columns.shape[1]
    bf16, f32 = jnp.bfloat16, jnp.float32
    dma = pltpu.SemaphoreType.DMA
    vmem, anywhere = pl.BlockSpec(memory_space=pltpu.VMEM), pl.BlockSpec(memory_space=pl.ANY)
    return pl.pallas_call(
        functools.partial(layer_body, n_row=n_row, n_col=n_col),
        out_shape=(
            jax.ShapeDtypeStruct((tok, out_width), bf16),
            jax.ShapeDtypeStruct((2, n_col * tok, width), bf16),
            jax.ShapeDtypeStruct(gate_shape, bf16),
        ),
        in_specs=[pl.BlockSpec(memory_space=pltpu.SMEM)] + [vmem] * 7 + [anywhere],
        out_specs=(vmem, anywhere, vmem),
        scratch_shapes=[
            pltpu.VMEM((tok, width), bf16),
            pltpu.VMEM((2, n_col * tok, width), bf16),
            pltpu.VMEM((n_row, tok, width), bf16),
            pltpu.VMEM((tok, out_width), bf16),
            pltpu.VMEM((n_row, 8, tok), f32),
            pltpu.VMEM((n_row, 8, tok), f32),
            pltpu.VMEM(gate_pieces.shape, bf16),
            dma((3, n_col)),
            dma((3, n_col)),
            dma((n_col // 2, 2, 4)),
            dma((n_col // 2, 2, 2)),
            dma((n_row, 2, 4)),
            dma((n_row, 2, 2)),
            dma((n_row,)),
            dma((n_row,)),
            dma((n_row,)),
            dma((n_row,)),
            dma((2,)),
        ],
        compiler_params=pltpu.CompilerParams(
            collective_id=2, has_side_effects=True, vmem_limit_bytes=60 << 20
        ),
        cost_estimate=pl.CostEstimate(
            flops=8_000_000_000, bytes_accessed=20_000_000, transcendentals=3_000_000
        ),
        name="attention_layer",
    )(lengths, projected, cosine, sine, gain, o_columns, post, gate_pieces, hidden)


def cache_body(lengths_ref, owner_ref, table_ref, kv_hbm, out_ref, windows, sems):
    tokens = kv_hbm.shape[1]
    col = lax.axis_index("col")
    begin = length = mine = end = 0
    for p in range(lengths_ref.shape[0]):
        here = owner_ref[p] == col
        begin, length = jnp.where(here, end, begin), jnp.where(here, lengths_ref[p], length)
        mine = jnp.where(here, p, mine)
        end = end + lengths_ref[p]

    def locate(page):
        first = jnp.minimum(begin + page * PAGE, tokens - 1)
        base = pl.multiple_of(jnp.minimum((first // ALIGN) * ALIGN, tokens - WINDOW), ALIGN)
        return first, base

    def fetch(page):
        _, base = locate(page)
        return pltpu.make_async_copy(
            kv_hbm.at[:, pl.ds(base, WINDOW), :], windows.at[page], sems.at[page]
        )

    each(PAGES, lambda page: fetch(page).start())

    def place(page):
        fetch(page).wait()
        first, base = locate(page)
        row = lax.broadcasted_iota(jnp.int32, (PAGE, WINDOW), 0)
        source = lax.broadcasted_iota(jnp.int32, (PAGE, WINDOW), 1)
        pick = (row + (first - base) == source) & (row + page * PAGE < length)
        pick = pick.astype(jnp.float32).astype(jnp.bfloat16)
        slot = table_ref[mine, page]
        for part in range(2):
            moved = jnp.dot(pick, windows[page, part], preferred_element_type=jnp.float32)
            out_ref[slot, part] = moved.astype(jnp.bfloat16)

    each(PAGES, place)


def build_cache(lengths, owner, page_table, kv):
    width = kv.shape[2]
    smem = pl.BlockSpec(memory_space=pltpu.SMEM)
    return pl.pallas_call(
        cache_body,
        out_shape=jax.ShapeDtypeStruct((PAGES, 2, PAGE, width), jnp.bfloat16),
        in_specs=[smem, smem, smem, pl.BlockSpec(memory_space=pl.ANY)],
        out_specs=pl.BlockSpec(memory_space=pltpu.VMEM),
        scratch_shapes=[
            pltpu.VMEM((PAGES, 2, WINDOW, width), jnp.bfloat16),
            pltpu.SemaphoreType.DMA((PAGES,)),
        ],
        compiler_params=pltpu.CompilerParams(vmem_limit_bytes=60 << 20),
        cost_estimate=pl.CostEstimate(flops=10_000_000, bytes_accessed=7_000_000, transcendentals=0),
        name="cache_pages",
    )(lengths, owner, page_table, kv)


def local(
    hidden, lengths, owner, page_table, qkv_train, qk_gain, o_weight, post_gain, gate_up_train
):
    n_row = lax.axis_size("row")
    n_col = lax.axis_size("col")
    col_index = lax.axis_index("col")
    tok_rows = hidden.shape[0]
    projected, weight_blocks, gate_pieces, o_columns = sync_weights(
        qkv_train, gate_up_train, hidden, o_weight, n_row, n_col
    )
    token_index = col_index * tok_rows + jnp.arange(tok_rows, dtype=jnp.int32)
    token_start = jnp.zeros_like(token_index)
    end = 0
    for p in range(lengths.shape[0]):
        end = end + lengths[p]
        token_start = jnp.where(token_index >= end, end, token_start)
    half_dim = HD // 2
    frequency = rope_theta ** (-2.0 * jnp.arange(half_dim, dtype=jnp.float32) / HD)
    angles = (token_index - token_start).astype(jnp.float32)[:, None] * frequency[None, :]
    cosine, sine = jnp.cos(angles), jnp.sin(angles)
    cosine = jnp.concatenate([cosine, cosine], axis=1)
    sine = jnp.concatenate([-sine, sine], axis=1)

    _, row_width, gate_part = gate_up_train.shape
    gate_shape = (2, n_row, row_width // n_col, 2 * gate_part)
    layer_out, kv, gate_up_blocks = attention_layer(
        lengths, projected, cosine, sine, qk_gain, o_columns,
        post_gain.reshape(-1, 128), gate_pieces, gate_shape, hidden, n_row, n_col,
    )
    cache_pages = build_cache(lengths, owner, page_table, kv)
    return (layer_out, cache_pages[None], weight_blocks, gate_up_blocks)


def solution(mesh):
    in_specs = (
        P("col", None),
        P(),
        P(),
        P(),
        P(None, "row", "col"),
        P(None, "row"),
        P("row", None),
        P("row"),
        P(None, "row", "col"),
    )
    out_specs = (
        P("col", "row"),
        P("col", None, None, None, "row"),
        P(None, None, "col", "row"),
        P(None, None, "col", "row"),
    )
    return jax.shard_map(local, mesh=mesh, in_specs=in_specs, out_specs=out_specs, check_vma=False)
```

```python
import functools
import math

import jax
import jax.numpy as jnp
from jax import lax
from jax.experimental import pallas as pl
from jax.experimental.pallas import tpu as pltpu
from jax.sharding import PartitionSpec as P

HD = 128
HEADS = 24
PAGE = 128
PAGES = 16
LMAX = 2048

norm_epsilon = 1e-06
rope_theta = 500000.0
big_negative = -1e30


ALIGN = 16
WINDOW = PAGE + ALIGN


def rdma(src, dst, send_sem, recv_sem, device):
    return pltpu.make_async_remote_copy(
        src_ref=src,
        dst_ref=dst,
        send_sem=send_sem,
        recv_sem=recv_sem,
        device_id=device,
        device_id_type=pl.DeviceIdType.MESH,
    )


def arrived(ref, recv_sem, send_sem, here):
    rdma(ref, ref, send_sem, recv_sem, here).wait_recv()


def each(count, body):
    lax.fori_loop(0, count, lambda i, carry: (body(i), carry)[1], 0)


def wrap(value, size):
    return lax.rem(value + size, size)


class Place:
    def __init__(self):
        self.row, self.col = lax.axis_index("row"), lax.axis_index("col")
        self.y, self.zl = self.row // 2, lax.rem(self.row, 2)
        self.zh, self.x, self.core = self.col // 8, lax.rem(self.col // 2, 4), lax.rem(self.col, 2)
        self.chip = self.col // 2
        self.here = (self.row, self.col)

    def at(self, y=None, zl=None, zh=None, x=None, core=None):
        y, zl = (self.y if y is None else y), (self.zl if zl is None else zl)
        zh, x = (self.zh if zh is None else zh), (self.x if x is None else x)
        core = self.core if core is None else core
        return (2 * y + zl, 8 * zh + 2 * x + core)


def signal(sem, device):
    pl.semaphore_signal(sem, inc=1, device_id=device, device_id_type=pl.DeviceIdType.MESH)


def near_first(step):
    return step + (step // 2) * (1 - 2 * lax.rem(step, 2))


class Relay:
    def __init__(self, me, src, stages, send, recv):
        self.me, self.src, self.stages, self.send, self.recv = me, src, stages, send, recv

    def go(self, away, stage, number, slot, src, device):
        dst = self.stages[stage].at[slot]

        @pl.when(away)
        def _():
            rdma(src, dst, self.send.at[stage, number], self.recv.at[stage, slot], device).start()

        @pl.when(jnp.logical_not(away))
        def _():
            dst[...] = src[...]

    def got(self, away, stage, slot):
        @pl.when(away)
        def _():
            arrived(
                self.stages[stage].at[slot], self.recv.at[stage, slot], self.send.at[stage, 0],
                self.me.here,
            )

    def first(self):
        me = self.me

        def send(i):
            dx, dk, zh = i // 4, lax.rem(i // 2, 2), lax.rem(i, 2)
            x, core = lax.rem(me.x + near_first(dx), 4), lax.rem(me.core + dk, 2)
            slot = (me.x * 2 + me.core) * 2 + zh
            away = jnp.logical_or(dx > 0, dk > 0)
            self.go(away, 0, i, slot, self.src.at[zh * 8 + 2 * x + core], me.at(x=x, core=core))

        each(16, send)

    def second(self):
        me = self.me

        def send(i):
            ks, zh = lax.rem(i // 2, 2), lax.rem(i, 2)
            xs = wrap(me.x - near_first(i // 4), 4)
            came = (xs * 2 + ks) * 2 + zh
            self.got(jnp.logical_or(i >= 4, ks != me.core), 0, came)
            zl = lax.rem(xs, 2)
            away = jnp.logical_or(zl != me.zl, zh != me.zh)
            slot = ((me.zh * 2 + me.zl) * 2 + xs // 2) * 2 + ks
            self.go(away, 1, came, slot, self.stages[0].at[came], me.at(zl=zl, zh=zh))

        each(16, send)

    def third(self, wait=True):
        me = self.me

        def send(i):
            zs = lax.rem(me.zh * 2 + me.zl + near_first(i // 4), 4)
            xh, ks = lax.rem(i // 2, 2), lax.rem(i, 2)
            came = (zs * 2 + xh) * 2 + ks
            if wait:
                self.got(i >= 4, 1, came)
            y = (zs // 2) * 2 + xh
            slot = (me.y * 2 + lax.rem(zs, 2)) * 2 + ks
            self.go(y != me.y, 2, came, slot, self.stages[1].at[came], me.at(y=y))

        each(16, send)

    def second_last(self):
        me = self.me
        each(16, lambda i: self.got(i // 4 != me.zh * 2 + me.zl, 1, i))

    def last(self):
        each(16, lambda i: self.got(i // 4 != self.me.y, 2, i))

    def drain(self, stages=(0, 1, 2)):
        me = self.me

        def sent(away, stage, number):
            if stage not in stages:
                return

            @pl.when(away)
            def _():
                rdma(
                    self.src.at[0], self.src.at[0], self.send.at[stage, number],
                    self.recv.at[stage, 0], me.here,
                ).wait_send()

        def each_piece(i):
            sent(jnp.logical_or(i >= 4, lax.rem(i // 2, 2) > 0), 0, i)
            xs, zh = i // 4, lax.rem(i, 2)
            sent(jnp.logical_or(lax.rem(xs, 2) != me.zl, zh != me.zh), 1, i)
            zs, xh = i // 4, lax.rem(i // 2, 2)
            sent((zs // 2) * 2 + xh != me.y, 2, i)

        each(16, each_piece)


def join(stage, r, j, rows, columns):
    halves = [
        stage[2 * r + half, j * rows:(j + 1) * rows, :columns].astype(jnp.float32)
        for half in range(2)
    ]
    return jnp.concatenate(halves, axis=1)


class Gather:
    def __init__(self, me, over_col, view, send, recv):
        self.me, self.over_col, self.view, self.send, self.recv = me, over_col, view, send, recv
        self.hand = (3,) if over_col else ()
        self.sent = []

    def block(self, dz, dr):
        me = self.me
        if self.over_col:
            return wrap(me.zh + dz, 2) * 4 + wrap(me.x + dr, 4)
        return wrap(me.y + dr, 4) * 2 + wrap(me.zl + dz, 2)

    def copy(self, dz, dr, half, kind):
        me = self.me
        if kind == 3:
            device = me.at(core=1 - me.core)
        elif kind == 2:
            device = me.at(zh=1 - me.zh) if self.over_col else me.at(zl=1 - me.zl)
        else:
            turn = 1 - 2 * kind
            device = (
                me.at(x=wrap(me.x + turn, 4)) if self.over_col else me.at(y=wrap(me.y + turn, 4))
            )
        block = self.block(dz, dr)
        ref = self.view(block, me.core, half)
        return rdma(
            ref, ref, self.send.at[block, half, kind], self.recv.at[block, me.core, half], device
        )

    def go(self, dz, dr, half, *kinds):
        for kind in kinds + self.hand:
            self.copy(dz, dr, half, kind).start()
            self.sent.append((dz, dr, half, kind))

    def got(self, dz, dr, half, sibling=False):
        block = self.block(dz, dr)
        core = 1 - self.me.core if sibling else self.me.core
        arrived(
            self.view(block, core, half), self.recv.at[block, core, half], self.send.at[0, 0, 0],
            self.me.here,
        )

    def start(self, half):
        self.go(0, 0, half, 2, 0, 1)

    def z_turn(self):
        for half in range(2):
            self.got(1, 0, half)
            self.go(1, 0, half, 0, 1)

    def x_turn(self, dz, *more):
        self.got(dz, -1, 0)
        self.go(dz, -1, 0, 0, *more)
        self.got(dz, 1, 0)
        self.go(dz, 1, 0, *more)
        self.got(dz, 1, 1)
        self.go(dz, 1, 1, 1, *more)
        self.got(dz, -1, 1)
        self.go(dz, -1, 1, *more)

    def x_end(self, dz, *more):
        for half in range(2):
            self.got(dz, 2, half)
            self.go(dz, 2, half, *more)

    def z_end(self):
        for half in range(2):
            for dr in (0, -1, 1, 2):
                self.got(1, dr, half)
                self.go(1, dr, half)

    def sibling(self, dz, dr):
        for half in range(2):
            self.got(dz, dr, half, sibling=True)

    def drain(self):
        for which in self.sent:
            self.copy(*which).wait_send()
        self.sent = []


def by_core(me, run):
    @pl.when(me.core == 0)
    def _():
        run(True)

    @pl.when(me.core == 1)
    def _():
        run(False)


def sync_body(
    qkv_ref, gate_hbm, hid_ref, ow_hbm,
    proj_ref, qblk_ref, g2, ocol_ref,
    hid_parts, qsrc, q1, q2, q3, w_all, gf32, gsrc, g1,
    q_send, q_recv, g_send, g_recv, w_send, w_recv, o_send, o_fwd, o_recv, local_sem,
    *, n_row, n_col,
):
    me = Place()
    row, col, core = me.row, me.col, me.core
    width_row = qkv_ref.shape[2]
    fine = width_row // n_col
    bf16, f32 = jnp.bfloat16, jnp.float32

    def fetch(j):
        return pltpu.make_async_copy(gate_hbm.at[j], gf32.at[j], local_sem.at[j])

    for j in range(2):
        fetch(j).start()

    def cut(part, pieces, j):
        turned = part.T
        if pieces.shape[2] > part.shape[0]:
            fill = jnp.zeros((part.shape[1], pieces.shape[2] - part.shape[0]), f32)
            turned = jnp.concatenate([turned, fill], axis=1)
        for c in range(n_col):
            rows = turned[c * fine:(c + 1) * fine, :].astype(bf16)
            pieces[c, j * fine:(j + 1) * fine, :] = rows

    barrier = pltpu.get_barrier_semaphore()
    for i in range(1, 8):
        signal(barrier, me.at(x=lax.rem(me.x + i // 2, 4), core=lax.rem(me.core + i, 2)))
    for i in range(1, 4):
        signal(barrier, me.at(zh=lax.rem(me.zh + i // 2, 2), zl=lax.rem(me.zl + i, 2)))
    for i in range(1, n_row):
        signal(barrier, (lax.rem(row + i, n_row), col))

    for j in range(3):
        cut(qkv_ref[j], qsrc, j)
    pl.semaphore_wait(barrier, 7 + 3 + n_row - 1)

    qkv = Relay(me, qsrc, (q1, q2, q3), q_send, q_recv)
    gate = Relay(me, gsrc, (g1, g2), g_send, g_recv)
    qkv.first()
    for j in range(2):
        fetch(j).wait()
        cut(gf32[j], gsrc, j)
    qkv.second()
    gate.first()
    qkv.third()
    qkv.last()

    depth = w_all.shape[2] // 4

    for j in range(3):
        for pair in range(n_row // 2):
            first, second = (join(q3, 2 * pair + i, j, fine, qkv_ref.shape[1]) for i in range(2))
            qblk_ref[j, 2 * pair] = first.astype(bf16)
            qblk_ref[j, 2 * pair + 1] = second.astype(bf16)
            both = jnp.concatenate([first, second], axis=0).astype(bf16)
            at = pl.multiple_of(core * depth * 2 + pair * 2 * fine, 16)
            w_all[me.chip, j, pl.ds(at, 2 * fine), :] = both


    def weight_rows(chip, of_core, half):
        at = pl.multiple_of((of_core * 2 + half) * depth, 16)
        return w_all.at[chip, :, pl.ds(at, depth), :]

    weights = Gather(me, True, weight_rows, w_send, w_recv)
    weights.start(0)
    weights.start(1)

    own_rows = ow_hbm.shape[0]
    half_o = own_rows // 2
    out_width = ocol_ref.shape[1]

    def o_src(to_row):
        return ow_hbm.at[
            pl.ds(pl.multiple_of(core * half_o, 16), half_o),
            pl.ds(pl.multiple_of(to_row * out_width, 128), out_width),
        ]

    def o_dst(of_row, of_core):
        return ocol_ref.at[
            pl.ds(pl.multiple_of(of_row * own_rows + of_core * half_o, 16), half_o), :
        ]

    def o_copy(i):
        to_row = lax.rem(row + 1 + i, n_row)
        return rdma(
            o_src(to_row), o_dst(row, core), o_send.at[i], o_recv.at[row, core], (to_row, col)
        )

    def o_forward(of_row):
        return rdma(
            o_dst(of_row, core), o_dst(of_row, core), o_fwd.at[of_row], o_recv.at[of_row, core],
            me.at(core=1 - core),
        )

    def o_arrived(of_row, of_core):
        arrived(o_dst(of_row, of_core), o_recv.at[of_row, of_core], o_send.at[0], me.here)

    own_o = pltpu.make_async_copy(
        ow_hbm.at[:, pl.ds(pl.multiple_of(row * out_width, 128), out_width)],
        ocol_ref.at[pl.ds(pl.multiple_of(row * own_rows, 16), own_rows), :],
        local_sem.at[2],
    )
    own_o.start()

    def part(chip):
        return jnp.concatenate(
            [
                hid_ref[:, r * width_row + c * fine:r * width_row + (c + 1) * fine]
                for c in (2 * chip, 2 * chip + 1)
                for r in range(n_row)
            ],
            axis=1,
        )

    for chip in range(n_col // 2):
        hid_parts[chip] = part(chip)

    for j in range(3):
        proj_ref[j] = jnp.zeros_like(proj_ref[j])

    def project(dz, dx):
        weights.sibling(dz, dx)
        chip = weights.block(dz, dx)
        for j in range(3):
            proj_ref[j] += jnp.dot(hid_parts[chip], w_all[chip, j], preferred_element_type=f32)

    gate.second()
    weights.z_turn()
    each(n_row - 1, lambda i: o_copy(i).start())
    weights.x_turn(0)
    project(0, 0)
    weights.x_turn(1)
    project(1, 0)
    weights.x_end(0)
    project(0, -1)
    project(0, 1)
    weights.x_end(1)
    project(1, -1)
    project(1, 1)
    project(0, 2)
    project(1, 2)

    def o_relay(i):
        of_row = lax.rem(row + n_row - 1 - i, n_row)
        o_arrived(of_row, core)
        o_forward(of_row).start()

    each(n_row - 1, o_relay)
    gate.second_last()
    each(n_row - 1, lambda i: o_arrived(lax.rem(row + 1 + i, n_row), 1 - core))
    own_o.wait()
    qkv.drain()
    gate.drain((0, 1))
    weights.drain()
    each(n_row - 1, lambda i: o_copy(i).wait_send())
    each(n_row - 1, lambda i: o_forward(lax.rem(row + 1 + i, n_row)).wait_send())


def sync_weights(qkv_train, gate_up_train, hidden, o_weight, n_row, n_col):
    tok, width_model = hidden.shape
    row_width, part = qkv_train.shape[1:]
    gate_part = gate_up_train.shape[2]
    width = 2 * part
    fine = row_width // n_col
    bf16, f32 = jnp.bfloat16, jnp.float32
    dma = pltpu.SemaphoreType.DMA
    vmem, anywhere = pl.BlockSpec(memory_space=pltpu.VMEM), pl.BlockSpec(memory_space=pl.ANY)
    gate_tiles = -(-gate_part // 128) * 128
    return pl.pallas_call(
        functools.partial(sync_body, n_row=n_row, n_col=n_col),
        out_shape=(
            jax.ShapeDtypeStruct((3, tok, width), f32),
            jax.ShapeDtypeStruct((3, n_row, fine, width), bf16),
            jax.ShapeDtypeStruct((n_col, 2 * fine, gate_tiles), bf16),
            jax.ShapeDtypeStruct((n_row * o_weight.shape[0], width_model // n_row), bf16),
        ),
        in_specs=[vmem, anywhere, vmem, anywhere],
        out_specs=(vmem, vmem, vmem, anywhere),
        scratch_shapes=[
            pltpu.VMEM((n_col // 2, tok, 2 * n_row * fine), bf16),
            *[pltpu.VMEM((n_col, 3 * fine, part), bf16)] * 4,
            pltpu.VMEM((n_col // 2, 3, 2 * n_row * fine, width), bf16),
            pltpu.VMEM((2, gate_part, row_width), f32),
            *[pltpu.VMEM((n_col, 2 * fine, gate_tiles), bf16)] * 2,
            dma((3, n_col)),
            dma((3, n_col)),
            dma((2, n_col)),
            dma((2, n_col)),
            dma((n_col // 2, 2, 4)),
            dma((n_col // 2, 2, 2)),
            dma((n_row,)),
            dma((n_row,)),
            dma((n_row, 2)),
            dma((3,)),
        ],
        compiler_params=pltpu.CompilerParams(
            collective_id=1, has_side_effects=True, vmem_limit_bytes=60 << 20
        ),
        cost_estimate=pl.CostEstimate(
            flops=2 * 3 * tok * width_model * width, bytes_accessed=30_000_000, transcendentals=0
        ),
        name="sync_weights",
    )(qkv_train.swapaxes(1, 2), gate_up_train.swapaxes(1, 2), hidden, o_weight)


def column_of(sums, at_row):
    pick = (lax.broadcasted_iota(jnp.int32, (8, 128), 0) == at_row).astype(jnp.float32)
    return lax.dot_general(
        sums, pick, (((0,), (0,)), ((), ())),
        precision=lax.Precision.HIGHEST, preferred_element_type=jnp.float32,
    )


def lane_sums(values):
    return lax.dot_general(
        jnp.ones((8, values.shape[1]), jnp.float32), values * values, (((1,), (1,)), ((), ())),
        precision=lax.Precision.HIGHEST, preferred_element_type=jnp.float32,
    )


def layer_body(
    lengths_ref, proj_ref, cos_ref, sin_ref, gain_ref, ocol_ref, post_ref, g2, hid_hbm,
    out_ref, kv_out, gblk_ref,
    query, kv, mixed_all, residual, sq_in, sq_out, g3, g_send, g_recv,
    kv_send, kv_recv, a_send, a_recv, s_send, s_recv, t_send, t_recv, local_sem,
    *, n_row, n_col,
):
    me = Place()
    row, col = me.row, me.col
    bf16, f32 = jnp.bfloat16, jnp.float32
    tok, width = query.shape
    heads = width // HD
    out_width = out_ref.shape[1]
    keep = pltpu.make_async_copy(
        hid_hbm.at[:, pl.ds(pl.multiple_of(row * out_width, 128), out_width)], residual, local_sem.at[0]
    )
    keep.start()

    barrier = pltpu.get_barrier_semaphore()
    signal(barrier, me.at(x=wrap(me.x + 1, 4)))
    signal(barrier, me.at(x=wrap(me.x - 1, 4)))
    signal(barrier, me.at(zh=1 - me.zh))
    signal(barrier, me.at(core=1 - me.core))
    for i in range(1, n_row):
        signal(barrier, (lax.rem(row + i, n_row), col))

    own = pl.ds(pl.multiple_of(col * tok, 64), tok)
    kv[1, own, :] = proj_ref[2].astype(bf16)
    top = lax.broadcasted_iota(jnp.int32, (8, tok), 0) < 4
    sq_in[row] = jnp.where(top, lane_sums(proj_ref[0]), lane_sums(proj_ref[1]))
    pl.semaphore_wait(barrier, 4 + n_row - 1)

    def share(buffer, send, recv, i):
        return rdma(
            buffer.at[row], buffer.at[row], send.at[i], recv.at[row],
            (lax.rem(row + 1 + i, n_row), col),
        )

    def shared(buffer, send, recv):
        def wait(i):
            src = lax.rem(row + 1 + i, n_row)
            arrived(buffer.at[src], recv.at[src], send.at[0], me.here)

        each(n_row - 1, wait)
        total = buffer[0]
        for src in range(1, n_row):
            total = total + buffer[src]
        return total

    each(n_row - 1, lambda i: share(sq_in, s_send, s_recv, i).start())

    def tokens_of(block, core, half):
        rows = pl.ds(pl.multiple_of((2 * block + core) * tok, 64), tok)
        return kv.at[1 - half, rows, :]

    gathers = [Gather(me, True, tokens_of, kv_send, kv_recv) for _ in range(2)]
    first_sends = Gather(me, True, tokens_of, kv_send, kv_recv)
    first_sends.start(0)

    squares = shared(sq_in, s_send, s_recv)
    cosine, sine = cos_ref[...], sin_ref[...]
    for which in (1, 0):
        scale = lax.rsqrt(column_of(squares, 4 * which) / (n_row * width) + norm_epsilon)
        for head in range(heads):
            lanes = slice(head * HD, (head + 1) * HD)
            x = proj_ref[which, :, lanes] * scale * gain_ref[which:which + 1, lanes]
            turned = (x * cosine + pltpu.roll(x, HD // 2, 1) * sine).astype(bf16)
            if which == 1:
                kv[0, own, lanes] = turned
            else:
                query[:, lanes] = turned
        if which == 1:
            first_sends.start(1)

    gate = Relay(me, g2, (g2, g2, g3), g_send, g_recv)
    gate.third(wait=False)

    def kv_gather(z_first):
        g = gathers[0 if z_first else 1]
        if z_first:
            g.z_turn()
            g.x_turn(0)
            g.x_turn(1)
            g.x_end(0)
            g.x_end(1)
        else:
            g.x_turn(0, 2)
            g.x_end(0, 2)
            g.z_end()

    by_core(me, kv_gather)
    for dz in range(2):
        for dx in range(4):
            if (dz, dx) != (0, 0):
                gathers[0].sibling(dz, dx)
    gathers[0].sibling(0, 0)

    give = pltpu.make_async_copy(kv, kv_out, local_sem.at[1])
    give.start()

    reach = -(-(LMAX - 1) // tok)
    span = min(reach + 1, n_col) * tok
    first_key = pl.multiple_of(jnp.maximum(col - reach, 0) * tok, 64)
    half_tok = tok // 2
    key_index = first_key + lax.broadcasted_iota(jnp.int32, (1, span), 1)

    def attend(half):
        part = slice(half * half_tok, (half + 1) * half_tok)
        query_index = col * tok + half * half_tok
        query_index = query_index + lax.broadcasted_iota(jnp.int32, (half_tok, 1), 0)
        prompt_start = jnp.zeros((half_tok, 1), jnp.int32)
        end = 0
        for p in range(lengths_ref.shape[0]):
            end = end + lengths_ref[p]
            prompt_start = jnp.where(query_index >= end, end, prompt_start)
        allowed = (key_index <= query_index) & (key_index >= prompt_start)
        for head in range(heads):
            attend_head(part, allowed, slice(head * HD, (head + 1) * HD))

    def attend_head(part, allowed, lanes):
        keys = kv[0, pl.ds(first_key, span), lanes]
        values = kv[1, pl.ds(first_key, span), lanes]
        scores = lax.dot_general(
            query[part, lanes], keys, (((1,), (1,)), ((), ())), preferred_element_type=f32
        ) * (1.0 / math.sqrt(HD))
        scores = jnp.where(allowed, scores, big_negative)
        exponent = jnp.exp(scores - jnp.max(scores, axis=1, keepdims=True))
        total = jnp.sum(exponent, axis=1, keepdims=True)
        mixed = jnp.dot(exponent.astype(bf16), values, preferred_element_type=f32)
        mixed_all[row, part, lanes] = (mixed / total).astype(bf16)

    def mixed_of(block, core, half):
        return mixed_all.at[block, pl.ds(half * half_tok, half_tok), :]

    row_gathers = [Gather(me, False, mixed_of, a_send, a_recv) for _ in range(3)]
    for half in range(2):
        attend(half)
        row_gathers[2].start(half)

    fine = gblk_ref.shape[2]

    def gate_join(r):
        for j in range(2):
            gblk_ref[j, r] = join(g3, r, j, fine, gblk_ref.shape[3] // 2).astype(bf16)

    def row_gather(z_first):
        g = row_gathers[0 if z_first else 1]
        gate.last()
        each(n_row, gate_join)
        if z_first:
            g.z_turn()
            g.x_turn(0)
            g.x_turn(1)
            g.x_end(0)
            g.x_end(1)
        else:
            g.x_turn(0, 2)
            g.x_end(0, 2)
            g.z_end()

    by_core(me, row_gather)

    product = jnp.zeros((tok, out_width), f32)
    for src in range(n_row):
        product += jnp.dot(
            mixed_all[src], ocol_ref[src * width:(src + 1) * width, :], preferred_element_type=f32
        )
    sq_out[row] = lane_sums(product)
    each(n_row - 1, lambda i: share(sq_out, t_send, t_recv, i).start())
    keep.wait()

    each(n_row - 1, lambda i: share(sq_in, s_send, s_recv, i).wait_send())
    first_sends.drain()

    def drain(z_first):
        which = 0 if z_first else 1
        gathers[which].drain()
        row_gathers[which].drain()

    by_core(me, drain)
    row_gathers[2].drain()
    gate.drain((2,))

    scale = lax.rsqrt(column_of(shared(sq_out, t_send, t_recv), 0) / (n_row * out_width) + norm_epsilon)
    for at in range(0, out_width, 128):
        lanes = slice(at, at + 128)
        out_ref[:, lanes] = (
            residual[:, lanes].astype(f32) + product[:, lanes] * scale * post_ref[at // 128:at // 128 + 1, :]
        ).astype(bf16)
    each(n_row - 1, lambda i: share(sq_out, t_send, t_recv, i).wait_send())
    give.wait()


def attention_layer(lengths, projected, cosine, sine, gain, o_columns, post, gate_pieces, gate_shape, hidden, n_row, n_col):
    _, tok, width = projected.shape
    out_width = o_columns.shape[1]
    bf16, f32 = jnp.bfloat16, jnp.float32
    dma = pltpu.SemaphoreType.DMA
    vmem, anywhere = pl.BlockSpec(memory_space=pltpu.VMEM), pl.BlockSpec(memory_space=pl.ANY)
    return pl.pallas_call(
        functools.partial(layer_body, n_row=n_row, n_col=n_col),
        out_shape=(
            jax.ShapeDtypeStruct((tok, out_width), bf16),
            jax.ShapeDtypeStruct((2, n_col * tok, width), bf16),
            jax.ShapeDtypeStruct(gate_shape, bf16),
        ),
        in_specs=[pl.BlockSpec(memory_space=pltpu.SMEM)] + [vmem] * 7 + [anywhere],
        out_specs=(vmem, anywhere, vmem),
        scratch_shapes=[
            pltpu.VMEM((tok, width), bf16),
            pltpu.VMEM((2, n_col * tok, width), bf16),
            pltpu.VMEM((n_row, tok, width), bf16),
            pltpu.VMEM((tok, out_width), bf16),
            pltpu.VMEM((n_row, 8, tok), f32),
            pltpu.VMEM((n_row, 8, tok), f32),
            pltpu.VMEM(gate_pieces.shape, bf16),
            dma((3, n_col)),
            dma((3, n_col)),
            dma((n_col // 2, 2, 4)),
            dma((n_col // 2, 2, 2)),
            dma((n_row, 2, 4)),
            dma((n_row, 2, 2)),
            dma((n_row,)),
            dma((n_row,)),
            dma((n_row,)),
            dma((n_row,)),
            dma((2,)),
        ],
        compiler_params=pltpu.CompilerParams(
            collective_id=2, has_side_effects=True, vmem_limit_bytes=60 << 20
        ),
        cost_estimate=pl.CostEstimate(
            flops=8_000_000_000, bytes_accessed=20_000_000, transcendentals=3_000_000
        ),
        name="attention_layer",
    )(lengths, projected, cosine, sine, gain, o_columns, post, gate_pieces, hidden)


def cache_body(lengths_ref, owner_ref, table_ref, kv_hbm, out_ref, windows, sems):
    tokens = kv_hbm.shape[1]
    col = lax.axis_index("col")
    begin = length = mine = end = 0
    for p in range(lengths_ref.shape[0]):
        here = owner_ref[p] == col
        begin, length = jnp.where(here, end, begin), jnp.where(here, lengths_ref[p], length)
        mine = jnp.where(here, p, mine)
        end = end + lengths_ref[p]

    def locate(page):
        first = jnp.minimum(begin + page * PAGE, tokens - 1)
        base = pl.multiple_of(jnp.minimum((first // ALIGN) * ALIGN, tokens - WINDOW), ALIGN)
        return first, base

    def fetch(page):
        _, base = locate(page)
        return pltpu.make_async_copy(
            kv_hbm.at[:, pl.ds(base, WINDOW), :], windows.at[page], sems.at[page]
        )

    each(PAGES, lambda page: fetch(page).start())

    def place(page):
        fetch(page).wait()
        first, base = locate(page)
        row = lax.broadcasted_iota(jnp.int32, (PAGE, WINDOW), 0)
        source = lax.broadcasted_iota(jnp.int32, (PAGE, WINDOW), 1)
        pick = (row + (first - base) == source) & (row + page * PAGE < length)
        pick = pick.astype(jnp.float32).astype(jnp.bfloat16)
        slot = table_ref[mine, page]
        for part in range(2):
            moved = jnp.dot(pick, windows[page, part], preferred_element_type=jnp.float32)
            out_ref[slot, part] = moved.astype(jnp.bfloat16)

    each(PAGES, place)


def build_cache(lengths, owner, page_table, kv):
    width = kv.shape[2]
    smem = pl.BlockSpec(memory_space=pltpu.SMEM)
    return pl.pallas_call(
        cache_body,
        out_shape=jax.ShapeDtypeStruct((PAGES, 2, PAGE, width), jnp.bfloat16),
        in_specs=[smem, smem, smem, pl.BlockSpec(memory_space=pl.ANY)],
        out_specs=pl.BlockSpec(memory_space=pltpu.VMEM),
        scratch_shapes=[
            pltpu.VMEM((PAGES, 2, WINDOW, width), jnp.bfloat16),
            pltpu.SemaphoreType.DMA((PAGES,)),
        ],
        compiler_params=pltpu.CompilerParams(vmem_limit_bytes=60 << 20),
        cost_estimate=pl.CostEstimate(flops=10_000_000, bytes_accessed=7_000_000, transcendentals=0),
        name="cache_pages",
    )(lengths, owner, page_table, kv)


def local(
    hidden, lengths, owner, page_table, qkv_train, qk_gain, o_weight, post_gain, gate_up_train
):
    n_row = lax.axis_size("row")
    n_col = lax.axis_size("col")
    col_index = lax.axis_index("col")
    tok_rows = hidden.shape[0]
    projected, weight_blocks, gate_pieces, o_columns = sync_weights(
        qkv_train, gate_up_train, hidden, o_weight, n_row, n_col
    )
    token_index = col_index * tok_rows + jnp.arange(tok_rows, dtype=jnp.int32)
    token_start = jnp.zeros_like(token_index)
    end = 0
    for p in range(lengths.shape[0]):
        end = end + lengths[p]
        token_start = jnp.where(token_index >= end, end, token_start)
    half_dim = HD // 2
    frequency = rope_theta ** (-2.0 * jnp.arange(half_dim, dtype=jnp.float32) / HD)
    angles = (token_index - token_start).astype(jnp.float32)[:, None] * frequency[None, :]
    cosine, sine = jnp.cos(angles), jnp.sin(angles)
    cosine = jnp.concatenate([cosine, cosine], axis=1)
    sine = jnp.concatenate([-sine, sine], axis=1)

    _, row_width, gate_part = gate_up_train.shape
    gate_shape = (2, n_row, row_width // n_col, 2 * gate_part)
    layer_out, kv, gate_up_blocks = attention_layer(
        lengths, projected, cosine, sine, qk_gain, o_columns,
        post_gain.reshape(-1, 128), gate_pieces, gate_shape, hidden, n_row, n_col,
    )
    cache_pages = build_cache(lengths, owner, page_table, kv)
    return (layer_out, cache_pages[None], weight_blocks, gate_up_blocks)


def solution(mesh):
    in_specs = (
        P("col", None),
        P(),
        P(),
        P(),
        P(None, "row", "col"),
        P(None, "row"),
        P("row", None),
        P("row"),
        P(None, "row", "col"),
    )
    out_specs = (
        P("col", "row"),
        P("col", None, None, None, "row"),
        P(None, None, "col", "row"),
        P(None, None, "col", "row"),
    )
    return jax.shard_map(local, mesh=mesh, in_specs=in_specs, out_specs=out_specs, check_vma=False)
```

```python
import functools
import math

import jax
import jax.numpy as jnp
from jax import lax
from jax.experimental import pallas as pl
from jax.experimental.pallas import tpu as pltpu
from jax.sharding import PartitionSpec as P

HD = 128
HEADS = 24
PAGE = 128
PAGES = 16
LMAX = 2048

norm_epsilon = 1e-06
rope_theta = 500000.0
big_negative = -1e30


ALIGN = 16
WINDOW = PAGE + ALIGN


def rdma(src, dst, send_sem, recv_sem, device):
    return pltpu.make_async_remote_copy(
        src_ref=src,
        dst_ref=dst,
        send_sem=send_sem,
        recv_sem=recv_sem,
        device_id=device,
        device_id_type=pl.DeviceIdType.MESH,
    )


def arrived(ref, recv_sem, send_sem, here):
    rdma(ref, ref, send_sem, recv_sem, here).wait_recv()


def each(count, body):
    lax.fori_loop(0, count, lambda i, carry: (body(i), carry)[1], 0)


def wrap(value, size):
    return lax.rem(value + size, size)


class Place:
    def __init__(self):
        self.row, self.col = lax.axis_index("row"), lax.axis_index("col")
        self.y, self.zl = self.row // 2, lax.rem(self.row, 2)
        self.zh, self.x, self.core = self.col // 8, lax.rem(self.col // 2, 4), lax.rem(self.col, 2)
        self.chip = self.col // 2
        self.here = (self.row, self.col)

    def at(self, y=None, zl=None, zh=None, x=None, core=None):
        y, zl = (self.y if y is None else y), (self.zl if zl is None else zl)
        zh, x = (self.zh if zh is None else zh), (self.x if x is None else x)
        core = self.core if core is None else core
        return (2 * y + zl, 8 * zh + 2 * x + core)


def signal(sem, device):
    pl.semaphore_signal(sem, inc=1, device_id=device, device_id_type=pl.DeviceIdType.MESH)


def near_first(step):
    return step + (step // 2) * (1 - 2 * lax.rem(step, 2))


class Relay:
    def __init__(self, me, src, stages, send, recv):
        self.me, self.src, self.stages, self.send, self.recv = me, src, stages, send, recv

    def go(self, away, stage, number, slot, src, device):
        dst = self.stages[stage].at[slot]

        @pl.when(away)
        def _():
            rdma(src, dst, self.send.at[stage, number], self.recv.at[stage, slot], device).start()

        @pl.when(jnp.logical_not(away))
        def _():
            dst[...] = src[...]

    def got(self, away, stage, slot):
        @pl.when(away)
        def _():
            arrived(
                self.stages[stage].at[slot], self.recv.at[stage, slot], self.send.at[stage, 0],
                self.me.here,
            )

    def first(self):
        me = self.me

        def send(i):
            dx, dk, zh = i // 4, lax.rem(i // 2, 2), lax.rem(i, 2)
            x, core = lax.rem(me.x + near_first(dx), 4), lax.rem(me.core + dk, 2)
            slot = (me.x * 2 + me.core) * 2 + zh
            away = jnp.logical_or(dx > 0, dk > 0)
            self.go(away, 0, i, slot, self.src.at[zh * 8 + 2 * x + core], me.at(x=x, core=core))

        each(16, send)

    def second(self):
        me = self.me

        def send(i):
            ks, zh = lax.rem(i // 2, 2), lax.rem(i, 2)
            xs = wrap(me.x - near_first(i // 4), 4)
            came = (xs * 2 + ks) * 2 + zh
            self.got(jnp.logical_or(i >= 4, ks != me.core), 0, came)
            zl = lax.rem(xs, 2)
            away = jnp.logical_or(zl != me.zl, zh != me.zh)
            slot = ((me.zh * 2 + me.zl) * 2 + xs // 2) * 2 + ks
            self.go(away, 1, came, slot, self.stages[0].at[came], me.at(zl=zl, zh=zh))

        each(16, send)

    def third(self, wait=True):
        me = self.me

        def send(i):
            zs = lax.rem(me.zh * 2 + me.zl + near_first(i // 4), 4)
            xh, ks = lax.rem(i // 2, 2), lax.rem(i, 2)
            came = (zs * 2 + xh) * 2 + ks
            if wait:
                self.got(i >= 4, 1, came)
            y = (zs // 2) * 2 + xh
            slot = (me.y * 2 + lax.rem(zs, 2)) * 2 + ks
            self.go(y != me.y, 2, came, slot, self.stages[1].at[came], me.at(y=y))

        each(16, send)

    def second_last(self):
        me = self.me
        each(16, lambda i: self.got(i // 4 != me.zh * 2 + me.zl, 1, i))

    def last(self):
        each(16, lambda i: self.got(i // 4 != self.me.y, 2, i))

    def drain(self, stages=(0, 1, 2)):
        me = self.me

        def sent(away, stage, number):
            if stage not in stages:
                return

            @pl.when(away)
            def _():
                rdma(
                    self.src.at[0], self.src.at[0], self.send.at[stage, number],
                    self.recv.at[stage, 0], me.here,
                ).wait_send()

        def each_piece(i):
            sent(jnp.logical_or(i >= 4, lax.rem(i // 2, 2) > 0), 0, i)
            xs, zh = i // 4, lax.rem(i, 2)
            sent(jnp.logical_or(lax.rem(xs, 2) != me.zl, zh != me.zh), 1, i)
            zs, xh = i // 4, lax.rem(i // 2, 2)
            sent((zs // 2) * 2 + xh != me.y, 2, i)

        each(16, each_piece)


def join(stage, r, j, rows, columns):
    halves = [
        stage[2 * r + half, j * rows:(j + 1) * rows, :columns].astype(jnp.float32)
        for half in range(2)
    ]
    return jnp.concatenate(halves, axis=1)


class Gather:
    def __init__(self, me, over_col, view, send, recv):
        self.me, self.over_col, self.view, self.send, self.recv = me, over_col, view, send, recv
        self.hand = (3,) if over_col else ()
        self.sent = []

    def block(self, dz, dr):
        me = self.me
        if self.over_col:
            return wrap(me.zh + dz, 2) * 4 + wrap(me.x + dr, 4)
        return wrap(me.y + dr, 4) * 2 + wrap(me.zl + dz, 2)

    def copy(self, dz, dr, half, kind):
        me = self.me
        if kind == 3:
            device = me.at(core=1 - me.core)
        elif kind == 2:
            device = me.at(zh=1 - me.zh) if self.over_col else me.at(zl=1 - me.zl)
        else:
            turn = 1 - 2 * kind
            device = (
                me.at(x=wrap(me.x + turn, 4)) if self.over_col else me.at(y=wrap(me.y + turn, 4))
            )
        block = self.block(dz, dr)
        ref = self.view(block, me.core, half)
        return rdma(
            ref, ref, self.send.at[block, half, kind], self.recv.at[block, me.core, half], device
        )

    def go(self, dz, dr, half, *kinds):
        for kind in kinds + self.hand:
            self.copy(dz, dr, half, kind).start()
            self.sent.append((dz, dr, half, kind))

    def got(self, dz, dr, half, sibling=False):
        block = self.block(dz, dr)
        core = 1 - self.me.core if sibling else self.me.core
        arrived(
            self.view(block, core, half), self.recv.at[block, core, half], self.send.at[0, 0, 0],
            self.me.here,
        )

    def start(self, half):
        self.go(0, 0, half, 2, 0, 1)

    def z_turn(self):
        for half in range(2):
            self.got(1, 0, half)
            self.go(1, 0, half, 0, 1)

    def x_turn(self, dz, *more):
        self.got(dz, -1, 0)
        self.go(dz, -1, 0, 0, *more)
        self.got(dz, 1, 0)
        self.go(dz, 1, 0, *more)
        self.got(dz, 1, 1)
        self.go(dz, 1, 1, 1, *more)
        self.got(dz, -1, 1)
        self.go(dz, -1, 1, *more)

    def x_end(self, dz, *more):
        for half in range(2):
            self.got(dz, 2, half)
            self.go(dz, 2, half, *more)

    def z_end(self):
        for half in range(2):
            for dr in (0, -1, 1, 2):
                self.got(1, dr, half)
                self.go(1, dr, half)

    def sibling(self, dz, dr):
        for half in range(2):
            self.got(dz, dr, half, sibling=True)

    def drain(self):
        for which in self.sent:
            self.copy(*which).wait_send()
        self.sent = []


def by_core(me, run):
    @pl.when(me.core == 0)
    def _():
        run(True)

    @pl.when(me.core == 1)
    def _():
        run(False)


def sync_body(
    qkv_ref, gate_hbm, hid_ref, ow_hbm,
    proj_ref, qblk_ref, g2, ocol_ref,
    hid_parts, qsrc, q1, q2, q3, w_all, gf32, gsrc, g1,
    q_send, q_recv, g_send, g_recv, w_send, w_recv, o_send, o_fwd, o_recv, local_sem,
    *, n_row, n_col,
):
    me = Place()
    row, col, core = me.row, me.col, me.core
    width_row = qkv_ref.shape[2]
    fine = width_row // n_col
    bf16, f32 = jnp.bfloat16, jnp.float32

    def fetch(j):
        return pltpu.make_async_copy(gate_hbm.at[j], gf32.at[j], local_sem.at[j])

    for j in range(2):
        fetch(j).start()

    def cut(part, pieces, j):
        turned = part.T
        if pieces.shape[2] > part.shape[0]:
            fill = jnp.zeros((part.shape[1], pieces.shape[2] - part.shape[0]), f32)
            turned = jnp.concatenate([turned, fill], axis=1)
        for c in range(n_col):
            rows = turned[c * fine:(c + 1) * fine, :].astype(bf16)
            pieces[c, j * fine:(j + 1) * fine, :] = rows

    barrier = pltpu.get_barrier_semaphore()
    for i in range(1, 8):
        signal(barrier, me.at(x=lax.rem(me.x + i // 2, 4), core=lax.rem(me.core + i, 2)))
    for i in range(1, 4):
        signal(barrier, me.at(zh=lax.rem(me.zh + i // 2, 2), zl=lax.rem(me.zl + i, 2)))
    for i in range(1, n_row):
        signal(barrier, (lax.rem(row + i, n_row), col))

    for j in range(3):
        cut(qkv_ref[j], qsrc, j)
    pl.semaphore_wait(barrier, 7 + 3 + n_row - 1)

    qkv = Relay(me, qsrc, (q1, q2, q3), q_send, q_recv)
    gate = Relay(me, gsrc, (g1, g2), g_send, g_recv)
    qkv.first()
    for j in range(2):
        fetch(j).wait()
        cut(gf32[j], gsrc, j)
    qkv.second()
    gate.first()
    qkv.third()
    qkv.last()

    depth = w_all.shape[2] // 4

    for j in range(3):
        for pair in range(n_row // 2):
            first, second = (join(q3, 2 * pair + i, j, fine, qkv_ref.shape[1]) for i in range(2))
            qblk_ref[j, 2 * pair] = first.astype(bf16)
            qblk_ref[j, 2 * pair + 1] = second.astype(bf16)
            both = jnp.concatenate([first, second], axis=0).astype(bf16)
            at = pl.multiple_of(core * depth * 2 + pair * 2 * fine, 16)
            w_all[me.chip, j, pl.ds(at, 2 * fine), :] = both


    def weight_rows(chip, of_core, half):
        at = pl.multiple_of((of_core * 2 + half) * depth, 16)
        return w_all.at[chip, :, pl.ds(at, depth), :]

    weights = Gather(me, True, weight_rows, w_send, w_recv)
    weights.start(0)
    weights.start(1)

    own_rows = ow_hbm.shape[0]
    half_o = own_rows // 2
    out_width = ocol_ref.shape[1]

    def o_src(to_row):
        return ow_hbm.at[
            pl.ds(pl.multiple_of(core * half_o, 16), half_o),
            pl.ds(pl.multiple_of(to_row * out_width, 128), out_width),
        ]

    def o_dst(of_row, of_core):
        return ocol_ref.at[
            pl.ds(pl.multiple_of(of_row * own_rows + of_core * half_o, 16), half_o), :
        ]

    def o_copy(i):
        to_row = lax.rem(row + 1 + i, n_row)
        return rdma(
            o_src(to_row), o_dst(row, core), o_send.at[i], o_recv.at[row, core], (to_row, col)
        )

    def o_forward(of_row):
        return rdma(
            o_dst(of_row, core), o_dst(of_row, core), o_fwd.at[of_row], o_recv.at[of_row, core],
            me.at(core=1 - core),
        )

    def o_arrived(of_row, of_core):
        arrived(o_dst(of_row, of_core), o_recv.at[of_row, of_core], o_send.at[0], me.here)

    own_o = pltpu.make_async_copy(
        ow_hbm.at[:, pl.ds(pl.multiple_of(row * out_width, 128), out_width)],
        ocol_ref.at[pl.ds(pl.multiple_of(row * own_rows, 16), own_rows), :],
        local_sem.at[2],
    )
    own_o.start()

    def part(chip):
        return jnp.concatenate(
            [
                hid_ref[:, r * width_row + c * fine:r * width_row + (c + 1) * fine]
                for c in (2 * chip, 2 * chip + 1)
                for r in range(n_row)
            ],
            axis=1,
        )

    for chip in range(n_col // 2):
        hid_parts[chip] = part(chip)

    for j in range(3):
        proj_ref[j] = jnp.zeros_like(proj_ref[j])

    def project(dz, dx):
        weights.sibling(dz, dx)
        chip = weights.block(dz, dx)
        for j in range(3):
            proj_ref[j] += jnp.dot(hid_parts[chip], w_all[chip, j], preferred_element_type=f32)

    gate.second()
    weights.z_turn()
    each(n_row - 1, lambda i: o_copy(i).start())
    weights.x_turn(0)
    project(0, 0)
    weights.x_turn(1)
    project(1, 0)
    weights.x_end(0)
    project(0, -1)
    project(0, 1)
    weights.x_end(1)
    project(1, -1)
    project(1, 1)
    project(0, 2)
    project(1, 2)

    def o_relay(i):
        of_row = lax.rem(row + n_row - 1 - i, n_row)
        o_arrived(of_row, core)
        o_forward(of_row).start()

    each(n_row - 1, o_relay)
    gate.second_last()
    each(n_row - 1, lambda i: o_arrived(lax.rem(row + 1 + i, n_row), 1 - core))
    own_o.wait()
    qkv.drain()
    gate.drain((0, 1))
    weights.drain()
    each(n_row - 1, lambda i: o_copy(i).wait_send())
    each(n_row - 1, lambda i: o_forward(lax.rem(row + 1 + i, n_row)).wait_send())


def sync_weights(qkv_train, gate_up_train, hidden, o_weight, n_row, n_col):
    tok, width_model = hidden.shape
    row_width, part = qkv_train.shape[1:]
    gate_part = gate_up_train.shape[2]
    width = 2 * part
    fine = row_width // n_col
    bf16, f32 = jnp.bfloat16, jnp.float32
    dma = pltpu.SemaphoreType.DMA
    vmem, anywhere = pl.BlockSpec(memory_space=pltpu.VMEM), pl.BlockSpec(memory_space=pl.ANY)
    gate_tiles = -(-gate_part // 128) * 128
    return pl.pallas_call(
        functools.partial(sync_body, n_row=n_row, n_col=n_col),
        out_shape=(
            jax.ShapeDtypeStruct((3, tok, width), f32),
            jax.ShapeDtypeStruct((3, n_row, fine, width), bf16),
            jax.ShapeDtypeStruct((n_col, 2 * fine, gate_tiles), bf16),
            jax.ShapeDtypeStruct((n_row * o_weight.shape[0], width_model // n_row), bf16),
        ),
        in_specs=[vmem, anywhere, vmem, anywhere],
        out_specs=(vmem, vmem, vmem, anywhere),
        scratch_shapes=[
            pltpu.VMEM((n_col // 2, tok, 2 * n_row * fine), bf16),
            *[pltpu.VMEM((n_col, 3 * fine, part), bf16)] * 4,
            pltpu.VMEM((n_col // 2, 3, 2 * n_row * fine, width), bf16),
            pltpu.VMEM((2, gate_part, row_width), f32),
            *[pltpu.VMEM((n_col, 2 * fine, gate_tiles), bf16)] * 2,
            dma((3, n_col)),
            dma((3, n_col)),
            dma((2, n_col)),
            dma((2, n_col)),
            dma((n_col // 2, 2, 4)),
            dma((n_col // 2, 2, 2)),
            dma((n_row,)),
            dma((n_row,)),
            dma((n_row, 2)),
            dma((3,)),
        ],
        compiler_params=pltpu.CompilerParams(
            collective_id=1, has_side_effects=True, vmem_limit_bytes=60 << 20
        ),
        cost_estimate=pl.CostEstimate(
            flops=2 * 3 * tok * width_model * width, bytes_accessed=30_000_000, transcendentals=0
        ),
        name="sync_weights",
    )(qkv_train.swapaxes(1, 2), gate_up_train.swapaxes(1, 2), hidden, o_weight)


def column_of(sums, at_row):
    pick = (lax.broadcasted_iota(jnp.int32, (8, 128), 0) == at_row).astype(jnp.float32)
    return lax.dot_general(
        sums, pick, (((0,), (0,)), ((), ())),
        precision=lax.Precision.HIGHEST, preferred_element_type=jnp.float32,
    )


def lane_sums(values):
    return lax.dot_general(
        jnp.ones((8, values.shape[1]), jnp.float32), values * values, (((1,), (1,)), ((), ())),
        precision=lax.Precision.HIGHEST, preferred_element_type=jnp.float32,
    )


def layer_body(
    lengths_ref, proj_ref, cos_ref, sin_ref, gain_ref, ocol_ref, post_ref, g2, hid_hbm,
    out_ref, kv_out, gblk_ref,
    query, kv, mixed_all, residual, sq_in, sq_out, g3, g_send, g_recv,
    kv_send, kv_recv, a_send, a_recv, s_send, s_recv, t_send, t_recv, local_sem,
    *, n_row, n_col,
):
    me = Place()
    row, col = me.row, me.col
    bf16, f32 = jnp.bfloat16, jnp.float32
    tok, width = query.shape
    heads = width // HD
    out_width = out_ref.shape[1]
    keep = pltpu.make_async_copy(
        hid_hbm.at[:, pl.ds(pl.multiple_of(row * out_width, 128), out_width)], residual, local_sem.at[0]
    )
    keep.start()

    barrier = pltpu.get_barrier_semaphore()
    signal(barrier, me.at(x=wrap(me.x + 1, 4)))
    signal(barrier, me.at(x=wrap(me.x - 1, 4)))
    signal(barrier, me.at(zh=1 - me.zh))
    signal(barrier, me.at(core=1 - me.core))
    for i in range(1, n_row):
        signal(barrier, (lax.rem(row + i, n_row), col))

    own = pl.ds(pl.multiple_of(col * tok, 64), tok)
    kv[1, own, :] = proj_ref[2].astype(bf16)
    top = lax.broadcasted_iota(jnp.int32, (8, tok), 0) < 4
    sq_in[row] = jnp.where(top, lane_sums(proj_ref[0]), lane_sums(proj_ref[1]))
    pl.semaphore_wait(barrier, 4 + n_row - 1)

    def share(buffer, send, recv, i):
        return rdma(
            buffer.at[row], buffer.at[row], send.at[i], recv.at[row],
            (lax.rem(row + 1 + i, n_row), col),
        )

    def shared(buffer, send, recv):
        def wait(i):
            src = lax.rem(row + 1 + i, n_row)
            arrived(buffer.at[src], recv.at[src], send.at[0], me.here)

        each(n_row - 1, wait)
        total = buffer[0]
        for src in range(1, n_row):
            total = total + buffer[src]
        return total

    each(n_row - 1, lambda i: share(sq_in, s_send, s_recv, i).start())

    def tokens_of(block, core, half):
        rows = pl.ds(pl.multiple_of((2 * block + core) * tok, 64), tok)
        return kv.at[1 - half, rows, :]

    gathers = [Gather(me, True, tokens_of, kv_send, kv_recv) for _ in range(2)]
    first_sends = Gather(me, True, tokens_of, kv_send, kv_recv)
    first_sends.start(0)

    squares = shared(sq_in, s_send, s_recv)
    cosine, sine = cos_ref[...], sin_ref[...]
    for which in (1, 0):
        scale = lax.rsqrt(column_of(squares, 4 * which) / (n_row * width) + norm_epsilon)
        for head in range(heads):
            lanes = slice(head * HD, (head + 1) * HD)
            x = proj_ref[which, :, lanes] * scale * gain_ref[which:which + 1, lanes]
            turned = (x * cosine + pltpu.roll(x, HD // 2, 1) * sine).astype(bf16)
            if which == 1:
                kv[0, own, lanes] = turned
            else:
                query[:, lanes] = turned
        if which == 1:
            first_sends.start(1)

    gate = Relay(me, g2, (g2, g2, g3), g_send, g_recv)
    gate.third(wait=False)

    def kv_gather(z_first):
        g = gathers[0 if z_first else 1]
        if z_first:
            g.z_turn()
            g.x_turn(0)
            g.x_turn(1)
            g.x_end(0)
            g.x_end(1)
        else:
            g.x_turn(0, 2)
            g.x_end(0, 2)
            g.z_end()

    by_core(me, kv_gather)
    for dz in range(2):
        for dx in range(4):
            if (dz, dx) != (0, 0):
                gathers[0].sibling(dz, dx)
    gathers[0].sibling(0, 0)

    give = pltpu.make_async_copy(kv, kv_out, local_sem.at[1])
    give.start()

    reach = -(-(LMAX - 1) // tok)
    span = min(reach + 1, n_col) * tok
    first_key = pl.multiple_of(jnp.maximum(col - reach, 0) * tok, 64)
    half_tok = tok // 2
    key_index = first_key + lax.broadcasted_iota(jnp.int32, (1, span), 1)

    def attend(half):
        part = slice(half * half_tok, (half + 1) * half_tok)
        query_index = col * tok + half * half_tok
        query_index = query_index + lax.broadcasted_iota(jnp.int32, (half_tok, 1), 0)
        prompt_start = jnp.zeros((half_tok, 1), jnp.int32)
        end = 0
        for p in range(lengths_ref.shape[0]):
            end = end + lengths_ref[p]
            prompt_start = jnp.where(query_index >= end, end, prompt_start)
        allowed = (key_index <= query_index) & (key_index >= prompt_start)
        for head in range(heads):
            attend_head(part, allowed, slice(head * HD, (head + 1) * HD))

    def attend_head(part, allowed, lanes):
        keys = kv[0, pl.ds(first_key, span), lanes]
        values = kv[1, pl.ds(first_key, span), lanes]
        scores = lax.dot_general(
            query[part, lanes], keys, (((1,), (1,)), ((), ())), preferred_element_type=f32
        ) * (1.0 / math.sqrt(HD))
        scores = jnp.where(allowed, scores, big_negative)
        exponent = jnp.exp(scores - jnp.max(scores, axis=1, keepdims=True))
        total = jnp.sum(exponent, axis=1, keepdims=True)
        mixed = jnp.dot(exponent.astype(bf16), values, preferred_element_type=f32)
        mixed_all[row, part, lanes] = (mixed / total).astype(bf16)

    def mixed_of(block, core, half):
        return mixed_all.at[block, pl.ds(half * half_tok, half_tok), :]

    row_gathers = [Gather(me, False, mixed_of, a_send, a_recv) for _ in range(3)]
    for half in range(2):
        attend(half)
        row_gathers[2].start(half)

    fine = gblk_ref.shape[2]

    def gate_join(r):
        for j in range(2):
            gblk_ref[j, r] = join(g3, r, j, fine, gblk_ref.shape[3] // 2).astype(bf16)

    def row_gather(z_first):
        g = row_gathers[0 if z_first else 1]
        if z_first:
            g.z_turn()
            g.x_turn(0)
            g.x_turn(1)
            gate.last()
            each(n_row, gate_join)
            g.x_end(0)
            g.x_end(1)
        else:
            g.x_turn(0, 2)
            g.x_end(0, 2)
            gate.last()
            each(n_row, gate_join)
            g.z_end()

    by_core(me, row_gather)

    product = jnp.zeros((tok, out_width), f32)
    for src in range(n_row):
        product += jnp.dot(
            mixed_all[src], ocol_ref[src * width:(src + 1) * width, :], preferred_element_type=f32
        )
    sq_out[row] = lane_sums(product)
    each(n_row - 1, lambda i: share(sq_out, t_send, t_recv, i).start())
    keep.wait()

    each(n_row - 1, lambda i: share(sq_in, s_send, s_recv, i).wait_send())
    first_sends.drain()

    def drain(z_first):
        which = 0 if z_first else 1
        gathers[which].drain()
        row_gathers[which].drain()

    by_core(me, drain)
    row_gathers[2].drain()
    gate.drain((2,))

    scale = lax.rsqrt(column_of(shared(sq_out, t_send, t_recv), 0) / (n_row * out_width) + norm_epsilon)
    for at in range(0, out_width, 128):
        lanes = slice(at, at + 128)
        out_ref[:, lanes] = (
            residual[:, lanes].astype(f32) + product[:, lanes] * scale * post_ref[at // 128:at // 128 + 1, :]
        ).astype(bf16)
    each(n_row - 1, lambda i: share(sq_out, t_send, t_recv, i).wait_send())
    give.wait()


def attention_layer(lengths, projected, cosine, sine, gain, o_columns, post, gate_pieces, gate_shape, hidden, n_row, n_col):
    _, tok, width = projected.shape
    out_width = o_columns.shape[1]
    bf16, f32 = jnp.bfloat16, jnp.float32
    dma = pltpu.SemaphoreType.DMA
    vmem, anywhere = pl.BlockSpec(memory_space=pltpu.VMEM), pl.BlockSpec(memory_space=pl.ANY)
    return pl.pallas_call(
        functools.partial(layer_body, n_row=n_row, n_col=n_col),
        out_shape=(
            jax.ShapeDtypeStruct((tok, out_width), bf16),
            jax.ShapeDtypeStruct((2, n_col * tok, width), bf16),
            jax.ShapeDtypeStruct(gate_shape, bf16),
        ),
        in_specs=[pl.BlockSpec(memory_space=pltpu.SMEM)] + [vmem] * 7 + [anywhere],
        out_specs=(vmem, anywhere, vmem),
        scratch_shapes=[
            pltpu.VMEM((tok, width), bf16),
            pltpu.VMEM((2, n_col * tok, width), bf16),
            pltpu.VMEM((n_row, tok, width), bf16),
            pltpu.VMEM((tok, out_width), bf16),
            pltpu.VMEM((n_row, 8, tok), f32),
            pltpu.VMEM((n_row, 8, tok), f32),
            pltpu.VMEM(gate_pieces.shape, bf16),
            dma((3, n_col)),
            dma((3, n_col)),
            dma((n_col // 2, 2, 4)),
            dma((n_col // 2, 2, 2)),
            dma((n_row, 2, 4)),
            dma((n_row, 2, 2)),
            dma((n_row,)),
            dma((n_row,)),
            dma((n_row,)),
            dma((n_row,)),
            dma((2,)),
        ],
        compiler_params=pltpu.CompilerParams(
            collective_id=2, has_side_effects=True, vmem_limit_bytes=60 << 20
        ),
        cost_estimate=pl.CostEstimate(
            flops=8_000_000_000, bytes_accessed=20_000_000, transcendentals=3_000_000
        ),
        name="attention_layer",
    )(lengths, projected, cosine, sine, gain, o_columns, post, gate_pieces, hidden)


def cache_body(lengths_ref, owner_ref, table_ref, kv_hbm, out_ref, windows, sems):
    tokens = kv_hbm.shape[1]
    col = lax.axis_index("col")
    begin = length = mine = end = 0
    for p in range(lengths_ref.shape[0]):
        here = owner_ref[p] == col
        begin, length = jnp.where(here, end, begin), jnp.where(here, lengths_ref[p], length)
        mine = jnp.where(here, p, mine)
        end = end + lengths_ref[p]

    def locate(page):
        first = jnp.minimum(begin + page * PAGE, tokens - 1)
        base = pl.multiple_of(jnp.minimum((first // ALIGN) * ALIGN, tokens - WINDOW), ALIGN)
        return first, base

    def fetch(page):
        _, base = locate(page)
        return pltpu.make_async_copy(
            kv_hbm.at[:, pl.ds(base, WINDOW), :], windows.at[page], sems.at[page]
        )

    each(PAGES, lambda page: fetch(page).start())

    def place(page):
        fetch(page).wait()
        first, base = locate(page)
        row = lax.broadcasted_iota(jnp.int32, (PAGE, WINDOW), 0)
        source = lax.broadcasted_iota(jnp.int32, (PAGE, WINDOW), 1)
        pick = (row + (first - base) == source) & (row + page * PAGE < length)
        pick = pick.astype(jnp.float32).astype(jnp.bfloat16)
        slot = table_ref[mine, page]
        for part in range(2):
            moved = jnp.dot(pick, windows[page, part], preferred_element_type=jnp.float32)
            out_ref[slot, part] = moved.astype(jnp.bfloat16)

    each(PAGES, place)


def build_cache(lengths, owner, page_table, kv):
    width = kv.shape[2]
    smem = pl.BlockSpec(memory_space=pltpu.SMEM)
    return pl.pallas_call(
        cache_body,
        out_shape=jax.ShapeDtypeStruct((PAGES, 2, PAGE, width), jnp.bfloat16),
        in_specs=[smem, smem, smem, pl.BlockSpec(memory_space=pl.ANY)],
        out_specs=pl.BlockSpec(memory_space=pltpu.VMEM),
        scratch_shapes=[
            pltpu.VMEM((PAGES, 2, WINDOW, width), jnp.bfloat16),
            pltpu.SemaphoreType.DMA((PAGES,)),
        ],
        compiler_params=pltpu.CompilerParams(vmem_limit_bytes=60 << 20),
        cost_estimate=pl.CostEstimate(flops=10_000_000, bytes_accessed=7_000_000, transcendentals=0),
        name="cache_pages",
    )(lengths, owner, page_table, kv)


def local(
    hidden, lengths, owner, page_table, qkv_train, qk_gain, o_weight, post_gain, gate_up_train
):
    n_row = lax.axis_size("row")
    n_col = lax.axis_size("col")
    col_index = lax.axis_index("col")
    tok_rows = hidden.shape[0]
    projected, weight_blocks, gate_pieces, o_columns = sync_weights(
        qkv_train, gate_up_train, hidden, o_weight, n_row, n_col
    )
    token_index = col_index * tok_rows + jnp.arange(tok_rows, dtype=jnp.int32)
    token_start = jnp.zeros_like(token_index)
    end = 0
    for p in range(lengths.shape[0]):
        end = end + lengths[p]
        token_start = jnp.where(token_index >= end, end, token_start)
    half_dim = HD // 2
    frequency = rope_theta ** (-2.0 * jnp.arange(half_dim, dtype=jnp.float32) / HD)
    angles = (token_index - token_start).astype(jnp.float32)[:, None] * frequency[None, :]
    cosine, sine = jnp.cos(angles), jnp.sin(angles)
    cosine = jnp.concatenate([cosine, cosine], axis=1)
    sine = jnp.concatenate([-sine, sine], axis=1)

    _, row_width, gate_part = gate_up_train.shape
    gate_shape = (2, n_row, row_width // n_col, 2 * gate_part)
    layer_out, kv, gate_up_blocks = attention_layer(
        lengths, projected, cosine, sine, qk_gain, o_columns,
        post_gain.reshape(-1, 128), gate_pieces, gate_shape, hidden, n_row, n_col,
    )
    cache_pages = build_cache(lengths, owner, page_table, kv)
    return (layer_out, cache_pages[None], weight_blocks, gate_up_blocks)


def solution(mesh):
    in_specs = (
        P("col", None),
        P(),
        P(),
        P(),
        P(None, "row", "col"),
        P(None, "row"),
        P("row", None),
        P("row"),
        P(None, "row", "col"),
    )
    out_specs = (
        P("col", "row"),
        P("col", None, None, None, "row"),
        P(None, None, "col", "row"),
        P(None, None, "col", "row"),
    )
    return jax.shard_map(local, mesh=mesh, in_specs=in_specs, out_specs=out_specs, check_vma=False)
```
